32 devices in a mesh: mem: 8 (over z, y), reg: 4 (over x, core).
Axes of the slice: x: 2, y: 2, z: 4, core: 2. Of those that a mesh axis runs over, the one named last changes fastest.
Arguments:
- prior_tracer_draws: float32 [8, 32, 2048], P('mem', 'reg'), may hold values from -6 to 6
- courant_row: bfloat16 [32, 2048], P('reg'), may hold values from -0.25 to 0.25
- courant_column: bfloat16 [32, 2048], P('reg'), may hold values from -0.25 to 0.25
- diffusion: bfloat16 [32, 2048], P('reg'), may hold values from 0.049804688 to 0.19921875
- obs_value: float32 [128], replicated, may hold values from -6 to 6
- observation_variance: float32 [128], replicated, may hold values from 0.25 to 1
- obs_noise: float32 [128, 8], replicated, may hold values from -5 to 5
- obs_owner: int32 [128], replicated, may hold values from 0 to 31
- obs_cell: int32 [128], replicated, may hold values from 0 to 2047
- obs_order: int32 [128], replicated, may hold values from 0 to 127, each once
Outputs:
- posterior_tracer_draws: float32 [8, 32, 2048], P('mem', 'reg')
The draws below stay inside these ranges and needn't reach their ends.
Inputs may be any that keep to these rules, and one draw needn't show every extreme that they name: `obs_owner`: numbers a slab as its index along mem times the size of reg plus its index along reg; slab (p, r) holds rows r * 8 + p * 1 to r * 8 + (p + 1) - 1. `obs_cell`: row-major cell within the slab's 1 x 2048 cells. `obs_order`: each observation once.
All inputs are finite; a program needn't handle non-finite values.
Results may differ from the reference program's by a relative error of at most 0.0003.
Values may be sent and summed in bfloat16 or wider, within the bound.
No kernel may reach another device: no remote copies, remote signals or barrier semaphores. Data moves between devices by JAX's collectives and lax.ppermute only.
A program may use at most 64 MiB of HBM per device.

```python
import math
import jax
import jax.numpy as jnp
from jax import lax

NY = 2048
RS = 1
NOB = 64
NBLK = 2
MEMBERS = 8
RX = 8
NX = 32
S = 2048
NOBS = 128
LX = 4
LY = 512
N_REG = 4
DEVICES = 32


def set_ends(result, rng, low, largest):
    spot = [jax.random.randint(jax.random.fold_in(rng, axis), (), 0, length) for axis, length in enumerate(result.shape)]
    main_axis = result.shape.index(max(result.shape))
    neighbour = spot[:main_axis] + [(spot[main_axis] + 1) % result.shape[main_axis]] + spot[main_axis + 1:]
    return result.at[tuple(spot)].set(low).at[tuple(neighbour)].set(largest)


def levels(stream_key, shape, cuts, least, high):
    factor_of = 1.0
    for dim, parts in cuts:
        steps = jax.random.uniform(jax.random.fold_in(jax.random.fold_in(stream_key, 6), dim), (parts,), jnp.float32, least / len(cuts), high / len(cuts))
        factor_of = factor_of * jnp.repeat(jnp.exp(steps), shape[dim] // parts).reshape((-1,) + (1,) * (len(shape) - 1 - dim))
    return factor_of


def bell_draw(stream_key, shape, scale, most, cuts=(), held_as=jnp.bfloat16):
    drawn = jax.random.normal(stream_key, shape, jnp.float32) * scale
    if len(cuts) > 0:
        drawn = levels(stream_key, shape, cuts, -0.22, 0.18) * drawn
    return jnp.clip(drawn, min=-most, max=most).astype(held_as)


def setup_inputs(seed: int = 0) -> dict:
    keys = jax.random.split(jax.random.key(seed), 11)
    return {
        "prior_tracer_draws": bell_draw(keys[0], (MEMBERS, NX, NY), 1.0, 6.0, ((0, 8), (1, 4)), jnp.float32),
        "courant_row": jnp.clip(jax.random.uniform(keys[1], (NX, NY), jnp.float32, -0.25, 0.25) * levels(keys[1], (NX, NY), ((0, 4),), -0.4, 0.0), -0.25, 0.25).astype(jnp.bfloat16),
        "courant_column": jnp.clip(jax.random.uniform(keys[2], (NX, NY), jnp.float32, -0.25, 0.25) * levels(keys[2], (NX, NY), ((0, 4),), -0.4, 0.0), -0.25, 0.25).astype(jnp.bfloat16),
        "diffusion": jnp.clip(jnp.exp(math.log(0.19921875) - 1.3862944 * jax.random.uniform(keys[3], (NX, NY), jnp.float32) ** levels(keys[3], (NX, NY), ((0, 4),), -0.2, 0.2)), 0.049804688, 0.19921875).astype(jnp.bfloat16),
        "obs_value": bell_draw(keys[4], (NOBS,), 1.0, 6.0, (), jnp.float32),
        "observation_variance": jnp.clip(jnp.exp(jax.random.uniform(keys[5], (NOBS,), jnp.float32, math.log(0.25), math.log(1.0))), 0.25, 1.0),
        "obs_noise": bell_draw(keys[6], (NOBS, MEMBERS), 1.0, 5.0, (), jnp.float32),
        "obs_owner": set_ends(jax.random.randint(keys[7], (NOBS,), 0, DEVICES), jax.random.fold_in(keys[7], 1), 0, DEVICES - 1).astype(jnp.int32),
        "obs_cell": set_ends(jax.random.randint(keys[8], (NOBS,), 0, S), jax.random.fold_in(keys[8], 1), 0, S - 1).astype(jnp.int32),
        "obs_order": jax.random.permutation(keys[9], NOBS).astype(jnp.int32),
    }


HIGH = lax.Precision.HIGHEST

def bell(delta, period, scale):
    delta = delta % period
    dist = jnp.minimum(delta, period - delta).astype(jnp.float32)
    return jnp.exp(-0.5 * (dist / scale) ** 2)

def step_forward(field, courant_row, courant_column, diffusion):
    north = jnp.roll(field, 1, axis=0)
    south = jnp.roll(field, -1, axis=0)
    west = jnp.roll(field, 1, axis=1)
    east = jnp.roll(field, -1, axis=1)
    return field - 0.5 * courant_column * (east - west) - 0.5 * courant_row * (south - north) + diffusion * (north + south + east + west - 4.0 * field)

def measured_kalman_gain(prior, values, variance, noise):
    members = prior.shape[0]
    anomaly = prior - lax.optimization_barrier(jnp.mean(prior, axis=0))
    spread = jnp.dot(anomaly.T.astype(jnp.float32), anomaly.astype(jnp.float32), precision=HIGH, preferred_element_type=jnp.float32) / (members - 1)
    system = spread + jnp.diag(variance)
    factor = jnp.linalg.cholesky(system)
    innovation = values[:, None] + jnp.sqrt(variance)[:, None] * noise - prior.T
    weights = jax.scipy.linalg.cho_solve((factor, True), innovation)
    return (anomaly, weights)

def increment(columns, anomaly, weights, taper):
    members = columns.shape[0]
    centred = columns - lax.optimization_barrier(jnp.mean(columns, axis=0))
    cross = lax.dot_general(centred.astype(jnp.float32), anomaly.astype(jnp.float32), (((0,), (0,)), ((), ())), precision=HIGH, preferred_element_type=jnp.float32) / (members - 1)
    return columns + lax.dot_general(weights.astype(jnp.float32), (taper * cross).astype(jnp.float32), (((0,), (1,)), ((), ())), precision=HIGH, preferred_element_type=jnp.float32)

def reference(prior_tracer_draws, courant_row, courant_column, diffusion, obs_value, observation_variance, obs_noise, obs_owner, obs_cell, obs_order):
    rate_row = courant_row.astype(jnp.float32)
    column_rate = courant_column.astype(jnp.float32)
    rate_diff = diffusion.astype(jnp.float32)
    members = prior_tracer_draws.shape[0]

    def propagate_sample_draw(sample_draw):
        return step_forward(step_forward(sample_draw, rate_row, column_rate, rate_diff), rate_row, column_rate, rate_diff)
    posterior_tracer_draws = lax.map(propagate_sample_draw, prior_tracer_draws)
    obs_row = obs_owner % N_REG * RX + obs_owner // N_REG * RS + obs_cell // NY
    observation_column = obs_cell % NY
    col_index = jnp.arange(NY, dtype=jnp.int32)
    for block in range(NBLK):
        chosen = obs_order[block * NOB:(block + 1) * NOB]
        orow = obs_row[chosen]
        ocol = observation_column[chosen]
        prior = posterior_tracer_draws[:, orow, ocol]
        anomaly, weights = measured_kalman_gain(prior, obs_value[chosen], observation_variance[chosen], obs_noise[chosen])
        col_taper = bell(col_index[:, None] - ocol[None, :], NY, LY)

        def region_update(subdomain_tile, current=posterior_tracer_draws, orow=orow, col_taper=col_taper, anomaly=anomaly, weights=weights):
            start = (subdomain_tile * RX).astype(jnp.int32)
            piece = lax.dynamic_slice_in_dim(current, start, RX, 1)
            rows_here = start + jnp.arange(RX, dtype=jnp.int32)
            row_taper = bell(rows_here[:, None] - orow[None, :], NX, LX)
            taper = (row_taper[:, None, :] * col_taper[None, :, :]).reshape(RX * NY, NOB)
            fresh = increment(piece.reshape(members, RX * NY), anomaly, weights, taper)
            return fresh.reshape(members, RX, NY)
        pieces = lax.map(region_update, jnp.arange(N_REG, dtype=jnp.int32))
        posterior_tracer_draws = jnp.transpose(pieces, (1, 0, 2, 3)).reshape(members, NX, NY)
    return posterior_tracer_draws
```

```python
import functools

import jax
import jax.numpy as jnp
from jax import lax
from jax.experimental import pallas as pl
from jax.experimental.pallas import tpu as pltpu
from jax.sharding import PartitionSpec as P

NOB = 64
NBLK = 2


HIGH = lax.Precision.HIGHEST


def extended(cells, sides, width):
    for axis, dim in sides:
        count = lax.axis_size(axis)
        head = lax.slice_in_dim(cells, 0, width, axis=dim)
        tail = lax.slice_in_dim(cells, cells.shape[dim] - width, cells.shape[dim], axis=dim)
        cells = jnp.concatenate(
            [
                lax.ppermute(tail, axis, [(i, (i + 1) % count) for i in range(count)]),
                cells,
                lax.ppermute(head, axis, [((i + 1) % count, i) for i in range(count)]),
            ],
            axis=dim,
        )
    return cells


def bell(delta, period, scale):
    delta = delta % period
    dist = jnp.minimum(delta, period - delta).astype(jnp.float32)
    return jnp.exp(-0.5 * (dist / scale) ** 2)


def advance_rows(haloed_extended_grid, courant_row, courant_column, diffusion):
    centre = haloed_extended_grid[1:-1]
    north = haloed_extended_grid[:-2]
    south = haloed_extended_grid[2:]
    west = jnp.roll(centre, 1, axis=1)
    east = jnp.roll(centre, -1, axis=1)
    return (
        centre
        - 0.5 * courant_column * (east - west)
        - 0.5 * courant_row * (south - north)
        + diffusion * (north + south + east + west - 4.0 * centre)
    )


def measured_kalman_gain(prior, values, variance, noise):
    members = prior.shape[0]
    anomaly = prior - jnp.mean(prior, axis=0)
    spread = jnp.dot(anomaly.T, anomaly, precision=HIGH, preferred_element_type=jnp.float32) / (
        members - 1
    )
    system = spread + jnp.diag(variance)
    factor = jnp.linalg.cholesky(system)
    innovation = values[:, None] + jnp.sqrt(variance)[:, None] * noise - prior.T
    weights = jax.scipy.linalg.cho_solve((factor, True), innovation)
    return (anomaly, weights)


def increment(columns, anomaly, weights, taper):
    members = columns.shape[0]
    centred = columns - jnp.mean(columns, axis=0)
    cross = lax.dot_general(
        centred,
        anomaly,
        (((0,), (0,)), ((), ())),
        precision=HIGH,
        preferred_element_type=jnp.float32,
    ) / (members - 1)
    return columns + lax.dot_general(
        weights,
        taper * cross,
        (((0,), (1,)), ((), ())),
        precision=HIGH,
        preferred_element_type=jnp.float32,
    )


def on_slabs(
    prior_tracer_draws,
    courant_row,
    courant_column,
    diffusion,
    obs_value,
    observation_variance,
    obs_noise,
    obs_owner,
    obs_cell,
    obs_order,
):
    region_rows = prior_tracer_draws.shape[1]
    columns = prior_tracer_draws.shape[2]
    mem_count = lax.axis_size("mem")
    reg_count = lax.axis_size("reg")
    slab_rows = region_rows // mem_count
    grid_rows = region_rows * reg_count
    latitude_weighting = region_rows // 2
    col_scale = columns // 4
    rate_row = courant_row.astype(jnp.float32)
    column_rate = courant_column.astype(jnp.float32)
    rate_diff = diffusion.astype(jnp.float32)
    field = prior_tracer_draws[0]
    for step in range(2):
        haloed_extended_grid = extended(field, (("reg", 0),), 1)
        field = advance_rows(haloed_extended_grid, rate_row, column_rate, rate_diff)
    slabs = lax.all_to_all(field[None], "mem", split_axis=1, concat_axis=0, tiled=True)
    members = slabs.shape[0]
    cells = slabs.reshape(members, slab_rows * columns)
    me_mem = lax.axis_index("mem")
    me_reg = lax.axis_index("reg")
    myself = me_mem * reg_count + me_reg
    owned_rows = me_reg * region_rows + me_mem * slab_rows + jnp.arange(slab_rows, dtype=jnp.int32)
    obs_row = (
        obs_owner % reg_count * region_rows
        + obs_owner // reg_count * slab_rows
        + obs_cell // columns
    )
    observation_column = obs_cell % columns
    col_index = jnp.arange(columns, dtype=jnp.int32)
    owners = obs_owner[obs_order]
    spots = obs_cell[obs_order]
    sorted_row = obs_row[obs_order]
    sorted_col = observation_column[obs_order]
    local = jnp.where((owners == myself)[None, :], cells[:, spots], 0.0)
    priors = lax.psum(local, ("mem", "reg"))
    for block in range(NBLK):
        lower = block * NOB
        upper = (block + 1) * NOB
        chosen = obs_order[lower:upper]
        prior = priors[:, lower:upper]
        anomaly, weights = measured_kalman_gain(
            prior, obs_value[chosen], observation_variance[chosen], obs_noise[chosen]
        )
        orow = sorted_row[lower:upper]
        ocol = sorted_col[lower:upper]
        row_taper = bell(owned_rows[:, None] - orow[None, :], grid_rows, latitude_weighting)
        col_taper = bell(col_index[:, None] - ocol[None, :], columns, col_scale)
        cells = increment(
            cells,
            anomaly,
            weights,
            (row_taper[:, None, :] * col_taper[None, :, :]).reshape(
                slab_rows * columns, orow.shape[0]
            ),
        )
        obs_taper = bell(sorted_row[:, None] - orow[None, :], grid_rows, latitude_weighting) * bell(
            sorted_col[:, None] - ocol[None, :], columns, col_scale
        )
        priors = increment(priors, anomaly, weights, obs_taper)
    return lax.all_to_all(
        cells.reshape(members, slab_rows, columns), "mem", split_axis=0, concat_axis=1, tiled=True
    )


SUBLANES = 8
LANES = 128
POINTS = [(dr, dc) for dr in range(-2, 3) for dc in range(-2, 3) if abs(dr) + abs(dc) <= 2]
CROSS = [(0, 0), (-1, 0), (1, 0), (0, -1), (0, 1)]
TILES = -(-(len(POINTS) + 3 * len(CROSS)) // SUBLANES)
PARTS = 4


def iota(axis, shape=(SUBLANES, LANES)):
    return lax.broadcasted_iota(jnp.int32, shape, axis)


def row_of(x, i):
    return jnp.broadcast_to(x[i : i + 1, :], x.shape)


def stencil(q, north, south, rate_row, rate_col, rate_diff):
    columns = q.shape[1]
    west = pltpu.roll(q, 1, axis=1)
    east = pltpu.roll(q, columns - 1, axis=1)
    return (
        q
        - 0.5 * rate_col * (east - west)
        - 0.5 * rate_row * (south - north)
        + rate_diff * (north + south + east + west - 4.0 * q)
    )


def slot(c):
    return c % SUBLANES, c // SUBLANES * LANES


def start_kernel(
    sizes,
    q_ref,
    row_ref,
    col_ref,
    diff_ref,
    owner_ref,
    cell_ref,
    order_ref,
    value_ref,
    variance_ref,
    noise_ref,
    down_ref,
    up_ref,
    points_ref,
    partial_ref,
    sorted_ref,
    noise_out,
):
    reg_count, region_rows, slab_rows, columns = sizes
    grid_rows = reg_count * region_rows
    packed = columns // SUBLANES
    me = lax.axis_index("reg")
    sub = iota(0)
    owner = owner_ref[...]
    cell = cell_ref[...]
    shift = columns.bit_length() - 1
    obs_row = (
        (owner & (reg_count - 1)) * region_rows
        + (owner >> (reg_count.bit_length() - 1)) * slab_rows
        + (cell >> shift)
    )
    obs_col = cell & (columns - 1)
    table = jnp.where(
        sub == 0,
        obs_row.astype(jnp.float32),
        jnp.where(
            sub == 1,
            obs_col.astype(jnp.float32),
            jnp.where(sub == 2, value_ref[...], jnp.where(sub == 3, variance_ref[...], 0.0)),
        ),
    )
    square = (LANES, LANES)
    pick = (iota(0, square) == order_ref[...]).astype(jnp.float32)
    both = jnp.dot(
        jnp.concatenate([table, noise_ref[...]], axis=0),
        pick,
        precision=HIGH,
        preferred_element_type=jnp.float32,
    )
    table = both[:SUBLANES]
    sorted_ref[...] = table
    noise_out[...] = both[SUBLANES:]
    orow = row_of(table, 0).astype(jnp.int32)
    ocol = row_of(table, 1).astype(jnp.int32)

    q = q_ref[0]
    rates = [r[...].astype(jnp.float32) for r in (row_ref, col_ref, diff_ref)]
    local_row = orow - me * region_rows
    for dc in range(-2, 3):
        index = (ocol + dc) & (columns - 1)
        lane = index & (LANES - 1)
        tile = index >> (LANES.bit_length() - 1)
        wanted = [(q, 0, POINTS)]
        if abs(dc) <= 1:
            for n, rate in enumerate(rates):
                wanted.append((rate, len(POINTS) + n * len(CROSS), CROSS))
        hits = [tile == t for t in range(columns // LANES)]
        for array, base, points in wanted:
            found = jnp.zeros((SUBLANES, LANES), jnp.float32)
            for t in range(columns // LANES):
                taken = jnp.take_along_axis(
                    array[:, t * LANES : (t + 1) * LANES], lane, axis=1, mode="promise_in_bounds"
                )
                found = jnp.where(hits[t], taken, found)
            for n, (dr, shift_col) in enumerate(points):
                if shift_col != dc:
                    continue
                here = ((local_row + dr) & (grid_rows - 1)) == sub
                s, at = slot(base + n)
                points_ref[s : s + 1, at : at + LANES] = jnp.sum(
                    jnp.where(here, found, 0.0), axis=0, keepdims=True
                )
    for c in range(len(POINTS) + 3 * len(CROSS), TILES * SUBLANES):
        s, at = slot(c)
        points_ref[s : s + 1, at : at + LANES] = jnp.zeros((1, LANES), jnp.float32)

    rate_row, rate_col, rate_diff = rates
    wide = iota(0, (SUBLANES, columns))
    north = jnp.where(wide == 0, 0.0, pltpu.roll(q, 1, axis=0))
    south = jnp.where(wide == SUBLANES - 1, 0.0, pltpu.roll(q, SUBLANES - 1, axis=0))
    partial = stencil(q, north, south, rate_row, rate_col, rate_diff)
    partial_ref[...] = partial
    for ref, edge, missing in (
        (down_ref, SUBLANES - 1, rate_diff - 0.5 * rate_row),
        (up_ref, 0, rate_diff + 0.5 * rate_row),
    ):
        for n, array in enumerate((q, partial, missing)):
            for s in range(SUBLANES):
                ref[s : s + 1, n * packed : (n + 1) * packed] = array[
                    edge : edge + 1, s * packed : (s + 1) * packed
                ]
        ref[:, 3 * packed :] = points_ref[...]


def bell_of(dist, period, scale):
    dist = jnp.abs(dist)
    dist = jnp.minimum(dist, period - dist) / scale
    return jnp.exp(-0.5 * (dist * dist))


def halves(x):
    high = x.astype(jnp.bfloat16)
    return high, (x - high.astype(jnp.float32)).astype(jnp.bfloat16)


def taper_kernel(sizes, sorted_ref, columns_ref, obs_ref, rows_ref):
    reg_count, region_rows, slab_rows, columns = sizes
    width = columns // PARTS
    grid_rows = reg_count * region_rows
    row_scale, col_scale = float(region_rows // 2), float(columns // 4)
    part = lax.axis_index("mem") % PARTS
    me = lax.axis_index("reg")
    square = (LANES, LANES)
    row_lanes = jnp.broadcast_to(sorted_ref[0:1, :], square)
    col_lanes = jnp.broadcast_to(sorted_ref[1:2, :], square)
    row_subs = row_lanes.T
    col_subs = col_lanes.T
    for t in range(width // LANES):
        at = (part * width + t * LANES + iota(1, square)).astype(jnp.float32)
        high, low = halves(bell_of(at - col_subs, float(columns), col_scale))
        columns_ref[0, :, t * LANES : (t + 1) * LANES] = high
        columns_ref[1, :, t * LANES : (t + 1) * LANES] = low
    high, low = halves(
        bell_of(row_lanes - row_subs, float(grid_rows), row_scale)
        * bell_of(col_lanes - col_subs, float(columns), col_scale)
    )
    obs_ref[0] = high
    obs_ref[1] = low
    rows = (me * region_rows + iota(0)).astype(jnp.float32)
    rows_ref[...] = bell_of(rows - row_lanes[:SUBLANES], float(grid_rows), row_scale)


def middle_kernel(
    sizes,
    partial_ref,
    row_ref,
    col_ref,
    diff_ref,
    down_ref,
    up_ref,
    points_ref,
    above_ref,
    below_ref,
    far_ref,
    out_ref,
    edge_ref,
):
    reg_count, region_rows, slab_rows, columns = sizes
    packed = columns // SUBLANES
    width = columns // PARTS
    wide = iota(0, (SUBLANES, columns))
    rate_row, rate_col, rate_diff = [
        r[...].astype(jnp.float32) for r in (row_ref, col_ref, diff_ref)
    ]

    def section(ref, n):
        return ref[:, n * packed : (n + 1) * packed]

    outer = (
        section(above_ref, 0),
        section(below_ref, 0),
        section(above_ref, 1) + section(above_ref, 2) * section(up_ref, 0),
        section(below_ref, 1) + section(below_ref, 2) * section(down_ref, 0),
    )
    for n, array in enumerate(outer):
        for s in range(SUBLANES):
            edge_ref[n : n + 1, s * packed : (s + 1) * packed] = array[s : s + 1, :]

    def edge(n):
        return jnp.broadcast_to(edge_ref[n : n + 1, :], (SUBLANES, columns))

    first, last = wide == 0, wide == SUBLANES - 1
    field = (
        partial_ref[...]
        + jnp.where(first, (rate_diff + 0.5 * rate_row) * edge(0), 0.0)
        + jnp.where(last, (rate_diff - 0.5 * rate_row) * edge(1), 0.0)
    )
    north = jnp.where(first, edge(2), pltpu.roll(field, 1, axis=0))
    south = jnp.where(last, edge(3), pltpu.roll(field, SUBLANES - 1, axis=0))
    field = stencil(field, north, south, rate_row, rate_col, rate_diff)

    points = points_ref[...] + far_ref[...] + above_ref[:, 3 * packed :] + below_ref[:, 3 * packed :]

    def point(c):
        s, at = slot(c)
        return points[s : s + 1, at : at + LANES]

    q0 = {p: point(n) for n, p in enumerate(POINTS)}
    rates = [
        {p: point(len(POINTS) + n * len(CROSS) + i) for i, p in enumerate(CROSS)} for n in range(3)
    ]

    def at_point(values, p):
        i, j = p
        here = values[p]
        north, south = values[i - 1, j], values[i + 1, j]
        west, east = values[i, j - 1], values[i, j + 1]
        return (
            here
            - 0.5 * rates[1][p] * (east - west)
            - 0.5 * rates[0][p] * (south - north)
            + rates[2][p] * (north + south + east + west - 4.0 * here)
        )

    q1 = {p: at_point(q0, p) for p in CROSS}
    seen = jnp.broadcast_to(at_point(q1, (0, 0)), (SUBLANES, LANES))
    for d in range(out_ref.shape[0]):
        g = d % PARTS
        out_ref[d, :, :width] = field[:, g * width : (g + 1) * width]
        out_ref[d, :, width:] = seen


def gain(anomaly, precision, innovation):
    members = anomaly.shape[0]
    sub = iota(0)
    weighted = anomaly * precision

    def against(x):
        total = jnp.sum(weighted * x, axis=1, keepdims=True)
        return jnp.broadcast_to(total, weighted.shape)

    system = [
        against(row_of(anomaly, b)) + jnp.where(sub == b, float(members - 1), 0.0)
        for b in range(members)
    ]
    load = [against(row_of(innovation, m)) for m in range(members)]
    held = anomaly
    for k in range(members):
        inverse = 1.0 / row_of(system[k], k)
        mine = sub == k

        def step(x, k=k, inverse=inverse, mine=mine):
            scaled = row_of(x, k) * inverse
            return jnp.where(mine, scaled, x - system[k] * scaled)

        held = step(held)
        for b in range(k + 1, members):
            system[b] = step(system[b])
    fitted = jnp.zeros_like(anomaly)
    for m in range(members):
        total = jnp.sum(load[m] * held, axis=0, keepdims=True)
        fitted = jnp.where(sub == m, jnp.broadcast_to(total, held.shape), fitted)
    return precision * (innovation - fitted)


def twice(x, block):
    lane = iota(1)
    half = LANES // 2
    return jnp.where(lane // half == block, x, pltpu.roll(x, half, axis=1))


def weigh(rows, table_ref, block):
    half = LANES // 2
    lane = iota(1, rows.shape)
    high = rows.astype(jnp.bfloat16).astype(jnp.float32)
    left = jnp.where(lane < half, high, rows - high).astype(jnp.bfloat16)
    high = table_ref[0, block * half : (block + 1) * half, :]
    low = table_ref[1, block * half : (block + 1) * half, :]
    return jnp.dot(
        jnp.concatenate([left, left], axis=1),
        jnp.concatenate([high, high, low, low], axis=0),
        preferred_element_type=jnp.float32,
    )


def finish_kernel(sizes, x_ref, sorted_ref, noise_ref, columns_ref, obs_ref, rows_ref, *outs):
    reg_count, region_rows, slab_rows, columns = sizes
    members = x_ref.shape[0]
    width = columns // PARTS
    now_ref = outs[-1]
    outs = outs[:-1]
    me = lax.axis_index("mem")
    sub, lane = iota(0), iota(1)
    half = LANES // 2
    seen = jnp.zeros((SUBLANES, LANES), jnp.float32)
    for m in range(members):
        seen = jnp.where(sub == m, x_ref[m, :, width:], seen)
    value, variance = row_of(sorted_ref, 2), row_of(sorted_ref, 3)
    observed = value + jnp.sqrt(variance) * noise_ref[...]
    inverse_variance = 1.0 / variance
    scale = 1.0 / (members - 1)
    current = [x_ref[m, :, :width] for m in range(members)]
    for block in range(NBLK):
        anomaly = seen - jnp.sum(seen, axis=0, keepdims=True) * (1.0 / members)
        precision = jnp.where(lane // half == block, inverse_variance, 0.0)
        gains = gain(anomaly, precision, observed - seen) * scale
        gains, local = twice(gains, block), twice(anomaly, block)
        pairs = [row_of(local, a) * gains for a in range(members)]
        if block + 1 < NBLK:
            moved = weigh(jnp.concatenate(pairs, axis=0), obs_ref, block)
            for a in range(members):
                seen = seen + row_of(anomaly, a) * moved[a * SUBLANES : (a + 1) * SUBLANES]
        row_taper = twice(rows_ref[...], block)
        mean = sum(current[1:], current[0]) * (1.0 / members)
        centred = [x - mean for x in current]
        if block + 1 < NBLK:
            chosen = list(range(members))
            terms = [
                [row_taper * row_of(pairs[a], m) for m in chosen] for a in range(members)
            ]
            start = current
        else:
            for m in range(members):
                now_ref[m] = current[m]
            chosen = list(range(PARTS))
            starts = [now_ref[me ^ x] for x in chosen]
            terms = []
            for a in range(members):
                held = pairs[a]
                row = []
                for x in chosen:
                    mine = jnp.sum(jnp.where(sub == (me ^ x), held, 0.0), axis=0, keepdims=True)
                    row.append(row_taper * mine)
                terms.append(row)
            start = starts
        weights = weigh(
            jnp.concatenate([t for row in terms for t in row], axis=0), columns_ref, block
        )
        updated = []
        for n in range(len(chosen)):
            total = start[n]
            for a in range(members):
                at = (a * len(chosen) + n) * SUBLANES
                total = total + centred[a] * weights[at : at + SUBLANES]
            updated.append(total)
        current = updated
    for ref, x in zip(outs, current):
        ref[...] = x


def join_kernel(columns, *refs):
    out_ref = refs[-1]
    width = columns // PARTS
    me = lax.axis_index("mem")
    for x, ref in enumerate(refs[:-1]):
        part = (me ^ x) % PARTS
        out_ref[0, :, pl.ds(pl.multiple_of(part * width, LANES), width)] = ref[...]


def call(kernel, outs, args, scratch=(), cost=None):
    space = pl.BlockSpec(memory_space=pltpu.VMEM)
    return pl.pallas_call(
        kernel,
        out_shape=[jax.ShapeDtypeStruct(s, d) for s, d in outs],
        in_specs=[space] * len(args),
        out_specs=[space] * len(outs),
        scratch_shapes=list(scratch),
        cost_estimate=cost,
    )(*args)


def on_tile(
    prior_tracer_draws,
    courant_row,
    courant_column,
    diffusion,
    obs_value,
    observation_variance,
    obs_noise,
    obs_owner,
    obs_cell,
    obs_order,
):
    f32 = jnp.float32
    region_rows, columns = prior_tracer_draws.shape[1:]
    members = obs_noise.shape[1]
    mem_count, reg_count = lax.axis_size("mem"), lax.axis_size("reg")
    sizes = (reg_count, region_rows, region_rows // mem_count, columns)
    packed = columns // SUBLANES
    width = columns // PARTS
    tile = (SUBLANES, LANES)
    field = (SUBLANES, columns)
    points_shape = (SUBLANES, TILES * LANES)
    message = (SUBLANES, 3 * packed + TILES * LANES)
    rates = (courant_row, courant_column, diffusion)
    flat = [x.reshape(1, LANES) for x in (obs_owner, obs_cell, obs_order, obs_value, observation_variance)]
    down, up, points, partial, table, noise = call(
        functools.partial(start_kernel, sizes),
        [(message, f32), (message, f32), (points_shape, f32), (field, f32), (tile, f32), (tile, f32)],
        (prior_tracer_draws, *rates, *flat, obs_noise.T),
    )

    def shifted(x, by):
        return lax.ppermute(x, "reg", [(i, (i + by) % reg_count) for i in range(reg_count)])

    above = shifted(down, 1)
    below = shifted(up, -1)
    far = [shifted(points, by) for by in range(2, reg_count - 1)]
    col_taper, obs_taper, row_taper = call(
        functools.partial(taper_kernel, sizes),
        [((2, LANES, width), jnp.bfloat16), ((2, LANES, LANES), jnp.bfloat16), (tile, f32)],
        (table,),
        cost=pl.CostEstimate(flops=10 * LANES * width, bytes_accessed=8 * LANES * width, transcendentals=LANES * width),
    )
    (send,) = call(
        functools.partial(middle_kernel, sizes),
        [((mem_count, SUBLANES, width + LANES), f32)],
        (partial, *rates, down, up, points, above, below, sum(far[1:], far[0])),
        scratch=[pltpu.VMEM(field, f32)],
    )
    slabs = lax.all_to_all(send, "mem", split_axis=0, concat_axis=0, tiled=True)
    pieces = call(
        functools.partial(finish_kernel, sizes),
        [((SUBLANES, width), f32)] * PARTS,
        (slabs, table, noise, col_taper, obs_taper, row_taper),
        scratch=[pltpu.VMEM((members, SUBLANES, width), f32)],
    )
    back = [pieces[0]] + [
        lax.ppermute(pieces[x], "mem", [(i, i ^ x) for i in range(mem_count)]) for x in range(1, PARTS)
    ]
    (out,) = call(
        functools.partial(join_kernel, columns), [(prior_tracer_draws.shape, f32)], back
    )
    return out


def fits_tile(*shapes):
    draws, noise = shapes
    members, region_rows, columns = draws
    counts = (lax.axis_size("mem"), lax.axis_size("reg"))
    return (
        members == 1
        and noise[1] == counts[0] == region_rows == SUBLANES
        and noise[0] == NOB * NBLK == LANES
        and counts[1] == PARTS
        and columns % (PARTS * LANES) == 0
        and columns & (columns - 1) == 0
    )


def on_device(*args):
    return (on_tile if fits_tile(args[0].shape, args[6].shape) else on_slabs)(*args)


def solution(mesh):
    placed = (
        P("mem", "reg", None),
        P("reg", None),
        P("reg", None),
        P("reg", None),
        P(),
        P(),
        P(),
        P(),
        P(),
        P(),
    )
    return jax.shard_map(
        on_device, mesh=mesh, in_specs=placed, out_specs=P("mem", "reg", None), check_vma=False
    )
```

```python
import functools

import jax
import jax.numpy as jnp
from jax import lax
from jax.experimental import pallas as pl
from jax.experimental.pallas import tpu as pltpu
from jax.sharding import PartitionSpec as P

NOB = 64
NBLK = 2


HIGH = lax.Precision.HIGHEST


def extended(cells, sides, width):
    for axis, dim in sides:
        count = lax.axis_size(axis)
        head = lax.slice_in_dim(cells, 0, width, axis=dim)
        tail = lax.slice_in_dim(cells, cells.shape[dim] - width, cells.shape[dim], axis=dim)
        cells = jnp.concatenate(
            [
                lax.ppermute(tail, axis, [(i, (i + 1) % count) for i in range(count)]),
                cells,
                lax.ppermute(head, axis, [((i + 1) % count, i) for i in range(count)]),
            ],
            axis=dim,
        )
    return cells


def bell(delta, period, scale):
    delta = delta % period
    dist = jnp.minimum(delta, period - delta).astype(jnp.float32)
    return jnp.exp(-0.5 * (dist / scale) ** 2)


def advance_rows(haloed_extended_grid, courant_row, courant_column, diffusion):
    centre = haloed_extended_grid[1:-1]
    north = haloed_extended_grid[:-2]
    south = haloed_extended_grid[2:]
    west = jnp.roll(centre, 1, axis=1)
    east = jnp.roll(centre, -1, axis=1)
    return (
        centre
        - 0.5 * courant_column * (east - west)
        - 0.5 * courant_row * (south - north)
        + diffusion * (north + south + east + west - 4.0 * centre)
    )


def measured_kalman_gain(prior, values, variance, noise):
    members = prior.shape[0]
    anomaly = prior - jnp.mean(prior, axis=0)
    spread = jnp.dot(anomaly.T, anomaly, precision=HIGH, preferred_element_type=jnp.float32) / (
        members - 1
    )
    system = spread + jnp.diag(variance)
    factor = jnp.linalg.cholesky(system)
    innovation = values[:, None] + jnp.sqrt(variance)[:, None] * noise - prior.T
    weights = jax.scipy.linalg.cho_solve((factor, True), innovation)
    return (anomaly, weights)


def increment(columns, anomaly, weights, taper):
    members = columns.shape[0]
    centred = columns - jnp.mean(columns, axis=0)
    cross = lax.dot_general(
        centred,
        anomaly,
        (((0,), (0,)), ((), ())),
        precision=HIGH,
        preferred_element_type=jnp.float32,
    ) / (members - 1)
    return columns + lax.dot_general(
        weights,
        taper * cross,
        (((0,), (1,)), ((), ())),
        precision=HIGH,
        preferred_element_type=jnp.float32,
    )


def on_slabs(
    prior_tracer_draws,
    courant_row,
    courant_column,
    diffusion,
    obs_value,
    observation_variance,
    obs_noise,
    obs_owner,
    obs_cell,
    obs_order,
):
    region_rows = prior_tracer_draws.shape[1]
    columns = prior_tracer_draws.shape[2]
    mem_count = lax.axis_size("mem")
    reg_count = lax.axis_size("reg")
    slab_rows = region_rows // mem_count
    grid_rows = region_rows * reg_count
    latitude_weighting = region_rows // 2
    col_scale = columns // 4
    rate_row = courant_row.astype(jnp.float32)
    column_rate = courant_column.astype(jnp.float32)
    rate_diff = diffusion.astype(jnp.float32)
    field = prior_tracer_draws[0]
    for step in range(2):
        haloed_extended_grid = extended(field, (("reg", 0),), 1)
        field = advance_rows(haloed_extended_grid, rate_row, column_rate, rate_diff)
    slabs = lax.all_to_all(field[None], "mem", split_axis=1, concat_axis=0, tiled=True)
    members = slabs.shape[0]
    cells = slabs.reshape(members, slab_rows * columns)
    me_mem = lax.axis_index("mem")
    me_reg = lax.axis_index("reg")
    myself = me_mem * reg_count + me_reg
    owned_rows = me_reg * region_rows + me_mem * slab_rows + jnp.arange(slab_rows, dtype=jnp.int32)
    obs_row = (
        obs_owner % reg_count * region_rows
        + obs_owner // reg_count * slab_rows
        + obs_cell // columns
    )
    observation_column = obs_cell % columns
    col_index = jnp.arange(columns, dtype=jnp.int32)
    owners = obs_owner[obs_order]
    spots = obs_cell[obs_order]
    sorted_row = obs_row[obs_order]
    sorted_col = observation_column[obs_order]
    local = jnp.where((owners == myself)[None, :], cells[:, spots], 0.0)
    priors = lax.psum(local, ("mem", "reg"))
    for block in range(NBLK):
        lower = block * NOB
        upper = (block + 1) * NOB
        chosen = obs_order[lower:upper]
        prior = priors[:, lower:upper]
        anomaly, weights = measured_kalman_gain(
            prior, obs_value[chosen], observation_variance[chosen], obs_noise[chosen]
        )
        orow = sorted_row[lower:upper]
        ocol = sorted_col[lower:upper]
        row_taper = bell(owned_rows[:, None] - orow[None, :], grid_rows, latitude_weighting)
        col_taper = bell(col_index[:, None] - ocol[None, :], columns, col_scale)
        cells = increment(
            cells,
            anomaly,
            weights,
            (row_taper[:, None, :] * col_taper[None, :, :]).reshape(
                slab_rows * columns, orow.shape[0]
            ),
        )
        obs_taper = bell(sorted_row[:, None] - orow[None, :], grid_rows, latitude_weighting) * bell(
            sorted_col[:, None] - ocol[None, :], columns, col_scale
        )
        priors = increment(priors, anomaly, weights, obs_taper)
    return lax.all_to_all(
        cells.reshape(members, slab_rows, columns), "mem", split_axis=0, concat_axis=1, tiled=True
    )


SUBLANES = 8
LANES = 128
POINTS = [(dr, dc) for dr in range(-2, 3) for dc in range(-2, 3) if abs(dr) + abs(dc) <= 2]
CROSS = [(0, 0), (-1, 0), (1, 0), (0, -1), (0, 1)]
TILES = -(-(len(POINTS) + 3 * len(CROSS)) // SUBLANES)
PARTS = 4
VMEM_GRANT = 8 << 20


def iota(axis, shape=(SUBLANES, LANES)):
    return lax.broadcasted_iota(jnp.int32, shape, axis)


def row_of(x, i):
    return jnp.broadcast_to(x[i : i + 1, :], x.shape)


def stencil(q, north, south, rate_row, rate_col, rate_diff):
    columns = q.shape[1]
    west = pltpu.roll(q, 1, axis=1)
    east = pltpu.roll(q, columns - 1, axis=1)
    return (
        q
        - 0.5 * rate_col * (east - west)
        - 0.5 * rate_row * (south - north)
        + rate_diff * (north + south + east + west - 4.0 * q)
    )


def slot(c):
    return c % SUBLANES, c // SUBLANES * LANES


def start_kernel(
    sizes,
    q_hbm,
    row_hbm,
    col_hbm,
    diff_hbm,
    owner_hbm,
    cell_hbm,
    order_hbm,
    value_hbm,
    variance_hbm,
    noise_hbm,
    down_ref,
    up_ref,
    points_ref,
    partial_ref,
    sorted_ref,
    noise_out,
    row_ref,
    col_ref,
    diff_ref,
    q_ref,
    owner_ref,
    cell_ref,
    order_ref,
    value_ref,
    variance_ref,
    noise_ref,
    arrived,
):
    fetched = (
        (owner_hbm, owner_ref),
        (cell_hbm, cell_ref),
        (order_hbm, order_ref),
        (value_hbm, value_ref),
        (variance_hbm, variance_ref),
        (noise_hbm, noise_ref),
        (q_hbm, q_ref),
        (row_hbm, row_ref),
        (col_hbm, col_ref),
        (diff_hbm, diff_ref),
    )
    copies = [
        pltpu.make_async_copy(source, target, arrived.at[n])
        for n, (source, target) in enumerate(fetched)
    ]
    for copy in copies:
        copy.start()
    for copy in copies[:6]:
        copy.wait()
    reg_count, region_rows, slab_rows, columns = sizes
    grid_rows = reg_count * region_rows
    packed = columns // SUBLANES
    me = lax.axis_index("reg")
    sub = iota(0)
    owner = owner_ref[...]
    cell = cell_ref[...]
    shift = columns.bit_length() - 1
    obs_row = (
        (owner & (reg_count - 1)) * region_rows
        + (owner >> (reg_count.bit_length() - 1)) * slab_rows
        + (cell >> shift)
    )
    obs_col = cell & (columns - 1)
    table = jnp.where(
        sub == 0,
        obs_row.astype(jnp.float32),
        jnp.where(
            sub == 1,
            obs_col.astype(jnp.float32),
            jnp.where(sub == 2, value_ref[...], jnp.where(sub == 3, variance_ref[...], 0.0)),
        ),
    )
    square = (LANES, LANES)
    pick = (iota(0, square) == order_ref[...]).astype(jnp.float32)
    both = jnp.dot(
        jnp.concatenate([table, noise_ref[...]], axis=0),
        pick,
        precision=HIGH,
        preferred_element_type=jnp.float32,
    )
    table = both[:SUBLANES]
    sorted_ref[...] = table
    noise_out[...] = both[SUBLANES:]
    orow = row_of(table, 0).astype(jnp.int32)
    ocol = row_of(table, 1).astype(jnp.int32)

    for copy in copies[6:]:
        copy.wait()
    q = q_ref[0]
    rates = [r[...].astype(jnp.float32) for r in (row_ref, col_ref, diff_ref)]
    local_row = orow - me * region_rows
    for dc in range(-2, 3):
        index = (ocol + dc) & (columns - 1)
        lane = index & (LANES - 1)
        tile = index >> (LANES.bit_length() - 1)
        wanted = [(q, 0, POINTS)]
        if abs(dc) <= 1:
            for n, rate in enumerate(rates):
                wanted.append((rate, len(POINTS) + n * len(CROSS), CROSS))
        hits = [tile == t for t in range(columns // LANES)]
        for array, base, points in wanted:
            found = jnp.zeros((SUBLANES, LANES), jnp.float32)
            for t in range(columns // LANES):
                taken = jnp.take_along_axis(
                    array[:, t * LANES : (t + 1) * LANES], lane, axis=1, mode="promise_in_bounds"
                )
                found = jnp.where(hits[t], taken, found)
            for n, (dr, shift_col) in enumerate(points):
                if shift_col != dc:
                    continue
                here = ((local_row + dr) & (grid_rows - 1)) == sub
                s, at = slot(base + n)
                points_ref[s : s + 1, at : at + LANES] = jnp.sum(
                    jnp.where(here, found, 0.0), axis=0, keepdims=True
                )
    for c in range(len(POINTS) + 3 * len(CROSS), TILES * SUBLANES):
        s, at = slot(c)
        points_ref[s : s + 1, at : at + LANES] = jnp.zeros((1, LANES), jnp.float32)

    rate_row, rate_col, rate_diff = rates
    wide = iota(0, (SUBLANES, columns))
    north = jnp.where(wide == 0, 0.0, pltpu.roll(q, 1, axis=0))
    south = jnp.where(wide == SUBLANES - 1, 0.0, pltpu.roll(q, SUBLANES - 1, axis=0))
    partial = stencil(q, north, south, rate_row, rate_col, rate_diff)
    partial_ref[...] = partial
    for ref, edge, missing in (
        (down_ref, SUBLANES - 1, rate_diff - 0.5 * rate_row),
        (up_ref, 0, rate_diff + 0.5 * rate_row),
    ):
        for n, array in enumerate((q, partial, missing)):
            for s in range(SUBLANES):
                ref[s : s + 1, n * packed : (n + 1) * packed] = array[
                    edge : edge + 1, s * packed : (s + 1) * packed
                ]
        ref[:, 3 * packed :] = points_ref[...]


def bell_of(dist, period, scale):
    dist = jnp.abs(dist)
    dist = jnp.minimum(dist, period - dist) / scale
    return jnp.exp(-0.5 * (dist * dist))


def halves(x):
    high = x.astype(jnp.bfloat16)
    return high, (x - high.astype(jnp.float32)).astype(jnp.bfloat16)


def taper_kernel(sizes, sorted_ref, columns_ref, obs_ref, rows_ref):
    reg_count, region_rows, slab_rows, columns = sizes
    width = columns // PARTS
    grid_rows = reg_count * region_rows
    row_scale, col_scale = float(region_rows // 2), float(columns // 4)
    part = lax.axis_index("mem") % PARTS
    me = lax.axis_index("reg")
    square = (LANES, LANES)
    row_lanes = jnp.broadcast_to(sorted_ref[0:1, :], square)
    col_lanes = jnp.broadcast_to(sorted_ref[1:2, :], square)
    row_subs = row_lanes.T
    col_subs = col_lanes.T
    for t in range(width // LANES):
        at = (part * width + t * LANES + iota(1, square)).astype(jnp.float32)
        high, low = halves(bell_of(at - col_subs, float(columns), col_scale))
        columns_ref[0, :, t * LANES : (t + 1) * LANES] = high
        columns_ref[1, :, t * LANES : (t + 1) * LANES] = low
    high, low = halves(
        bell_of(row_lanes - row_subs, float(grid_rows), row_scale)
        * bell_of(col_lanes - col_subs, float(columns), col_scale)
    )
    obs_ref[0] = high
    obs_ref[1] = low
    rows = (me * region_rows + iota(0)).astype(jnp.float32)
    rows_ref[...] = bell_of(rows - row_lanes[:SUBLANES], float(grid_rows), row_scale)


def middle_kernel(
    sizes,
    partial_ref,
    row_ref,
    col_ref,
    diff_ref,
    down_ref,
    up_ref,
    points_ref,
    above_ref,
    below_ref,
    far_ref,
    out_ref,
    edge_ref,
):
    reg_count, region_rows, slab_rows, columns = sizes
    packed = columns // SUBLANES
    width = columns // PARTS
    wide = iota(0, (SUBLANES, columns))
    rate_row, rate_col, rate_diff = [
        r[...].astype(jnp.float32) for r in (row_ref, col_ref, diff_ref)
    ]

    def section(ref, n):
        return ref[:, n * packed : (n + 1) * packed]

    outer = (
        section(above_ref, 0),
        section(below_ref, 0),
        section(above_ref, 1) + section(above_ref, 2) * section(up_ref, 0),
        section(below_ref, 1) + section(below_ref, 2) * section(down_ref, 0),
    )
    for n, array in enumerate(outer):
        for s in range(SUBLANES):
            edge_ref[n : n + 1, s * packed : (s + 1) * packed] = array[s : s + 1, :]

    def edge(n):
        return jnp.broadcast_to(edge_ref[n : n + 1, :], (SUBLANES, columns))

    first, last = wide == 0, wide == SUBLANES - 1
    field = (
        partial_ref[...]
        + jnp.where(first, (rate_diff + 0.5 * rate_row) * edge(0), 0.0)
        + jnp.where(last, (rate_diff - 0.5 * rate_row) * edge(1), 0.0)
    )
    north = jnp.where(first, edge(2), pltpu.roll(field, 1, axis=0))
    south = jnp.where(last, edge(3), pltpu.roll(field, SUBLANES - 1, axis=0))
    field = stencil(field, north, south, rate_row, rate_col, rate_diff)

    points = points_ref[...] + far_ref[...] + above_ref[:, 3 * packed :] + below_ref[:, 3 * packed :]

    def point(c):
        s, at = slot(c)
        return points[s : s + 1, at : at + LANES]

    q0 = {p: point(n) for n, p in enumerate(POINTS)}
    rates = [
        {p: point(len(POINTS) + n * len(CROSS) + i) for i, p in enumerate(CROSS)} for n in range(3)
    ]

    def at_point(values, p):
        i, j = p
        here = values[p]
        north, south = values[i - 1, j], values[i + 1, j]
        west, east = values[i, j - 1], values[i, j + 1]
        return (
            here
            - 0.5 * rates[1][p] * (east - west)
            - 0.5 * rates[0][p] * (south - north)
            + rates[2][p] * (north + south + east + west - 4.0 * here)
        )

    q1 = {p: at_point(q0, p) for p in CROSS}
    seen = jnp.broadcast_to(at_point(q1, (0, 0)), (SUBLANES, LANES))
    for d in range(out_ref.shape[0]):
        g = d % PARTS
        out_ref[d, :, :width] = field[:, g * width : (g + 1) * width]
        out_ref[d, :, width:] = seen


def gain(anomaly, precision, innovation):
    members = anomaly.shape[0]
    sub = iota(0)
    weighted = anomaly * precision

    def against(x):
        total = jnp.sum(weighted * x, axis=1, keepdims=True)
        return jnp.broadcast_to(total, weighted.shape)

    system = [
        against(row_of(anomaly, b)) + jnp.where(sub == b, float(members - 1), 0.0)
        for b in range(members)
    ]
    load = [against(row_of(innovation, m)) for m in range(members)]
    held = anomaly
    for k in range(members):
        inverse = 1.0 / row_of(system[k], k)
        mine = sub == k

        def step(x, k=k, inverse=inverse, mine=mine):
            scaled = row_of(x, k) * inverse
            return jnp.where(mine, scaled, x - system[k] * scaled)

        held = step(held)
        for b in range(k + 1, members):
            system[b] = step(system[b])
    fitted = jnp.zeros_like(anomaly)
    for m in range(members):
        total = jnp.sum(load[m] * held, axis=0, keepdims=True)
        fitted = jnp.where(sub == m, jnp.broadcast_to(total, held.shape), fitted)
    return precision * (innovation - fitted)


def twice(x, block):
    lane = iota(1)
    half = LANES // 2
    return jnp.where(lane // half == block, x, pltpu.roll(x, half, axis=1))


def weigh(rows, table_ref, block):
    half = LANES // 2
    lane = iota(1, rows.shape)
    high = rows.astype(jnp.bfloat16).astype(jnp.float32)
    left = jnp.where(lane < half, high, rows - high).astype(jnp.bfloat16)
    high = table_ref[0, block * half : (block + 1) * half, :]
    low = table_ref[1, block * half : (block + 1) * half, :]
    return jnp.dot(
        jnp.concatenate([left, left], axis=1),
        jnp.concatenate([high, high, low, low], axis=0),
        preferred_element_type=jnp.float32,
    )


def finish_kernel(sizes, x_ref, sorted_ref, noise_ref, columns_ref, obs_ref, rows_ref, *outs):
    reg_count, region_rows, slab_rows, columns = sizes
    members = x_ref.shape[0]
    width = columns // PARTS
    now_ref = outs[-1]
    outs = outs[:-1]
    me = lax.axis_index("mem")
    sub, lane = iota(0), iota(1)
    half = LANES // 2
    seen = jnp.zeros((SUBLANES, LANES), jnp.float32)
    for m in range(members):
        seen = jnp.where(sub == m, x_ref[m, :, width:], seen)
    value, variance = row_of(sorted_ref, 2), row_of(sorted_ref, 3)
    observed = value + jnp.sqrt(variance) * noise_ref[...]
    inverse_variance = 1.0 / variance
    scale = 1.0 / (members - 1)
    current = [x_ref[m, :, :width] for m in range(members)]
    for block in range(NBLK):
        anomaly = seen - jnp.sum(seen, axis=0, keepdims=True) * (1.0 / members)
        precision = jnp.where(lane // half == block, inverse_variance, 0.0)
        gains = gain(anomaly, precision, observed - seen) * scale
        gains, local = twice(gains, block), twice(anomaly, block)
        pairs = [row_of(local, a) * gains for a in range(members)]
        if block + 1 < NBLK:
            moved = weigh(jnp.concatenate(pairs, axis=0), obs_ref, block)
            for a in range(members):
                seen = seen + row_of(anomaly, a) * moved[a * SUBLANES : (a + 1) * SUBLANES]
        row_taper = twice(rows_ref[...], block)
        mean = sum(current[1:], current[0]) * (1.0 / members)
        centred = [x - mean for x in current]
        if block + 1 < NBLK:
            chosen = list(range(members))
            terms = [
                [row_taper * row_of(pairs[a], m) for m in chosen] for a in range(members)
            ]
            start = current
        else:
            for m in range(members):
                now_ref[m] = current[m]
            chosen = list(range(PARTS))
            starts = [now_ref[me ^ x] for x in chosen]
            terms = []
            for a in range(members):
                held = pairs[a]
                row = []
                for x in chosen:
                    mine = jnp.sum(jnp.where(sub == (me ^ x), held, 0.0), axis=0, keepdims=True)
                    row.append(row_taper * mine)
                terms.append(row)
            start = starts
        weights = weigh(
            jnp.concatenate([t for row in terms for t in row], axis=0), columns_ref, block
        )
        updated = []
        for n in range(len(chosen)):
            total = start[n]
            for a in range(members):
                at = (a * len(chosen) + n) * SUBLANES
                total = total + centred[a] * weights[at : at + SUBLANES]
            updated.append(total)
        current = updated
    for ref, x in zip(outs, current):
        ref[...] = x


def join_kernel(columns, *refs):
    out_ref = refs[-1]
    width = columns // PARTS
    me = lax.axis_index("mem")
    for x, ref in enumerate(refs[:-1]):
        part = (me ^ x) % PARTS
        out_ref[0, :, pl.ds(pl.multiple_of(part * width, LANES), width)] = ref[...]


def call(kernel, outs, args, scratch=(), cost=None, space=pltpu.VMEM):
    held = pl.BlockSpec(memory_space=pltpu.VMEM)
    return pl.pallas_call(
        kernel,
        out_shape=[jax.ShapeDtypeStruct(s, d) for s, d in outs],
        in_specs=[pl.BlockSpec(memory_space=space)] * len(args),
        out_specs=[held] * len(outs),
        scratch_shapes=list(scratch),
        cost_estimate=cost,
        compiler_params=pltpu.CompilerParams(vmem_limit_bytes=VMEM_GRANT),
    )(*args)


def on_tile(
    prior_tracer_draws,
    courant_row,
    courant_column,
    diffusion,
    obs_value,
    observation_variance,
    obs_noise,
    obs_owner,
    obs_cell,
    obs_order,
):
    f32 = jnp.float32
    region_rows, columns = prior_tracer_draws.shape[1:]
    members = obs_noise.shape[1]
    mem_count, reg_count = lax.axis_size("mem"), lax.axis_size("reg")
    sizes = (reg_count, region_rows, region_rows // mem_count, columns)
    packed = columns // SUBLANES
    width = columns // PARTS
    tile = (SUBLANES, LANES)
    field = (SUBLANES, columns)
    points_shape = (SUBLANES, TILES * LANES)
    message = (SUBLANES, 3 * packed + TILES * LANES)
    rates = (courant_row, courant_column, diffusion)
    flat = [x.reshape(1, LANES) for x in (obs_owner, obs_cell, obs_order, obs_value, observation_variance)]
    operands = (prior_tracer_draws, *rates, *flat, obs_noise.T)
    down, up, points, partial, table, noise, *rates = call(
        functools.partial(start_kernel, sizes),
        [(message, f32), (message, f32), (points_shape, f32), (field, f32), (tile, f32), (tile, f32)]
        + [(x.shape, x.dtype) for x in rates],
        [pltpu.with_memory_space_constraint(x, pltpu.HBM) for x in operands],
        scratch=[pltpu.VMEM(prior_tracer_draws.shape, f32)]
        + [pltpu.VMEM(x.shape, x.dtype) for x in operands[4:]]
        + [pltpu.SemaphoreType.DMA((len(operands),))],
        space=pltpu.HBM,
    )

    def shifted(x, by):
        return lax.ppermute(x, "reg", [(i, (i + by) % reg_count) for i in range(reg_count)])

    above = shifted(down, 1)
    below = shifted(up, -1)
    far = [shifted(points, by) for by in range(2, reg_count - 1)]
    col_taper, obs_taper, row_taper = call(
        functools.partial(taper_kernel, sizes),
        [((2, LANES, width), jnp.bfloat16), ((2, LANES, LANES), jnp.bfloat16), (tile, f32)],
        (table,),
        cost=pl.CostEstimate(flops=10 * LANES * width, bytes_accessed=8 * LANES * width, transcendentals=LANES * width),
    )
    (send,) = call(
        functools.partial(middle_kernel, sizes),
        [((mem_count, SUBLANES, width + LANES), f32)],
        (partial, *rates, down, up, points, above, below, sum(far[1:], far[0])),
        scratch=[pltpu.VMEM(field, f32)],
    )
    slabs = lax.all_to_all(send, "mem", split_axis=0, concat_axis=0, tiled=True)
    pieces = call(
        functools.partial(finish_kernel, sizes),
        [((SUBLANES, width), f32)] * PARTS,
        (slabs, table, noise, col_taper, obs_taper, row_taper),
        scratch=[pltpu.VMEM((members, SUBLANES, width), f32)],
    )
    back = [pieces[0]] + [
        lax.ppermute(pieces[x], "mem", [(i, i ^ x) for i in range(mem_count)]) for x in range(1, PARTS)
    ]
    (out,) = call(
        functools.partial(join_kernel, columns), [(prior_tracer_draws.shape, f32)], back
    )
    return out


def fits_tile(*shapes):
    draws, noise = shapes
    members, region_rows, columns = draws
    counts = (lax.axis_size("mem"), lax.axis_size("reg"))
    return (
        members == 1
        and noise[1] == counts[0] == region_rows == SUBLANES
        and noise[0] == NOB * NBLK == LANES
        and counts[1] == PARTS
        and columns % (PARTS * LANES) == 0
        and columns & (columns - 1) == 0
    )


def on_device(*args):
    return (on_tile if fits_tile(args[0].shape, args[6].shape) else on_slabs)(*args)


def solution(mesh):
    placed = (
        P("mem", "reg", None),
        P("reg", None),
        P("reg", None),
        P("reg", None),
        P(),
        P(),
        P(),
        P(),
        P(),
        P(),
    )
    return jax.shard_map(
        on_device, mesh=mesh, in_specs=placed, out_specs=P("mem", "reg", None), check_vma=False
    )
```

```python
import functools

import jax
import jax.numpy as jnp
from jax import lax
from jax.experimental import pallas as pl
from jax.experimental.pallas import tpu as pltpu
from jax.sharding import PartitionSpec as P

NOB = 64
NBLK = 2


HIGH = lax.Precision.HIGHEST


def extended(cells, sides, width):
    for axis, dim in sides:
        count = lax.axis_size(axis)
        head = lax.slice_in_dim(cells, 0, width, axis=dim)
        tail = lax.slice_in_dim(cells, cells.shape[dim] - width, cells.shape[dim], axis=dim)
        cells = jnp.concatenate(
            [
                lax.ppermute(tail, axis, [(i, (i + 1) % count) for i in range(count)]),
                cells,
                lax.ppermute(head, axis, [((i + 1) % count, i) for i in range(count)]),
            ],
            axis=dim,
        )
    return cells


def bell(delta, period, scale):
    delta = delta % period
    dist = jnp.minimum(delta, period - delta).astype(jnp.float32)
    return jnp.exp(-0.5 * (dist / scale) ** 2)


def advance_rows(haloed_extended_grid, courant_row, courant_column, diffusion):
    centre = haloed_extended_grid[1:-1]
    north = haloed_extended_grid[:-2]
    south = haloed_extended_grid[2:]
    west = jnp.roll(centre, 1, axis=1)
    east = jnp.roll(centre, -1, axis=1)
    return (
        centre
        - 0.5 * courant_column * (east - west)
        - 0.5 * courant_row * (south - north)
        + diffusion * (north + south + east + west - 4.0 * centre)
    )


def measured_kalman_gain(prior, values, variance, noise):
    members = prior.shape[0]
    anomaly = prior - jnp.mean(prior, axis=0)
    spread = jnp.dot(anomaly.T, anomaly, precision=HIGH, preferred_element_type=jnp.float32) / (
        members - 1
    )
    system = spread + jnp.diag(variance)
    factor = jnp.linalg.cholesky(system)
    innovation = values[:, None] + jnp.sqrt(variance)[:, None] * noise - prior.T
    weights = jax.scipy.linalg.cho_solve((factor, True), innovation)
    return (anomaly, weights)


def increment(columns, anomaly, weights, taper):
    members = columns.shape[0]
    centred = columns - jnp.mean(columns, axis=0)
    cross = lax.dot_general(
        centred,
        anomaly,
        (((0,), (0,)), ((), ())),
        precision=HIGH,
        preferred_element_type=jnp.float32,
    ) / (members - 1)
    return columns + lax.dot_general(
        weights,
        taper * cross,
        (((0,), (1,)), ((), ())),
        precision=HIGH,
        preferred_element_type=jnp.float32,
    )


def on_slabs(
    prior_tracer_draws,
    courant_row,
    courant_column,
    diffusion,
    obs_value,
    observation_variance,
    obs_noise,
    obs_owner,
    obs_cell,
    obs_order,
):
    region_rows = prior_tracer_draws.shape[1]
    columns = prior_tracer_draws.shape[2]
    mem_count = lax.axis_size("mem")
    reg_count = lax.axis_size("reg")
    slab_rows = region_rows // mem_count
    grid_rows = region_rows * reg_count
    latitude_weighting = region_rows // 2
    col_scale = columns // 4
    rate_row = courant_row.astype(jnp.float32)
    column_rate = courant_column.astype(jnp.float32)
    rate_diff = diffusion.astype(jnp.float32)
    field = prior_tracer_draws[0]
    for step in range(2):
        haloed_extended_grid = extended(field, (("reg", 0),), 1)
        field = advance_rows(haloed_extended_grid, rate_row, column_rate, rate_diff)
    slabs = lax.all_to_all(field[None], "mem", split_axis=1, concat_axis=0, tiled=True)
    members = slabs.shape[0]
    cells = slabs.reshape(members, slab_rows * columns)
    me_mem = lax.axis_index("mem")
    me_reg = lax.axis_index("reg")
    myself = me_mem * reg_count + me_reg
    owned_rows = me_reg * region_rows + me_mem * slab_rows + jnp.arange(slab_rows, dtype=jnp.int32)
    obs_row = (
        obs_owner % reg_count * region_rows
        + obs_owner // reg_count * slab_rows
        + obs_cell // columns
    )
    observation_column = obs_cell % columns
    col_index = jnp.arange(columns, dtype=jnp.int32)
    owners = obs_owner[obs_order]
    spots = obs_cell[obs_order]
    sorted_row = obs_row[obs_order]
    sorted_col = observation_column[obs_order]
    local = jnp.where((owners == myself)[None, :], cells[:, spots], 0.0)
    priors = lax.psum(local, ("mem", "reg"))
    for block in range(NBLK):
        lower = block * NOB
        upper = (block + 1) * NOB
        chosen = obs_order[lower:upper]
        prior = priors[:, lower:upper]
        anomaly, weights = measured_kalman_gain(
            prior, obs_value[chosen], observation_variance[chosen], obs_noise[chosen]
        )
        orow = sorted_row[lower:upper]
        ocol = sorted_col[lower:upper]
        row_taper = bell(owned_rows[:, None] - orow[None, :], grid_rows, latitude_weighting)
        col_taper = bell(col_index[:, None] - ocol[None, :], columns, col_scale)
        cells = increment(
            cells,
            anomaly,
            weights,
            (row_taper[:, None, :] * col_taper[None, :, :]).reshape(
                slab_rows * columns, orow.shape[0]
            ),
        )
        obs_taper = bell(sorted_row[:, None] - orow[None, :], grid_rows, latitude_weighting) * bell(
            sorted_col[:, None] - ocol[None, :], columns, col_scale
        )
        priors = increment(priors, anomaly, weights, obs_taper)
    return lax.all_to_all(
        cells.reshape(members, slab_rows, columns), "mem", split_axis=0, concat_axis=1, tiled=True
    )


SUBLANES = 8
LANES = 128
POINTS = [(dr, dc) for dr in range(-2, 3) for dc in range(-2, 3) if abs(dr) + abs(dc) <= 2]
CROSS = [(0, 0), (-1, 0), (1, 0), (0, -1), (0, 1)]
TILES = -(-(len(POINTS) + 3 * len(CROSS)) // SUBLANES)
CHUNK = 4 * LANES
CODE_STEP = 2.0**-20
CODE_TOP = 32767.0
SEEN_UNIT = 2.0**-11
SEEN_REST = 2.0**-15
VMEM_GRANT = 8 << 20


def iota(axis, shape=(SUBLANES, LANES)):
    return lax.broadcasted_iota(jnp.int32, shape, axis)


def row_of(x, i):
    return jnp.broadcast_to(x[i : i + 1, :], x.shape)


def stencil(q, north, south, rate_row, rate_col, rate_diff):
    columns = q.shape[1]
    west = pltpu.roll(q, 1, axis=1)
    east = pltpu.roll(q, columns - 1, axis=1)
    return (
        q
        - 0.5 * rate_col * (east - west)
        - 0.5 * rate_row * (south - north)
        + rate_diff * (north + south + east + west - 4.0 * q)
    )


def slot(c):
    return c % SUBLANES, c // SUBLANES * LANES


def start_kernel(
    sizes,
    q_hbm,
    row_hbm,
    col_hbm,
    diff_hbm,
    owner_hbm,
    cell_hbm,
    order_hbm,
    value_hbm,
    variance_hbm,
    noise_hbm,
    down_ref,
    up_ref,
    points_ref,
    partial_ref,
    sorted_ref,
    noise_out,
    row_ref,
    col_ref,
    diff_ref,
    q_ref,
    owner_ref,
    cell_ref,
    order_ref,
    value_ref,
    variance_ref,
    noise_ref,
    arrived,
):
    fetched = (
        (owner_hbm, owner_ref),
        (cell_hbm, cell_ref),
        (order_hbm, order_ref),
        (value_hbm, value_ref),
        (variance_hbm, variance_ref),
        (noise_hbm, noise_ref),
        (q_hbm, q_ref),
        (row_hbm, row_ref),
        (col_hbm, col_ref),
        (diff_hbm, diff_ref),
    )
    copies = [
        pltpu.make_async_copy(source, target, arrived.at[n])
        for n, (source, target) in enumerate(fetched)
    ]
    for copy in copies:
        copy.start()
    for copy in copies[:6]:
        copy.wait()
    reg_count, region_rows, slab_rows, columns = sizes
    grid_rows = reg_count * region_rows
    packed = columns // SUBLANES
    me = lax.axis_index("reg")
    sub = iota(0)
    owner = owner_ref[...]
    cell = cell_ref[...]
    shift = columns.bit_length() - 1
    obs_row = (
        (owner & (reg_count - 1)) * region_rows
        + (owner >> (reg_count.bit_length() - 1)) * slab_rows
        + (cell >> shift)
    )
    obs_col = cell & (columns - 1)
    table = jnp.where(
        sub == 0,
        obs_row.astype(jnp.float32),
        jnp.where(
            sub == 1,
            obs_col.astype(jnp.float32),
            jnp.where(sub == 2, value_ref[...], jnp.where(sub == 3, variance_ref[...], 0.0)),
        ),
    )
    square = (LANES, LANES)
    pick = (iota(0, square) == order_ref[...]).astype(jnp.float32)
    both = jnp.dot(
        jnp.concatenate([table, noise_ref[...]], axis=0),
        pick,
        precision=HIGH,
        preferred_element_type=jnp.float32,
    )
    table = both[:SUBLANES]
    sorted_ref[...] = table
    noise_out[...] = both[SUBLANES:]
    orow = row_of(table, 0).astype(jnp.int32)
    ocol = row_of(table, 1).astype(jnp.int32)

    for copy in copies[6:]:
        copy.wait()
    q = q_ref[0]
    rates = [r[...].astype(jnp.float32) for r in (row_ref, col_ref, diff_ref)]
    local_row = orow - me * region_rows
    for dc in range(-2, 3):
        index = (ocol + dc) & (columns - 1)
        lane = index & (LANES - 1)
        tile = index >> (LANES.bit_length() - 1)
        wanted = [(q, 0, POINTS)]
        if abs(dc) <= 1:
            for n, rate in enumerate(rates):
                wanted.append((rate, len(POINTS) + n * len(CROSS), CROSS))
        hits = [tile == t for t in range(columns // LANES)]
        for array, base, points in wanted:
            found = jnp.zeros((SUBLANES, LANES), jnp.float32)
            for t in range(columns // LANES):
                taken = jnp.take_along_axis(
                    array[:, t * LANES : (t + 1) * LANES], lane, axis=1, mode="promise_in_bounds"
                )
                found = jnp.where(hits[t], taken, found)
            for n, (dr, shift_col) in enumerate(points):
                if shift_col != dc:
                    continue
                here = ((local_row + dr) & (grid_rows - 1)) == sub
                s, at = slot(base + n)
                points_ref[s : s + 1, at : at + LANES] = jnp.sum(
                    jnp.where(here, found, 0.0), axis=0, keepdims=True
                )
    for c in range(len(POINTS) + 3 * len(CROSS), TILES * SUBLANES):
        s, at = slot(c)
        points_ref[s : s + 1, at : at + LANES] = jnp.zeros((1, LANES), jnp.float32)

    rate_row, rate_col, rate_diff = rates
    wide = iota(0, (SUBLANES, columns))
    north = jnp.where(wide == 0, 0.0, pltpu.roll(q, 1, axis=0))
    south = jnp.where(wide == SUBLANES - 1, 0.0, pltpu.roll(q, SUBLANES - 1, axis=0))
    partial = stencil(q, north, south, rate_row, rate_col, rate_diff)
    partial_ref[...] = partial
    for ref, edge, missing in (
        (down_ref, SUBLANES - 1, rate_diff - 0.5 * rate_row),
        (up_ref, 0, rate_diff + 0.5 * rate_row),
    ):
        for n, array in enumerate((q, partial, missing)):
            for s in range(SUBLANES):
                ref[s : s + 1, n * packed : (n + 1) * packed] = array[
                    edge : edge + 1, s * packed : (s + 1) * packed
                ]
        ref[:, 3 * packed :] = points_ref[...]


def bell_of(dist, period, scale):
    dist = jnp.abs(dist)
    dist = jnp.minimum(dist, period - dist) / scale
    return jnp.exp(-0.5 * (dist * dist))


def halves(x):
    high = x.astype(jnp.bfloat16)
    return high, (x - high.astype(jnp.float32)).astype(jnp.bfloat16)


def taper_kernel(sizes, sorted_ref, columns_ref, obs_ref, rows_ref):
    reg_count, region_rows, slab_rows, columns = sizes
    grid_rows = reg_count * region_rows
    row_scale, col_scale = float(region_rows // 2), float(columns // 4)
    me = lax.axis_index("reg")
    square = (LANES, LANES)
    row_lanes = jnp.broadcast_to(sorted_ref[0:1, :], square)
    col_lanes = jnp.broadcast_to(sorted_ref[1:2, :], square)
    row_subs = row_lanes.T
    col_subs = col_lanes.T
    for t in range(columns // LANES):
        at = (t * LANES + iota(1, square)).astype(jnp.float32)
        high, low = halves(bell_of(at - col_subs, float(columns), col_scale))
        columns_ref[0, :, t * LANES : (t + 1) * LANES] = high
        columns_ref[1, :, t * LANES : (t + 1) * LANES] = low
    high, low = halves(
        bell_of(row_lanes - row_subs, float(grid_rows), row_scale)
        * bell_of(col_lanes - col_subs, float(columns), col_scale)
    )
    obs_ref[0] = high
    obs_ref[1] = low
    rows = (me * region_rows + iota(0)).astype(jnp.float32)
    rows_ref[...] = bell_of(rows - row_lanes[:SUBLANES], float(grid_rows), row_scale)


def middle_kernel(
    sizes,
    partial_ref,
    row_ref,
    col_ref,
    diff_ref,
    down_ref,
    up_ref,
    points_ref,
    above_ref,
    below_ref,
    far_ref,
    field_ref,
    out_ref,
    edge_ref,
):
    reg_count, region_rows, slab_rows, columns = sizes
    packed = columns // SUBLANES
    wide = iota(0, (SUBLANES, columns))
    rate_row, rate_col, rate_diff = [
        r[...].astype(jnp.float32) for r in (row_ref, col_ref, diff_ref)
    ]

    def section(ref, n):
        return ref[:, n * packed : (n + 1) * packed]

    outer = (
        section(above_ref, 0),
        section(below_ref, 0),
        section(above_ref, 1) + section(above_ref, 2) * section(up_ref, 0),
        section(below_ref, 1) + section(below_ref, 2) * section(down_ref, 0),
    )
    for n, array in enumerate(outer):
        for s in range(SUBLANES):
            edge_ref[n : n + 1, s * packed : (s + 1) * packed] = array[s : s + 1, :]

    def edge(n):
        return jnp.broadcast_to(edge_ref[n : n + 1, :], (SUBLANES, columns))

    first, last = wide == 0, wide == SUBLANES - 1
    field = (
        partial_ref[...]
        + jnp.where(first, (rate_diff + 0.5 * rate_row) * edge(0), 0.0)
        + jnp.where(last, (rate_diff - 0.5 * rate_row) * edge(1), 0.0)
    )
    north = jnp.where(first, edge(2), pltpu.roll(field, 1, axis=0))
    south = jnp.where(last, edge(3), pltpu.roll(field, SUBLANES - 1, axis=0))
    field = stencil(field, north, south, rate_row, rate_col, rate_diff)

    points = points_ref[...] + far_ref[...] + above_ref[:, 3 * packed :] + below_ref[:, 3 * packed :]

    def point(c):
        s, at = slot(c)
        return points[s : s + 1, at : at + LANES]

    q0 = {p: point(n) for n, p in enumerate(POINTS)}
    rates = [
        {p: point(len(POINTS) + n * len(CROSS) + i) for i, p in enumerate(CROSS)} for n in range(3)
    ]

    def at_point(values, p):
        i, j = p
        here = values[p]
        north, south = values[i - 1, j], values[i + 1, j]
        west, east = values[i, j - 1], values[i, j + 1]
        return (
            here
            - 0.5 * rates[1][p] * (east - west)
            - 0.5 * rates[0][p] * (south - north)
            + rates[2][p] * (north + south + east + west - 4.0 * here)
        )

    q1 = {p: at_point(q0, p) for p in CROSS}
    seen = jnp.broadcast_to(at_point(q1, (0, 0)), (SUBLANES, LANES)) / SEEN_UNIT
    whole = jnp.round(seen)
    rest = jnp.round((seen - whole) / SEEN_REST)
    field_ref[...] = field
    peak = jnp.max(jnp.max(jnp.abs(field), axis=1, keepdims=True), axis=0, keepdims=True)
    steps = jnp.maximum(jnp.ceil(peak * (1.0 / (CODE_TOP * CODE_STEP))), 1.0)
    code = jnp.round(field * (1.0 / (steps * CODE_STEP)))
    sub = iota(0)
    tail = jnp.where(
        sub == 0, whole, jnp.where(sub == 1, rest, jnp.broadcast_to(steps, (SUBLANES, LANES)))
    )
    message = jnp.concatenate([code, tail], axis=1).astype(jnp.int32).astype(jnp.int16)
    for d in range(out_ref.shape[0]):
        out_ref[d] = message


def gain(anomaly, precision, innovation):
    members = anomaly.shape[0]
    sub = iota(0)
    weighted = anomaly * precision

    def against(x):
        total = jnp.sum(weighted * x, axis=1, keepdims=True)
        return jnp.broadcast_to(total, weighted.shape)

    system = [
        against(row_of(anomaly, b)) + jnp.where(sub == b, float(members - 1), 0.0)
        for b in range(members)
    ]
    load = [against(row_of(innovation, m)) for m in range(members)]
    held = anomaly
    for k in range(members):
        inverse = 1.0 / row_of(system[k], k)
        mine = sub == k

        def step(x, k=k, inverse=inverse, mine=mine):
            scaled = row_of(x, k) * inverse
            return jnp.where(mine, scaled, x - system[k] * scaled)

        held = step(held)
        for b in range(k + 1, members):
            system[b] = step(system[b])
    fitted = jnp.zeros_like(anomaly)
    for m in range(members):
        total = jnp.sum(load[m] * held, axis=0, keepdims=True)
        fitted = jnp.where(sub == m, jnp.broadcast_to(total, held.shape), fitted)
    return precision * (innovation - fitted)


def twice(x, block):
    lane = iota(1)
    half = LANES // 2
    return jnp.where(lane // half == block, x, pltpu.roll(x, half, axis=1))


def split(rows):
    half = LANES // 2
    high = rows.astype(jnp.bfloat16).astype(jnp.float32)
    left = jnp.where(iota(1, rows.shape) < half, high, rows - high).astype(jnp.bfloat16)
    return jnp.concatenate([left, left], axis=1)


def stacked(table_ref, block, part=slice(None)):
    half = LANES // 2
    high = table_ref[0, block * half : (block + 1) * half, part]
    low = table_ref[1, block * half : (block + 1) * half, part]
    return jnp.concatenate([high, high, low, low], axis=0)


def finish_kernel(
    sizes,
    x_ref,
    field_ref,
    sorted_ref,
    noise_ref,
    columns_ref,
    obs_ref,
    rows_ref,
    out_ref,
    now_ref,
):
    columns = sizes[-1]
    members = x_ref.shape[0]
    me = lax.axis_index("mem")
    sub, lane = iota(0), iota(1)
    half = LANES // 2
    seen = jnp.zeros((SUBLANES, LANES), jnp.float32)
    steps = []
    for m in range(members):
        tail = x_ref[m, :, columns:].astype(jnp.float32)
        value = (row_of(tail, 0) + row_of(tail, 1) * SEEN_REST) * SEEN_UNIT
        seen = jnp.where(sub == m, value, seen)
        steps.append(row_of(tail, 2) * CODE_STEP)
    value, variance = row_of(sorted_ref, 2), row_of(sorted_ref, 3)
    observed = value + jnp.sqrt(variance) * noise_ref[...]
    inverse_variance = 1.0 / variance
    scale = 1.0 / (members - 1)
    lefts = []
    for block in range(NBLK):
        last = block + 1 == NBLK
        anomaly = seen - jnp.sum(seen, axis=0, keepdims=True) * (1.0 / members)
        precision = jnp.where(lane // half == block, inverse_variance, 0.0)
        gains = gain(anomaly, precision, observed - seen) * scale
        gains, local = twice(gains, block), twice(anomaly, block)
        pairs = [row_of(local, a) * gains for a in range(members)]
        row_taper = twice(rows_ref[...], block)
        if last:
            own = [
                jnp.sum(jnp.where(sub == me, pair, 0.0), axis=0, keepdims=True) for pair in pairs
            ]
            lefts.append([row_taper * x for x in own])
        else:
            moved = jnp.dot(
                split(jnp.concatenate(pairs, axis=0)),
                stacked(obs_ref, block),
                preferred_element_type=jnp.float32,
            )
            for a in range(members):
                seen = seen + row_of(anomaly, a) * moved[a * SUBLANES : (a + 1) * SUBLANES]
            lefts.append([row_taper * row_of(pair, m) for pair in pairs for m in range(members)])
    lefts = [split(jnp.concatenate(x, axis=0)) for x in lefts]

    def added(starts, centred, weights):
        updated = []
        for n, total in enumerate(starts):
            for a in range(members):
                at = (a * len(starts) + n) * SUBLANES
                total = total + centred[a] * weights[at : at + SUBLANES]
            updated.append(total)
        return updated

    def centre(fields):
        mean = sum(fields[1:], fields[0]) * (1.0 / members)
        return [x - mean for x in fields]

    for begin in range(0, columns, CHUNK):
        part = slice(begin, begin + CHUNK)

        def decoded(m, part=part):
            return x_ref[m, :, part].astype(jnp.float32)

        current = [decoded(m) * steps[m][:, :1] for m in range(members)]
        for m in range(members):
            now_ref[m] = current[m]
        sent = now_ref[me]
        for block in range(NBLK):
            weights = jnp.dot(
                lefts[block],
                stacked(columns_ref, block, part),
                preferred_element_type=jnp.float32,
            )
            if block + 1 < NBLK:
                current = added(current, centre(current), weights)
                for m in range(members):
                    now_ref[m] = current[m]
            else:
                own = now_ref[me] + (field_ref[:, part] - sent)
                (own,) = added([own], centre(current), weights)
                out_ref[0, :, part] = own


def call(kernel, outs, args, scratch=(), cost=None, space=pltpu.VMEM):
    held = pl.BlockSpec(memory_space=pltpu.VMEM)
    return pl.pallas_call(
        kernel,
        out_shape=[jax.ShapeDtypeStruct(s, d) for s, d in outs],
        in_specs=[pl.BlockSpec(memory_space=space)] * len(args),
        out_specs=[held] * len(outs),
        scratch_shapes=list(scratch),
        cost_estimate=cost,
        compiler_params=pltpu.CompilerParams(vmem_limit_bytes=VMEM_GRANT),
    )(*args)


def on_tile(
    prior_tracer_draws,
    courant_row,
    courant_column,
    diffusion,
    obs_value,
    observation_variance,
    obs_noise,
    obs_owner,
    obs_cell,
    obs_order,
):
    f32 = jnp.float32
    region_rows, columns = prior_tracer_draws.shape[1:]
    members = obs_noise.shape[1]
    mem_count, reg_count = lax.axis_size("mem"), lax.axis_size("reg")
    sizes = (reg_count, region_rows, region_rows // mem_count, columns)
    packed = columns // SUBLANES
    tile = (SUBLANES, LANES)
    field = (SUBLANES, columns)
    points_shape = (SUBLANES, TILES * LANES)
    message = (SUBLANES, 3 * packed + TILES * LANES)
    rates = (courant_row, courant_column, diffusion)
    flat = [x.reshape(1, LANES) for x in (obs_owner, obs_cell, obs_order, obs_value, observation_variance)]
    operands = (prior_tracer_draws, *rates, *flat, obs_noise.T)
    down, up, points, partial, table, noise, *rates = call(
        functools.partial(start_kernel, sizes),
        [(message, f32), (message, f32), (points_shape, f32), (field, f32), (tile, f32), (tile, f32)]
        + [(x.shape, x.dtype) for x in rates],
        [pltpu.with_memory_space_constraint(x, pltpu.HBM) for x in operands],
        scratch=[pltpu.VMEM(prior_tracer_draws.shape, f32)]
        + [pltpu.VMEM(x.shape, x.dtype) for x in operands[4:]]
        + [pltpu.SemaphoreType.DMA((len(operands),))],
        space=pltpu.HBM,
    )

    def shifted(x, by):
        return lax.ppermute(x, "reg", [(i, (i + by) % reg_count) for i in range(reg_count)])

    above = shifted(down, 1)
    below = shifted(up, -1)
    far = [shifted(points, by) for by in range(2, reg_count - 1)]
    col_taper, obs_taper, row_taper = call(
        functools.partial(taper_kernel, sizes),
        [((2, LANES, columns), jnp.bfloat16), ((2, LANES, LANES), jnp.bfloat16), (tile, f32)],
        (table,),
        cost=pl.CostEstimate(flops=10 * LANES * columns, bytes_accessed=8 * LANES * columns, transcendentals=LANES * columns),
    )
    forecast, send = call(
        functools.partial(middle_kernel, sizes),
        [(field, f32), ((mem_count, SUBLANES, columns + LANES), jnp.int16)],
        (partial, *rates, down, up, points, above, below, sum(far[1:], far[0])),
        scratch=[pltpu.VMEM(field, f32)],
    )
    slabs = lax.all_to_all(send, "mem", split_axis=0, concat_axis=0, tiled=True)
    (out,) = call(
        functools.partial(finish_kernel, sizes),
        [(prior_tracer_draws.shape, f32)],
        (slabs, forecast, table, noise, col_taper, obs_taper, row_taper),
        scratch=[pltpu.VMEM((members, SUBLANES, CHUNK), f32)],
    )
    return out


def fits_tile(*shapes):
    draws, noise = shapes
    members, region_rows, columns = draws
    counts = (lax.axis_size("mem"), lax.axis_size("reg"))
    return (
        members == 1
        and noise[1] == counts[0] == region_rows == SUBLANES
        and noise[0] == NOB * NBLK == LANES
        and counts[1] >= 4
        and counts[1] & (counts[1] - 1) == 0
        and columns % CHUNK == 0
        and columns & (columns - 1) == 0
    )


def on_device(*args):
    return (on_tile if fits_tile(args[0].shape, args[6].shape) else on_slabs)(*args)


def solution(mesh):
    placed = (
        P("mem", "reg", None),
        P("reg", None),
        P("reg", None),
        P("reg", None),
        P(),
        P(),
        P(),
        P(),
        P(),
        P(),
    )
    return jax.shard_map(
        on_device, mesh=mesh, in_specs=placed, out_specs=P("mem", "reg", None), check_vma=False
    )
```

```python
import functools

import jax
import jax.numpy as jnp
from jax import lax
from jax.experimental import pallas as pl
from jax.experimental.pallas import tpu as pltpu
from jax.sharding import PartitionSpec as P

NOB = 64
NBLK = 2


HIGH = lax.Precision.HIGHEST


def extended(cells, sides, width):
    for axis, dim in sides:
        count = lax.axis_size(axis)
        head = lax.slice_in_dim(cells, 0, width, axis=dim)
        tail = lax.slice_in_dim(cells, cells.shape[dim] - width, cells.shape[dim], axis=dim)
        cells = jnp.concatenate(
            [
                lax.ppermute(tail, axis, [(i, (i + 1) % count) for i in range(count)]),
                cells,
                lax.ppermute(head, axis, [((i + 1) % count, i) for i in range(count)]),
            ],
            axis=dim,
        )
    return cells


def bell(delta, period, scale):
    delta = delta % period
    dist = jnp.minimum(delta, period - delta).astype(jnp.float32)
    return jnp.exp(-0.5 * (dist / scale) ** 2)


def advance_rows(haloed_extended_grid, courant_row, courant_column, diffusion):
    centre = haloed_extended_grid[1:-1]
    north = haloed_extended_grid[:-2]
    south = haloed_extended_grid[2:]
    west = jnp.roll(centre, 1, axis=1)
    east = jnp.roll(centre, -1, axis=1)
    return (
        centre
        - 0.5 * courant_column * (east - west)
        - 0.5 * courant_row * (south - north)
        + diffusion * (north + south + east + west - 4.0 * centre)
    )


def measured_kalman_gain(prior, values, variance, noise):
    members = prior.shape[0]
    anomaly = prior - jnp.mean(prior, axis=0)
    spread = jnp.dot(anomaly.T, anomaly, precision=HIGH, preferred_element_type=jnp.float32) / (
        members - 1
    )
    system = spread + jnp.diag(variance)
    factor = jnp.linalg.cholesky(system)
    innovation = values[:, None] + jnp.sqrt(variance)[:, None] * noise - prior.T
    weights = jax.scipy.linalg.cho_solve((factor, True), innovation)
    return (anomaly, weights)


def increment(columns, anomaly, weights, taper):
    members = columns.shape[0]
    centred = columns - jnp.mean(columns, axis=0)
    cross = lax.dot_general(
        centred,
        anomaly,
        (((0,), (0,)), ((), ())),
        precision=HIGH,
        preferred_element_type=jnp.float32,
    ) / (members - 1)
    return columns + lax.dot_general(
        weights,
        taper * cross,
        (((0,), (1,)), ((), ())),
        precision=HIGH,
        preferred_element_type=jnp.float32,
    )


def on_slabs(
    prior_tracer_draws,
    courant_row,
    courant_column,
    diffusion,
    obs_value,
    observation_variance,
    obs_noise,
    obs_owner,
    obs_cell,
    obs_order,
):
    region_rows = prior_tracer_draws.shape[1]
    columns = prior_tracer_draws.shape[2]
    mem_count = lax.axis_size("mem")
    reg_count = lax.axis_size("reg")
    slab_rows = region_rows // mem_count
    grid_rows = region_rows * reg_count
    latitude_weighting = region_rows // 2
    col_scale = columns // 4
    rate_row = courant_row.astype(jnp.float32)
    column_rate = courant_column.astype(jnp.float32)
    rate_diff = diffusion.astype(jnp.float32)
    field = prior_tracer_draws[0]
    for step in range(2):
        haloed_extended_grid = extended(field, (("reg", 0),), 1)
        field = advance_rows(haloed_extended_grid, rate_row, column_rate, rate_diff)
    slabs = lax.all_to_all(field[None], "mem", split_axis=1, concat_axis=0, tiled=True)
    members = slabs.shape[0]
    cells = slabs.reshape(members, slab_rows * columns)
    me_mem = lax.axis_index("mem")
    me_reg = lax.axis_index("reg")
    myself = me_mem * reg_count + me_reg
    owned_rows = me_reg * region_rows + me_mem * slab_rows + jnp.arange(slab_rows, dtype=jnp.int32)
    obs_row = (
        obs_owner % reg_count * region_rows
        + obs_owner // reg_count * slab_rows
        + obs_cell // columns
    )
    observation_column = obs_cell % columns
    col_index = jnp.arange(columns, dtype=jnp.int32)
    owners = obs_owner[obs_order]
    spots = obs_cell[obs_order]
    sorted_row = obs_row[obs_order]
    sorted_col = observation_column[obs_order]
    local = jnp.where((owners == myself)[None, :], cells[:, spots], 0.0)
    priors = lax.psum(local, ("mem", "reg"))
    for block in range(NBLK):
        lower = block * NOB
        upper = (block + 1) * NOB
        chosen = obs_order[lower:upper]
        prior = priors[:, lower:upper]
        anomaly, weights = measured_kalman_gain(
            prior, obs_value[chosen], observation_variance[chosen], obs_noise[chosen]
        )
        orow = sorted_row[lower:upper]
        ocol = sorted_col[lower:upper]
        row_taper = bell(owned_rows[:, None] - orow[None, :], grid_rows, latitude_weighting)
        col_taper = bell(col_index[:, None] - ocol[None, :], columns, col_scale)
        cells = increment(
            cells,
            anomaly,
            weights,
            (row_taper[:, None, :] * col_taper[None, :, :]).reshape(
                slab_rows * columns, orow.shape[0]
            ),
        )
        obs_taper = bell(sorted_row[:, None] - orow[None, :], grid_rows, latitude_weighting) * bell(
            sorted_col[:, None] - ocol[None, :], columns, col_scale
        )
        priors = increment(priors, anomaly, weights, obs_taper)
    return lax.all_to_all(
        cells.reshape(members, slab_rows, columns), "mem", split_axis=0, concat_axis=1, tiled=True
    )


SUBLANES = 8
LANES = 128
POINTS = [(dr, dc) for dr in range(-2, 3) for dc in range(-2, 3) if abs(dr) + abs(dc) <= 2]
CROSS = [(0, 0), (-1, 0), (1, 0), (0, -1), (0, 1)]
TILES = -(-(len(POINTS) + 3 * len(CROSS)) // SUBLANES)
CHUNK = 4 * LANES
CODE_STEP = 2.0**-20
CODE_TOP = 32767.0
SEEN_UNIT = 2.0**-11
SEEN_REST = 2.0**-15
VMEM_GRANT = 8 << 20


def iota(axis, shape=(SUBLANES, LANES)):
    return lax.broadcasted_iota(jnp.int32, shape, axis)


def row_of(x, i):
    return jnp.broadcast_to(x[i : i + 1, :], x.shape)


def stencil(q, north, south, rate_row, rate_col, rate_diff):
    columns = q.shape[1]
    west = pltpu.roll(q, 1, axis=1)
    east = pltpu.roll(q, columns - 1, axis=1)
    return (
        q
        - 0.5 * rate_col * (east - west)
        - 0.5 * rate_row * (south - north)
        + rate_diff * (north + south + east + west - 4.0 * q)
    )


def slot(c):
    return c % SUBLANES, c // SUBLANES * LANES


def start_kernel(
    sizes,
    q_hbm,
    row_hbm,
    col_hbm,
    diff_hbm,
    owner_hbm,
    cell_hbm,
    order_hbm,
    value_hbm,
    variance_hbm,
    noise_hbm,
    pair_ref,
    cross_ref,
    points_ref,
    partial_ref,
    sorted_ref,
    noise_out,
    row_ref,
    col_ref,
    diff_ref,
    q_ref,
    owner_ref,
    cell_ref,
    order_ref,
    value_ref,
    variance_ref,
    noise_ref,
    arrived,
):
    fetched = (
        (owner_hbm, owner_ref),
        (cell_hbm, cell_ref),
        (order_hbm, order_ref),
        (value_hbm, value_ref),
        (variance_hbm, variance_ref),
        (noise_hbm, noise_ref),
        (q_hbm, q_ref),
        (row_hbm, row_ref),
        (col_hbm, col_ref),
        (diff_hbm, diff_ref),
    )
    copies = [
        pltpu.make_async_copy(source, target, arrived.at[n])
        for n, (source, target) in enumerate(fetched)
    ]
    for copy in copies:
        copy.start()
    for copy in copies[:6]:
        copy.wait()
    reg_count, region_rows, slab_rows, columns = sizes
    grid_rows = reg_count * region_rows
    packed = columns // SUBLANES
    me = lax.axis_index("reg")
    sub = iota(0)
    owner = owner_ref[...]
    cell = cell_ref[...]
    shift = columns.bit_length() - 1
    obs_row = (
        (owner & (reg_count - 1)) * region_rows
        + (owner >> (reg_count.bit_length() - 1)) * slab_rows
        + (cell >> shift)
    )
    obs_col = cell & (columns - 1)
    table = jnp.where(
        sub == 0,
        obs_row.astype(jnp.float32),
        jnp.where(
            sub == 1,
            obs_col.astype(jnp.float32),
            jnp.where(sub == 2, value_ref[...], jnp.where(sub == 3, variance_ref[...], 0.0)),
        ),
    )
    square = (LANES, LANES)
    pick = (iota(0, square) == order_ref[...]).astype(jnp.float32)
    both = jnp.dot(
        jnp.concatenate([table, noise_ref[...]], axis=0),
        pick,
        precision=HIGH,
        preferred_element_type=jnp.float32,
    )
    table = both[:SUBLANES]
    sorted_ref[...] = table
    noise_out[...] = both[SUBLANES:]
    orow = row_of(table, 0).astype(jnp.int32)
    ocol = row_of(table, 1).astype(jnp.int32)

    for copy in copies[6:]:
        copy.wait()
    q = q_ref[0]
    rates = [r[...].astype(jnp.float32) for r in (row_ref, col_ref, diff_ref)]
    local_row = orow - me * region_rows
    for dc in range(-2, 3):
        index = (ocol + dc) & (columns - 1)
        lane = index & (LANES - 1)
        tile = index >> (LANES.bit_length() - 1)
        wanted = [(q, 0, POINTS)]
        if abs(dc) <= 1:
            for n, rate in enumerate(rates):
                wanted.append((rate, len(POINTS) + n * len(CROSS), CROSS))
        hits = [tile == t for t in range(columns // LANES)]
        for array, base, points in wanted:
            found = jnp.zeros((SUBLANES, LANES), jnp.float32)
            for t in range(columns // LANES):
                taken = jnp.take_along_axis(
                    array[:, t * LANES : (t + 1) * LANES], lane, axis=1, mode="promise_in_bounds"
                )
                found = jnp.where(hits[t], taken, found)
            for n, (dr, shift_col) in enumerate(points):
                if shift_col != dc:
                    continue
                here = ((local_row + dr) & (grid_rows - 1)) == sub
                s, at = slot(base + n)
                points_ref[s : s + 1, at : at + LANES] = jnp.sum(
                    jnp.where(here, found, 0.0), axis=0, keepdims=True
                )
    for c in range(len(POINTS) + 3 * len(CROSS), TILES * SUBLANES):
        s, at = slot(c)
        points_ref[s : s + 1, at : at + LANES] = jnp.zeros((1, LANES), jnp.float32)

    rate_row, rate_col, rate_diff = rates
    wide = iota(0, (SUBLANES, columns))
    north = jnp.where(wide == 0, 0.0, pltpu.roll(q, 1, axis=0))
    south = jnp.where(wide == SUBLANES - 1, 0.0, pltpu.roll(q, SUBLANES - 1, axis=0))
    partial = stencil(q, north, south, rate_row, rate_col, rate_diff)
    partial_ref[...] = partial
    even = (me & 1) == 0
    edges = [
        (array[SUBLANES - 1 :, :], array[:1, :])
        for array in (q, partial)
    ] + [((rate_diff - 0.5 * rate_row)[SUBLANES - 1 :, :], (rate_diff + 0.5 * rate_row)[:1, :])]
    for n, (lower, upper) in enumerate(edges):
        for ref, row in (
            (pair_ref, jnp.where(even, lower, upper)),
            (cross_ref, jnp.where(even, upper, lower)),
        ):
            for s in range(SUBLANES):
                ref[s : s + 1, n * packed : (n + 1) * packed] = row[
                    :, s * packed : (s + 1) * packed
                ]
    pair_ref[:, 3 * packed :] = points_ref[...]
    cross_ref[:, 3 * packed :] = points_ref[...]


def bell_of(dist, period, scale):
    dist = jnp.abs(dist)
    dist = jnp.minimum(dist, period - dist) / scale
    return jnp.exp(-0.5 * (dist * dist))


def halves(x):
    high = x.astype(jnp.bfloat16)
    return high, (x - high.astype(jnp.float32)).astype(jnp.bfloat16)


def taper_kernel(sizes, sorted_ref, columns_ref, obs_ref, rows_ref):
    reg_count, region_rows, slab_rows, columns = sizes
    grid_rows = reg_count * region_rows
    row_scale, col_scale = float(region_rows // 2), float(columns // 4)
    me = lax.axis_index("reg")
    square = (LANES, LANES)
    row_lanes = jnp.broadcast_to(sorted_ref[0:1, :], square)
    col_lanes = jnp.broadcast_to(sorted_ref[1:2, :], square)
    row_subs = row_lanes.T
    col_subs = col_lanes.T
    for t in range(columns // LANES):
        at = (t * LANES + iota(1, square)).astype(jnp.float32)
        high, low = halves(bell_of(at - col_subs, float(columns), col_scale))
        columns_ref[0, :, t * LANES : (t + 1) * LANES] = high
        columns_ref[1, :, t * LANES : (t + 1) * LANES] = low
    high, low = halves(
        bell_of(row_lanes - row_subs, float(grid_rows), row_scale)
        * bell_of(col_lanes - col_subs, float(columns), col_scale)
    )
    obs_ref[0] = high
    obs_ref[1] = low
    rows = (me * region_rows + iota(0)).astype(jnp.float32)
    rows_ref[...] = bell_of(rows - row_lanes[:SUBLANES], float(grid_rows), row_scale)


def middle_kernel(
    sizes,
    partial_ref,
    row_ref,
    col_ref,
    diff_ref,
    pair_ref,
    cross_ref,
    points_ref,
    paired_ref,
    crossed_ref,
    far_ref,
    field_ref,
    out_ref,
    edge_ref,
):
    reg_count, region_rows, slab_rows, columns = sizes
    packed = columns // SUBLANES
    wide = iota(0, (SUBLANES, columns))
    rate_row, rate_col, rate_diff = [
        r[...].astype(jnp.float32) for r in (row_ref, col_ref, diff_ref)
    ]

    def section(ref, n):
        return ref[:, n * packed : (n + 1) * packed]

    def ahead(ref, sent_ref):
        return section(ref, 0), section(ref, 1) + section(ref, 2) * section(sent_ref, 0)

    even = (lax.axis_index("reg") & 1) == 0
    paired, crossed = ahead(paired_ref, pair_ref), ahead(crossed_ref, cross_ref)
    outer = [
        jnp.where(even, one, other)
        for x, y in zip(paired, crossed)
        for one, other in ((y, x), (x, y))
    ]
    for n, array in enumerate(outer):
        for s in range(SUBLANES):
            edge_ref[n : n + 1, s * packed : (s + 1) * packed] = array[s : s + 1, :]

    def edge(n):
        return jnp.broadcast_to(edge_ref[n : n + 1, :], (SUBLANES, columns))

    first, last = wide == 0, wide == SUBLANES - 1
    field = (
        partial_ref[...]
        + jnp.where(first, (rate_diff + 0.5 * rate_row) * edge(0), 0.0)
        + jnp.where(last, (rate_diff - 0.5 * rate_row) * edge(1), 0.0)
    )
    north = jnp.where(first, edge(2), pltpu.roll(field, 1, axis=0))
    south = jnp.where(last, edge(3), pltpu.roll(field, SUBLANES - 1, axis=0))
    field = stencil(field, north, south, rate_row, rate_col, rate_diff)

    points = (
        points_ref[...] + far_ref[...] + paired_ref[:, 3 * packed :] + crossed_ref[:, 3 * packed :]
    )

    def point(c):
        s, at = slot(c)
        return points[s : s + 1, at : at + LANES]

    q0 = {p: point(n) for n, p in enumerate(POINTS)}
    rates = [
        {p: point(len(POINTS) + n * len(CROSS) + i) for i, p in enumerate(CROSS)} for n in range(3)
    ]

    def at_point(values, p):
        i, j = p
        here = values[p]
        north, south = values[i - 1, j], values[i + 1, j]
        west, east = values[i, j - 1], values[i, j + 1]
        return (
            here
            - 0.5 * rates[1][p] * (east - west)
            - 0.5 * rates[0][p] * (south - north)
            + rates[2][p] * (north + south + east + west - 4.0 * here)
        )

    q1 = {p: at_point(q0, p) for p in CROSS}
    seen = jnp.broadcast_to(at_point(q1, (0, 0)), (SUBLANES, LANES)) / SEEN_UNIT
    whole = jnp.round(seen)
    rest = jnp.round((seen - whole) / SEEN_REST)
    field_ref[...] = field
    peak = jnp.max(jnp.max(jnp.abs(field), axis=1, keepdims=True), axis=0, keepdims=True)
    steps = jnp.maximum(jnp.ceil(peak * (1.0 / (CODE_TOP * CODE_STEP))), 1.0)
    code = jnp.round(field * (1.0 / (steps * CODE_STEP)))
    sub = iota(0)
    tail = jnp.where(
        sub == 0, whole, jnp.where(sub == 1, rest, jnp.broadcast_to(steps, (SUBLANES, LANES)))
    )
    message = jnp.concatenate([code, tail], axis=1).astype(jnp.int32).astype(jnp.int16)
    for d in range(out_ref.shape[0]):
        out_ref[d] = message


def gain(anomaly, precision, innovation):
    members = anomaly.shape[0]
    sub = iota(0)
    weighted = anomaly * precision

    def against(x):
        total = jnp.sum(weighted * x, axis=1, keepdims=True)
        return jnp.broadcast_to(total, weighted.shape)

    system = [
        against(row_of(anomaly, b)) + jnp.where(sub == b, float(members - 1), 0.0)
        for b in range(members)
    ]
    load = [against(row_of(innovation, m)) for m in range(members)]
    held = anomaly
    for k in range(members):
        inverse = 1.0 / row_of(system[k], k)
        mine = sub == k

        def step(x, k=k, inverse=inverse, mine=mine):
            scaled = row_of(x, k) * inverse
            return jnp.where(mine, scaled, x - system[k] * scaled)

        held = step(held)
        for b in range(k + 1, members):
            system[b] = step(system[b])
    fitted = jnp.zeros_like(anomaly)
    for m in range(members):
        total = jnp.sum(load[m] * held, axis=0, keepdims=True)
        fitted = jnp.where(sub == m, jnp.broadcast_to(total, held.shape), fitted)
    return precision * (innovation - fitted)


def twice(x, block):
    lane = iota(1)
    half = LANES // 2
    return jnp.where(lane // half == block, x, pltpu.roll(x, half, axis=1))


def split(rows):
    half = LANES // 2
    high = rows.astype(jnp.bfloat16).astype(jnp.float32)
    left = jnp.where(iota(1, rows.shape) < half, high, rows - high).astype(jnp.bfloat16)
    return jnp.concatenate([left, left], axis=1)


def stacked(table_ref, block, part=slice(None)):
    half = LANES // 2
    high = table_ref[0, block * half : (block + 1) * half, part]
    low = table_ref[1, block * half : (block + 1) * half, part]
    return jnp.concatenate([high, high, low, low], axis=0)


def finish_kernel(
    sizes,
    order,
    x_ref,
    field_ref,
    sorted_ref,
    noise_ref,
    columns_ref,
    obs_ref,
    rows_ref,
    out_ref,
    now_ref,
):
    columns = sizes[-1]
    members = x_ref.shape[0]
    me = lax.axis_index("mem")
    sub, lane = iota(0), iota(1)
    half = LANES // 2
    place = [order.index(m) for m in range(members)]
    seen = jnp.zeros((SUBLANES, LANES), jnp.float32)
    steps = []
    for m in range(members):
        tail = x_ref[place[m], :, columns:].astype(jnp.float32)
        value = (row_of(tail, 0) + row_of(tail, 1) * SEEN_REST) * SEEN_UNIT
        seen = jnp.where(sub == m, value, seen)
        steps.append(row_of(tail, 2) * CODE_STEP)
    value, variance = row_of(sorted_ref, 2), row_of(sorted_ref, 3)
    observed = value + jnp.sqrt(variance) * noise_ref[...]
    inverse_variance = 1.0 / variance
    scale = 1.0 / (members - 1)
    lefts = []
    for block in range(NBLK):
        last = block + 1 == NBLK
        anomaly = seen - jnp.sum(seen, axis=0, keepdims=True) * (1.0 / members)
        precision = jnp.where(lane // half == block, inverse_variance, 0.0)
        gains = gain(anomaly, precision, observed - seen) * scale
        gains, local = twice(gains, block), twice(anomaly, block)
        pairs = [row_of(local, a) * gains for a in range(members)]
        row_taper = twice(rows_ref[...], block)
        if last:
            own = [
                jnp.sum(jnp.where(sub == me, pair, 0.0), axis=0, keepdims=True) for pair in pairs
            ]
            lefts.append([row_taper * x for x in own])
        else:
            moved = jnp.dot(
                split(jnp.concatenate(pairs, axis=0)),
                stacked(obs_ref, block),
                preferred_element_type=jnp.float32,
            )
            for a in range(members):
                seen = seen + row_of(anomaly, a) * moved[a * SUBLANES : (a + 1) * SUBLANES]
            lefts.append([row_taper * row_of(pair, m) for pair in pairs for m in range(members)])
    lefts = [split(jnp.concatenate(x, axis=0)) for x in lefts]

    def added(starts, centred, weights):
        updated = []
        for n, total in enumerate(starts):
            for a in range(members):
                at = (a * len(starts) + n) * SUBLANES
                total = total + centred[a] * weights[at : at + SUBLANES]
            updated.append(total)
        return updated

    def centre(fields):
        mean = sum(fields[1:], fields[0]) * (1.0 / members)
        return [x - mean for x in fields]

    for begin in range(0, columns, CHUNK):
        part = slice(begin, begin + CHUNK)

        def decoded(m, part=part):
            return x_ref[place[m], :, part].astype(jnp.float32)

        current = [decoded(m) * steps[m][:, :1] for m in range(members)]
        for m in range(members):
            now_ref[m] = current[m]
        sent = now_ref[me]
        for block in range(NBLK):
            weights = jnp.dot(
                lefts[block],
                stacked(columns_ref, block, part),
                preferred_element_type=jnp.float32,
            )
            if block + 1 < NBLK:
                current = added(current, centre(current), weights)
                for m in range(members):
                    now_ref[m] = current[m]
            else:
                own = now_ref[me] + (field_ref[:, part] - sent)
                (own,) = added([own], centre(current), weights)
                out_ref[0, :, part] = own


def call(kernel, outs, args, scratch=(), cost=None, space=pltpu.VMEM):
    held = pl.BlockSpec(memory_space=pltpu.VMEM)
    return pl.pallas_call(
        kernel,
        out_shape=[jax.ShapeDtypeStruct(s, d) for s, d in outs],
        in_specs=[pl.BlockSpec(memory_space=space)] * len(args),
        out_specs=[held] * len(outs),
        scratch_shapes=list(scratch),
        cost_estimate=cost,
        compiler_params=pltpu.CompilerParams(vmem_limit_bytes=VMEM_GRANT),
    )(*args)


def on_tile(
    prior_tracer_draws,
    courant_row,
    courant_column,
    diffusion,
    obs_value,
    observation_variance,
    obs_noise,
    obs_owner,
    obs_cell,
    obs_order,
):
    f32 = jnp.float32
    region_rows, columns = prior_tracer_draws.shape[1:]
    members = obs_noise.shape[1]
    mem_count, reg_count = lax.axis_size("mem"), lax.axis_size("reg")
    sizes = (reg_count, region_rows, region_rows // mem_count, columns)
    packed = columns // SUBLANES
    tile = (SUBLANES, LANES)
    field = (SUBLANES, columns)
    points_shape = (SUBLANES, TILES * LANES)
    message = (SUBLANES, 3 * packed + TILES * LANES)
    rates = (courant_row, courant_column, diffusion)
    flat = [x.reshape(1, LANES) for x in (obs_owner, obs_cell, obs_order, obs_value, observation_variance)]
    operands = (prior_tracer_draws, *rates, *flat, obs_noise.T)
    pair, cross, points, partial, table, noise, *rates = call(
        functools.partial(start_kernel, sizes),
        [(message, f32), (message, f32), (points_shape, f32), (field, f32), (tile, f32), (tile, f32)]
        + [(x.shape, x.dtype) for x in rates],
        [pltpu.with_memory_space_constraint(x, pltpu.HBM) for x in operands],
        scratch=[pltpu.VMEM(prior_tracer_draws.shape, f32)]
        + [pltpu.VMEM(x.shape, x.dtype) for x in operands[4:]]
        + [pltpu.SemaphoreType.DMA((len(operands),))],
        space=pltpu.HBM,
    )

    pairs = [(i, i ^ 1) for i in range(reg_count)]
    crosses = [(i, (i - 1 + 2 * (i & 1)) % reg_count) for i in range(reg_count)]
    crossed = lax.ppermute(cross, "reg", crosses)
    paired = lax.ppermute(pair, "reg", pairs)
    far = lax.ppermute(points, "reg", [(i, i ^ 2) for i in range(reg_count)])
    col_taper, obs_taper, row_taper = call(
        functools.partial(taper_kernel, sizes),
        [((2, LANES, columns), jnp.bfloat16), ((2, LANES, LANES), jnp.bfloat16), (tile, f32)],
        (table,),
        cost=pl.CostEstimate(flops=10 * LANES * columns, bytes_accessed=8 * LANES * columns, transcendentals=LANES * columns),
    )
    forecast, send = call(
        functools.partial(middle_kernel, sizes),
        [(field, f32), ((mem_count, SUBLANES, columns + LANES), jnp.int16)],
        (partial, *rates, pair, cross, points, paired, crossed, far),
        scratch=[pltpu.VMEM(field, f32)],
    )
    half = mem_count // 2
    along = [*range(half // 2, -1, -1), *range(half // 2 + 1, half)]
    order = [2 * z + y for y in range(2) for z in along]
    slabs = lax.all_to_all(
        send, "mem", split_axis=0, concat_axis=0, tiled=True, axis_index_groups=[order]
    )
    (out,) = call(
        functools.partial(finish_kernel, sizes, order),
        [(prior_tracer_draws.shape, f32)],
        (slabs, forecast, table, noise, col_taper, obs_taper, row_taper),
        scratch=[pltpu.VMEM((members, SUBLANES, CHUNK), f32)],
    )
    return out


def fits_tile(*shapes):
    draws, noise = shapes
    members, region_rows, columns = draws
    counts = (lax.axis_size("mem"), lax.axis_size("reg"))
    return (
        members == 1
        and noise[1] == counts[0] == region_rows == SUBLANES
        and noise[0] == NOB * NBLK == LANES
        and counts[1] == 4
        and columns % CHUNK == 0
        and columns & (columns - 1) == 0
    )


def on_device(*args):
    return (on_tile if fits_tile(args[0].shape, args[6].shape) else on_slabs)(*args)


def solution(mesh):
    placed = (
        P("mem", "reg", None),
        P("reg", None),
        P("reg", None),
        P("reg", None),
        P(),
        P(),
        P(),
        P(),
        P(),
        P(),
    )
    return jax.shard_map(
        on_device, mesh=mesh, in_specs=placed, out_specs=P("mem", "reg", None), check_vma=False
    )
```

```python
import functools

import jax
import jax.numpy as jnp
from jax import lax
from jax.experimental import pallas as pl
from jax.experimental.pallas import tpu as pltpu
from jax.sharding import PartitionSpec as P

NOB = 64
NBLK = 2


HIGH = lax.Precision.HIGHEST


def extended(cells, sides, width):
    for axis, dim in sides:
        count = lax.axis_size(axis)
        head = lax.slice_in_dim(cells, 0, width, axis=dim)
        tail = lax.slice_in_dim(cells, cells.shape[dim] - width, cells.shape[dim], axis=dim)
        cells = jnp.concatenate(
            [
                lax.ppermute(tail, axis, [(i, (i + 1) % count) for i in range(count)]),
                cells,
                lax.ppermute(head, axis, [((i + 1) % count, i) for i in range(count)]),
            ],
            axis=dim,
        )
    return cells


def bell(delta, period, scale):
    delta = delta % period
    dist = jnp.minimum(delta, period - delta).astype(jnp.float32)
    return jnp.exp(-0.5 * (dist / scale) ** 2)


def advance_rows(haloed_extended_grid, courant_row, courant_column, diffusion):
    centre = haloed_extended_grid[1:-1]
    north = haloed_extended_grid[:-2]
    south = haloed_extended_grid[2:]
    west = jnp.roll(centre, 1, axis=1)
    east = jnp.roll(centre, -1, axis=1)
    return (
        centre
        - 0.5 * courant_column * (east - west)
        - 0.5 * courant_row * (south - north)
        + diffusion * (north + south + east + west - 4.0 * centre)
    )


def measured_kalman_gain(prior, values, variance, noise):
    members = prior.shape[0]
    anomaly = prior - jnp.mean(prior, axis=0)
    spread = jnp.dot(anomaly.T, anomaly, precision=HIGH, preferred_element_type=jnp.float32) / (
        members - 1
    )
    system = spread + jnp.diag(variance)
    factor = jnp.linalg.cholesky(system)
    innovation = values[:, None] + jnp.sqrt(variance)[:, None] * noise - prior.T
    weights = jax.scipy.linalg.cho_solve((factor, True), innovation)
    return (anomaly, weights)


def increment(columns, anomaly, weights, taper):
    members = columns.shape[0]
    centred = columns - jnp.mean(columns, axis=0)
    cross = lax.dot_general(
        centred,
        anomaly,
        (((0,), (0,)), ((), ())),
        precision=HIGH,
        preferred_element_type=jnp.float32,
    ) / (members - 1)
    return columns + lax.dot_general(
        weights,
        taper * cross,
        (((0,), (1,)), ((), ())),
        precision=HIGH,
        preferred_element_type=jnp.float32,
    )


def on_slabs(
    prior_tracer_draws,
    courant_row,
    courant_column,
    diffusion,
    obs_value,
    observation_variance,
    obs_noise,
    obs_owner,
    obs_cell,
    obs_order,
):
    region_rows = prior_tracer_draws.shape[1]
    columns = prior_tracer_draws.shape[2]
    mem_count = lax.axis_size("mem")
    reg_count = lax.axis_size("reg")
    slab_rows = region_rows // mem_count
    grid_rows = region_rows * reg_count
    latitude_weighting = region_rows // 2
    col_scale = columns // 4
    rate_row = courant_row.astype(jnp.float32)
    column_rate = courant_column.astype(jnp.float32)
    rate_diff = diffusion.astype(jnp.float32)
    field = prior_tracer_draws[0]
    for step in range(2):
        haloed_extended_grid = extended(field, (("reg", 0),), 1)
        field = advance_rows(haloed_extended_grid, rate_row, column_rate, rate_diff)
    slabs = lax.all_to_all(field[None], "mem", split_axis=1, concat_axis=0, tiled=True)
    members = slabs.shape[0]
    cells = slabs.reshape(members, slab_rows * columns)
    me_mem = lax.axis_index("mem")
    me_reg = lax.axis_index("reg")
    myself = me_mem * reg_count + me_reg
    owned_rows = me_reg * region_rows + me_mem * slab_rows + jnp.arange(slab_rows, dtype=jnp.int32)
    obs_row = (
        obs_owner % reg_count * region_rows
        + obs_owner // reg_count * slab_rows
        + obs_cell // columns
    )
    observation_column = obs_cell % columns
    col_index = jnp.arange(columns, dtype=jnp.int32)
    owners = obs_owner[obs_order]
    spots = obs_cell[obs_order]
    sorted_row = obs_row[obs_order]
    sorted_col = observation_column[obs_order]
    local = jnp.where((owners == myself)[None, :], cells[:, spots], 0.0)
    priors = lax.psum(local, ("mem", "reg"))
    for block in range(NBLK):
        lower = block * NOB
        upper = (block + 1) * NOB
        chosen = obs_order[lower:upper]
        prior = priors[:, lower:upper]
        anomaly, weights = measured_kalman_gain(
            prior, obs_value[chosen], observation_variance[chosen], obs_noise[chosen]
        )
        orow = sorted_row[lower:upper]
        ocol = sorted_col[lower:upper]
        row_taper = bell(owned_rows[:, None] - orow[None, :], grid_rows, latitude_weighting)
        col_taper = bell(col_index[:, None] - ocol[None, :], columns, col_scale)
        cells = increment(
            cells,
            anomaly,
            weights,
            (row_taper[:, None, :] * col_taper[None, :, :]).reshape(
                slab_rows * columns, orow.shape[0]
            ),
        )
        obs_taper = bell(sorted_row[:, None] - orow[None, :], grid_rows, latitude_weighting) * bell(
            sorted_col[:, None] - ocol[None, :], columns, col_scale
        )
        priors = increment(priors, anomaly, weights, obs_taper)
    return lax.all_to_all(
        cells.reshape(members, slab_rows, columns), "mem", split_axis=0, concat_axis=1, tiled=True
    )


SUBLANES = 8
LANES = 128
POINTS = [(dr, dc) for dr in range(-2, 3) for dc in range(-2, 3) if abs(dr) + abs(dc) <= 2]
CROSS = [(0, 0), (-1, 0), (1, 0), (0, -1), (0, 1)]
TILES = -(-(len(POINTS) + 3 * len(CROSS)) // SUBLANES)
CHUNK = 4 * LANES
CODE_STEP = 2.0**-20
CODE_TOP = 32767.0
SEEN_UNIT = 2.0**-11
SEEN_REST = 2.0**-15
VMEM_GRANT = 8 << 20


def iota(axis, shape=(SUBLANES, LANES)):
    return lax.broadcasted_iota(jnp.int32, shape, axis)


def row_of(x, i):
    return jnp.broadcast_to(x[i : i + 1, :], x.shape)


def stencil(q, north, south, rate_row, rate_col, rate_diff):
    columns = q.shape[1]
    west = pltpu.roll(q, 1, axis=1)
    east = pltpu.roll(q, columns - 1, axis=1)
    return (
        q
        - 0.5 * rate_col * (east - west)
        - 0.5 * rate_row * (south - north)
        + rate_diff * (north + south + east + west - 4.0 * q)
    )


def slot(c):
    return c % SUBLANES, c // SUBLANES * LANES


def start_kernel(
    sizes,
    q_hbm,
    row_hbm,
    col_hbm,
    diff_hbm,
    owner_hbm,
    cell_hbm,
    order_hbm,
    value_hbm,
    variance_hbm,
    noise_hbm,
    pair_ref,
    cross_ref,
    points_ref,
    partial_ref,
    sorted_ref,
    noise_out,
    row_ref,
    col_ref,
    diff_ref,
    q_ref,
    owner_ref,
    cell_ref,
    order_ref,
    value_ref,
    variance_ref,
    noise_ref,
    arrived,
):
    fetched = (
        (owner_hbm, owner_ref),
        (cell_hbm, cell_ref),
        (order_hbm, order_ref),
        (value_hbm, value_ref),
        (variance_hbm, variance_ref),
        (noise_hbm, noise_ref),
        (q_hbm, q_ref),
        (row_hbm, row_ref),
        (col_hbm, col_ref),
        (diff_hbm, diff_ref),
    )
    copies = [
        pltpu.make_async_copy(source, target, arrived.at[n])
        for n, (source, target) in enumerate(fetched)
    ]
    for copy in copies:
        copy.start()
    for copy in copies[:6]:
        copy.wait()
    reg_count, region_rows, slab_rows, columns = sizes
    grid_rows = reg_count * region_rows
    packed = columns // SUBLANES
    me = lax.axis_index("reg")
    sub = iota(0)
    owner = owner_ref[...]
    cell = cell_ref[...]
    shift = columns.bit_length() - 1
    obs_row = (
        (owner & (reg_count - 1)) * region_rows
        + (owner >> (reg_count.bit_length() - 1)) * slab_rows
        + (cell >> shift)
    )
    obs_col = cell & (columns - 1)
    table = jnp.where(
        sub == 0,
        obs_row.astype(jnp.float32),
        jnp.where(
            sub == 1,
            obs_col.astype(jnp.float32),
            jnp.where(sub == 2, value_ref[...], jnp.where(sub == 3, variance_ref[...], 0.0)),
        ),
    )
    square = (LANES, LANES)
    pick = (iota(0, square) == order_ref[...]).astype(jnp.float32)
    both = jnp.dot(
        jnp.concatenate([table, noise_ref[...]], axis=0),
        pick,
        precision=HIGH,
        preferred_element_type=jnp.float32,
    )
    table = both[:SUBLANES]
    sorted_ref[...] = table
    noise_out[...] = both[SUBLANES:]
    orow = row_of(table, 0).astype(jnp.int32)
    ocol = row_of(table, 1).astype(jnp.int32)

    for copy in copies[6:]:
        copy.wait()
    q = q_ref[0]
    rates = [r[...].astype(jnp.float32) for r in (row_ref, col_ref, diff_ref)]
    local_row = orow - me * region_rows
    for dc in range(-2, 3):
        index = (ocol + dc) & (columns - 1)
        lane = index & (LANES - 1)
        tile = index >> (LANES.bit_length() - 1)
        wanted = [(q, 0, POINTS)]
        if abs(dc) <= 1:
            for n, rate in enumerate(rates):
                wanted.append((rate, len(POINTS) + n * len(CROSS), CROSS))
        hits = [tile == t for t in range(columns // LANES)]
        for array, base, points in wanted:
            found = jnp.zeros((SUBLANES, LANES), jnp.float32)
            for t in range(columns // LANES):
                taken = jnp.take_along_axis(
                    array[:, t * LANES : (t + 1) * LANES], lane, axis=1, mode="promise_in_bounds"
                )
                found = jnp.where(hits[t], taken, found)
            for n, (dr, shift_col) in enumerate(points):
                if shift_col != dc:
                    continue
                here = ((local_row + dr) & (grid_rows - 1)) == sub
                s, at = slot(base + n)
                points_ref[s : s + 1, at : at + LANES] = jnp.sum(
                    jnp.where(here, found, 0.0), axis=0, keepdims=True
                )
    for c in range(len(POINTS) + 3 * len(CROSS), TILES * SUBLANES):
        s, at = slot(c)
        points_ref[s : s + 1, at : at + LANES] = jnp.zeros((1, LANES), jnp.float32)

    rate_row, rate_col, rate_diff = rates
    wide = iota(0, (SUBLANES, columns))
    north = jnp.where(wide == 0, 0.0, pltpu.roll(q, 1, axis=0))
    south = jnp.where(wide == SUBLANES - 1, 0.0, pltpu.roll(q, SUBLANES - 1, axis=0))
    partial = stencil(q, north, south, rate_row, rate_col, rate_diff)
    partial_ref[...] = partial
    even = (me & 1) == 0
    edges = [
        (array[SUBLANES - 1 :, :], array[:1, :])
        for array in (q, partial)
    ] + [((rate_diff - 0.5 * rate_row)[SUBLANES - 1 :, :], (rate_diff + 0.5 * rate_row)[:1, :])]
    for n, (lower, upper) in enumerate(edges):
        for ref, row in (
            (pair_ref, jnp.where(even, lower, upper)),
            (cross_ref, jnp.where(even, upper, lower)),
        ):
            for s in range(SUBLANES):
                ref[s : s + 1, n * packed : (n + 1) * packed] = row[
                    :, s * packed : (s + 1) * packed
                ]
    pair_ref[:, 3 * packed :] = points_ref[...]
    cross_ref[:, 3 * packed :] = points_ref[...]


def bell_of(dist, period, scale):
    dist = jnp.abs(dist)
    dist = jnp.minimum(dist, period - dist) / scale
    return jnp.exp(-0.5 * (dist * dist))


def halves(x):
    high = x.astype(jnp.bfloat16)
    return high, (x - high.astype(jnp.float32)).astype(jnp.bfloat16)


def taper_kernel(sizes, sorted_ref, columns_ref, obs_ref, rows_ref):
    reg_count, region_rows, slab_rows, columns = sizes
    grid_rows = reg_count * region_rows
    row_scale, col_scale = float(region_rows // 2), float(columns // 4)
    me = lax.axis_index("reg")
    square = (LANES, LANES)
    row_lanes = jnp.broadcast_to(sorted_ref[0:1, :], square)
    col_lanes = jnp.broadcast_to(sorted_ref[1:2, :], square)
    row_subs = row_lanes.T
    col_subs = col_lanes.T
    for t in range(columns // LANES):
        at = (t * LANES + iota(1, square)).astype(jnp.float32)
        high, low = halves(bell_of(at - col_subs, float(columns), col_scale))
        columns_ref[0, :, t * LANES : (t + 1) * LANES] = high
        columns_ref[1, :, t * LANES : (t + 1) * LANES] = low
    high, low = halves(
        bell_of(row_lanes - row_subs, float(grid_rows), row_scale)
        * bell_of(col_lanes - col_subs, float(columns), col_scale)
    )
    obs_ref[0] = high
    obs_ref[1] = low
    rows = (me * region_rows + iota(0)).astype(jnp.float32)
    rows_ref[...] = bell_of(rows - row_lanes[:SUBLANES], float(grid_rows), row_scale)


def middle_kernel(
    sizes,
    partial_ref,
    row_ref,
    col_ref,
    diff_ref,
    pair_ref,
    cross_ref,
    paired_ref,
    crossed_ref,
    field_ref,
    code_ref,
    steps_ref,
    edge_ref,
):
    reg_count, region_rows, slab_rows, columns = sizes
    packed = columns // SUBLANES
    wide = iota(0, (SUBLANES, columns))
    rate_row, rate_col, rate_diff = [
        r[...].astype(jnp.float32) for r in (row_ref, col_ref, diff_ref)
    ]

    def section(ref, n):
        return ref[:, n * packed : (n + 1) * packed]

    def ahead(ref, sent_ref):
        return section(ref, 0), section(ref, 1) + section(ref, 2) * section(sent_ref, 0)

    even = (lax.axis_index("reg") & 1) == 0
    paired, crossed = ahead(paired_ref, pair_ref), ahead(crossed_ref, cross_ref)
    outer = [
        jnp.where(even, one, other)
        for x, y in zip(paired, crossed)
        for one, other in ((y, x), (x, y))
    ]
    for n, array in enumerate(outer):
        for s in range(SUBLANES):
            edge_ref[n : n + 1, s * packed : (s + 1) * packed] = array[s : s + 1, :]

    def edge(n):
        return jnp.broadcast_to(edge_ref[n : n + 1, :], (SUBLANES, columns))

    first, last = wide == 0, wide == SUBLANES - 1
    field = (
        partial_ref[...]
        + jnp.where(first, (rate_diff + 0.5 * rate_row) * edge(0), 0.0)
        + jnp.where(last, (rate_diff - 0.5 * rate_row) * edge(1), 0.0)
    )
    north = jnp.where(first, edge(2), pltpu.roll(field, 1, axis=0))
    south = jnp.where(last, edge(3), pltpu.roll(field, SUBLANES - 1, axis=0))
    field = stencil(field, north, south, rate_row, rate_col, rate_diff)

    field_ref[...] = field
    peak = jnp.max(jnp.max(jnp.abs(field), axis=1, keepdims=True), axis=0, keepdims=True)
    steps = jnp.maximum(jnp.ceil(peak * (1.0 / (CODE_TOP * CODE_STEP))), 1.0)
    code = jnp.round(field * (1.0 / (steps * CODE_STEP)))
    code_ref[...] = code.astype(jnp.int32).astype(jnp.int16)
    steps_ref[...] = jnp.broadcast_to(steps, (SUBLANES, LANES))


def observe_kernel(
    sizes, points_ref, paired_ref, crossed_ref, far_ref, code_ref, steps_ref, out_ref
):
    packed = sizes[-1] // SUBLANES
    points = (
        points_ref[...] + far_ref[...] + paired_ref[:, 3 * packed :] + crossed_ref[:, 3 * packed :]
    )

    def point(c):
        s, at = slot(c)
        return points[s : s + 1, at : at + LANES]

    q0 = {p: point(n) for n, p in enumerate(POINTS)}
    rates = [
        {p: point(len(POINTS) + n * len(CROSS) + i) for i, p in enumerate(CROSS)} for n in range(3)
    ]

    def at_point(values, p):
        i, j = p
        here = values[p]
        north, south = values[i - 1, j], values[i + 1, j]
        west, east = values[i, j - 1], values[i, j + 1]
        return (
            here
            - 0.5 * rates[1][p] * (east - west)
            - 0.5 * rates[0][p] * (south - north)
            + rates[2][p] * (north + south + east + west - 4.0 * here)
        )

    q1 = {p: at_point(q0, p) for p in CROSS}
    seen = jnp.broadcast_to(at_point(q1, (0, 0)), (SUBLANES, LANES)) / SEEN_UNIT
    whole = jnp.round(seen)
    rest = jnp.round((seen - whole) / SEEN_REST)
    sub = iota(0)
    tail = jnp.where(sub == 0, whole, jnp.where(sub == 1, rest, steps_ref[...]))
    message = jnp.concatenate([code_ref[...], tail.astype(jnp.int32).astype(jnp.int16)], axis=1)
    for d in range(out_ref.shape[0]):
        out_ref[d] = message


def gain(anomaly, precision, innovation):
    members = anomaly.shape[0]
    sub = iota(0)
    weighted = anomaly * precision

    def against(x):
        total = jnp.sum(weighted * x, axis=1, keepdims=True)
        return jnp.broadcast_to(total, weighted.shape)

    system = [
        against(row_of(anomaly, b)) + jnp.where(sub == b, float(members - 1), 0.0)
        for b in range(members)
    ]
    load = [against(row_of(innovation, m)) for m in range(members)]
    held = anomaly
    for k in range(members):
        inverse = 1.0 / row_of(system[k], k)
        mine = sub == k

        def step(x, k=k, inverse=inverse, mine=mine):
            scaled = row_of(x, k) * inverse
            return jnp.where(mine, scaled, x - system[k] * scaled)

        held = step(held)
        for b in range(k + 1, members):
            system[b] = step(system[b])
    fitted = jnp.zeros_like(anomaly)
    for m in range(members):
        total = jnp.sum(load[m] * held, axis=0, keepdims=True)
        fitted = jnp.where(sub == m, jnp.broadcast_to(total, held.shape), fitted)
    return precision * (innovation - fitted)


def twice(x, block):
    lane = iota(1)
    half = LANES // 2
    return jnp.where(lane // half == block, x, pltpu.roll(x, half, axis=1))


def split(rows):
    half = LANES // 2
    high = rows.astype(jnp.bfloat16).astype(jnp.float32)
    left = jnp.where(iota(1, rows.shape) < half, high, rows - high).astype(jnp.bfloat16)
    return jnp.concatenate([left, left], axis=1)


def stacked(table_ref, block, part=slice(None)):
    half = LANES // 2
    high = table_ref[0, block * half : (block + 1) * half, part]
    low = table_ref[1, block * half : (block + 1) * half, part]
    return jnp.concatenate([high, high, low, low], axis=0)


def finish_kernel(
    sizes,
    order,
    x_ref,
    field_ref,
    sorted_ref,
    noise_ref,
    columns_ref,
    obs_ref,
    rows_ref,
    out_ref,
    now_ref,
):
    columns = sizes[-1]
    members = x_ref.shape[0]
    me = lax.axis_index("mem")
    sub, lane = iota(0), iota(1)
    half = LANES // 2
    place = [order.index(m) for m in range(members)]
    seen = jnp.zeros((SUBLANES, LANES), jnp.float32)
    steps = []
    for m in range(members):
        tail = x_ref[place[m], :, columns:].astype(jnp.float32)
        value = (row_of(tail, 0) + row_of(tail, 1) * SEEN_REST) * SEEN_UNIT
        seen = jnp.where(sub == m, value, seen)
        steps.append(row_of(tail, 2) * CODE_STEP)
    value, variance = row_of(sorted_ref, 2), row_of(sorted_ref, 3)
    observed = value + jnp.sqrt(variance) * noise_ref[...]
    inverse_variance = 1.0 / variance
    scale = 1.0 / (members - 1)
    lefts = []
    for block in range(NBLK):
        last = block + 1 == NBLK
        anomaly = seen - jnp.sum(seen, axis=0, keepdims=True) * (1.0 / members)
        precision = jnp.where(lane // half == block, inverse_variance, 0.0)
        gains = gain(anomaly, precision, observed - seen) * scale
        gains, local = twice(gains, block), twice(anomaly, block)
        pairs = [row_of(local, a) * gains for a in range(members)]
        row_taper = twice(rows_ref[...], block)
        used = pairs[: members - 1]
        if last:
            own = [
                jnp.sum(jnp.where(sub == me, pair, 0.0), axis=0, keepdims=True) for pair in used
            ]
            lefts.append([row_taper * x for x in own])
        else:
            moved = jnp.dot(
                split(jnp.concatenate(pairs, axis=0)),
                stacked(obs_ref, block),
                preferred_element_type=jnp.float32,
            )
            for a in range(members):
                seen = seen + row_of(anomaly, a) * moved[a * SUBLANES : (a + 1) * SUBLANES]
            lefts.append([row_taper * row_of(pair, m) for pair in used for m in range(members)])
    lefts = [split(jnp.concatenate(x, axis=0)) for x in lefts]

    def added(starts, fields, weights):
        apart = [x - fields[-1] for x in fields[:-1]]
        updated = []
        for n, total in enumerate(starts):
            for a, x in enumerate(apart):
                at = (a * len(starts) + n) * SUBLANES
                total = total + x * weights[at : at + SUBLANES]
            updated.append(total)
        return updated

    for begin in range(0, columns, CHUNK):
        part = slice(begin, begin + CHUNK)

        def decoded(m, part=part):
            return x_ref[place[m], :, part].astype(jnp.float32)

        current = [decoded(m) * steps[m][:, :1] for m in range(members)]
        for m in range(members):
            now_ref[m] = current[m]
        sent = now_ref[me]
        for block in range(NBLK):
            weights = jnp.dot(
                lefts[block],
                stacked(columns_ref, block, part),
                preferred_element_type=jnp.float32,
            )
            if block + 1 < NBLK:
                current = added(current, current, weights)
                for m in range(members):
                    now_ref[m] = current[m]
            else:
                own = now_ref[me] + (field_ref[:, part] - sent)
                (own,) = added([own], current, weights)
                out_ref[0, :, part] = own


def call(kernel, outs, args, scratch=(), cost=None, space=pltpu.VMEM):
    held = pl.BlockSpec(memory_space=pltpu.VMEM)
    return pl.pallas_call(
        kernel,
        out_shape=[jax.ShapeDtypeStruct(s, d) for s, d in outs],
        in_specs=[pl.BlockSpec(memory_space=space)] * len(args),
        out_specs=[held] * len(outs),
        scratch_shapes=list(scratch),
        cost_estimate=cost,
        compiler_params=pltpu.CompilerParams(vmem_limit_bytes=VMEM_GRANT),
    )(*args)


def on_tile(
    prior_tracer_draws,
    courant_row,
    courant_column,
    diffusion,
    obs_value,
    observation_variance,
    obs_noise,
    obs_owner,
    obs_cell,
    obs_order,
):
    f32 = jnp.float32
    region_rows, columns = prior_tracer_draws.shape[1:]
    members = obs_noise.shape[1]
    mem_count, reg_count = lax.axis_size("mem"), lax.axis_size("reg")
    sizes = (reg_count, region_rows, region_rows // mem_count, columns)
    packed = columns // SUBLANES
    tile = (SUBLANES, LANES)
    field = (SUBLANES, columns)
    points_shape = (SUBLANES, TILES * LANES)
    message = (SUBLANES, 3 * packed + TILES * LANES)
    rates = (courant_row, courant_column, diffusion)
    flat = [x.reshape(1, LANES) for x in (obs_owner, obs_cell, obs_order, obs_value, observation_variance)]
    operands = (prior_tracer_draws, *rates, *flat, obs_noise.T)
    pair, cross, points, partial, table, noise, *rates = call(
        functools.partial(start_kernel, sizes),
        [(message, f32), (message, f32), (points_shape, f32), (field, f32), (tile, f32), (tile, f32)]
        + [(x.shape, x.dtype) for x in rates],
        [pltpu.with_memory_space_constraint(x, pltpu.HBM) for x in operands],
        scratch=[pltpu.VMEM(prior_tracer_draws.shape, f32)]
        + [pltpu.VMEM(x.shape, x.dtype) for x in operands[4:]]
        + [pltpu.SemaphoreType.DMA((len(operands),))],
        space=pltpu.HBM,
    )

    pairs = [(i, i ^ 1) for i in range(reg_count)]
    crosses = [(i, (i - 1 + 2 * (i & 1)) % reg_count) for i in range(reg_count)]
    crossed = lax.ppermute(cross, "reg", crosses)
    paired = lax.ppermute(pair, "reg", pairs)
    far = lax.ppermute(points, "reg", [(i, i ^ 2) for i in range(reg_count)])
    col_taper, obs_taper, row_taper = call(
        functools.partial(taper_kernel, sizes),
        [((2, LANES, columns), jnp.bfloat16), ((2, LANES, LANES), jnp.bfloat16), (tile, f32)],
        (table,),
        cost=pl.CostEstimate(flops=10 * LANES * columns, bytes_accessed=8 * LANES * columns, transcendentals=LANES * columns),
    )
    forecast, code, steps = call(
        functools.partial(middle_kernel, sizes),
        [(field, f32), (field, jnp.int16), (tile, f32)],
        (partial, *rates, pair, cross, paired, crossed),
        scratch=[pltpu.VMEM(field, f32)],
    )
    (send,) = call(
        functools.partial(observe_kernel, sizes),
        [((mem_count, SUBLANES, columns + LANES), jnp.int16)],
        (points, paired, crossed, far, code, steps),
    )
    half = mem_count // 2
    along = [*range(half // 2, -1, -1), *range(half // 2 + 1, half)]
    order = [2 * z + y for y in range(2) for z in along]
    slabs = lax.all_to_all(
        send, "mem", split_axis=0, concat_axis=0, tiled=True, axis_index_groups=[order]
    )
    (out,) = call(
        functools.partial(finish_kernel, sizes, order),
        [(prior_tracer_draws.shape, f32)],
        (slabs, forecast, table, noise, col_taper, obs_taper, row_taper),
        scratch=[pltpu.VMEM((members, SUBLANES, CHUNK), f32)],
    )
    return out


def fits_tile(*shapes):
    draws, noise = shapes
    members, region_rows, columns = draws
    counts = (lax.axis_size("mem"), lax.axis_size("reg"))
    return (
        members == 1
        and noise[1] == counts[0] == region_rows == SUBLANES
        and noise[0] == NOB * NBLK == LANES
        and counts[1] == 4
        and columns % CHUNK == 0
        and columns & (columns - 1) == 0
    )


def on_device(*args):
    return (on_tile if fits_tile(args[0].shape, args[6].shape) else on_slabs)(*args)


def solution(mesh):
    placed = (
        P("mem", "reg", None),
        P("reg", None),
        P("reg", None),
        P("reg", None),
        P(),
        P(),
        P(),
        P(),
        P(),
        P(),
    )
    return jax.shard_map(
        on_device, mesh=mesh, in_specs=placed, out_specs=P("mem", "reg", None), check_vma=False
    )
```

```python
import functools

import jax
import jax.numpy as jnp
from jax import lax
from jax.experimental import pallas as pl
from jax.experimental.pallas import tpu as pltpu
from jax.sharding import PartitionSpec as P

NOB = 64
NBLK = 2


HIGH = lax.Precision.HIGHEST


def extended(cells, sides, width):
    for axis, dim in sides:
        count = lax.axis_size(axis)
        head = lax.slice_in_dim(cells, 0, width, axis=dim)
        tail = lax.slice_in_dim(cells, cells.shape[dim] - width, cells.shape[dim], axis=dim)
        cells = jnp.concatenate(
            [
                lax.ppermute(tail, axis, [(i, (i + 1) % count) for i in range(count)]),
                cells,
                lax.ppermute(head, axis, [((i + 1) % count, i) for i in range(count)]),
            ],
            axis=dim,
        )
    return cells


def bell(delta, period, scale):
    delta = delta % period
    dist = jnp.minimum(delta, period - delta).astype(jnp.float32)
    return jnp.exp(-0.5 * (dist / scale) ** 2)


def advance_rows(haloed_extended_grid, courant_row, courant_column, diffusion):
    centre = haloed_extended_grid[1:-1]
    north = haloed_extended_grid[:-2]
    south = haloed_extended_grid[2:]
    west = jnp.roll(centre, 1, axis=1)
    east = jnp.roll(centre, -1, axis=1)
    return (
        centre
        - 0.5 * courant_column * (east - west)
        - 0.5 * courant_row * (south - north)
        + diffusion * (north + south + east + west - 4.0 * centre)
    )


def measured_kalman_gain(prior, values, variance, noise):
    members = prior.shape[0]
    anomaly = prior - jnp.mean(prior, axis=0)
    spread = jnp.dot(anomaly.T, anomaly, precision=HIGH, preferred_element_type=jnp.float32) / (
        members - 1
    )
    system = spread + jnp.diag(variance)
    factor = jnp.linalg.cholesky(system)
    innovation = values[:, None] + jnp.sqrt(variance)[:, None] * noise - prior.T
    weights = jax.scipy.linalg.cho_solve((factor, True), innovation)
    return (anomaly, weights)


def increment(columns, anomaly, weights, taper):
    members = columns.shape[0]
    centred = columns - jnp.mean(columns, axis=0)
    cross = lax.dot_general(
        centred,
        anomaly,
        (((0,), (0,)), ((), ())),
        precision=HIGH,
        preferred_element_type=jnp.float32,
    ) / (members - 1)
    return columns + lax.dot_general(
        weights,
        taper * cross,
        (((0,), (1,)), ((), ())),
        precision=HIGH,
        preferred_element_type=jnp.float32,
    )


def on_slabs(
    prior_tracer_draws,
    courant_row,
    courant_column,
    diffusion,
    obs_value,
    observation_variance,
    obs_noise,
    obs_owner,
    obs_cell,
    obs_order,
):
    region_rows = prior_tracer_draws.shape[1]
    columns = prior_tracer_draws.shape[2]
    mem_count = lax.axis_size("mem")
    reg_count = lax.axis_size("reg")
    slab_rows = region_rows // mem_count
    grid_rows = region_rows * reg_count
    latitude_weighting = region_rows // 2
    col_scale = columns // 4
    rate_row = courant_row.astype(jnp.float32)
    column_rate = courant_column.astype(jnp.float32)
    rate_diff = diffusion.astype(jnp.float32)
    field = prior_tracer_draws[0]
    for step in range(2):
        haloed_extended_grid = extended(field, (("reg", 0),), 1)
        field = advance_rows(haloed_extended_grid, rate_row, column_rate, rate_diff)
    slabs = lax.all_to_all(field[None], "mem", split_axis=1, concat_axis=0, tiled=True)
    members = slabs.shape[0]
    cells = slabs.reshape(members, slab_rows * columns)
    me_mem = lax.axis_index("mem")
    me_reg = lax.axis_index("reg")
    myself = me_mem * reg_count + me_reg
    owned_rows = me_reg * region_rows + me_mem * slab_rows + jnp.arange(slab_rows, dtype=jnp.int32)
    obs_row = (
        obs_owner % reg_count * region_rows
        + obs_owner // reg_count * slab_rows
        + obs_cell // columns
    )
    observation_column = obs_cell % columns
    col_index = jnp.arange(columns, dtype=jnp.int32)
    owners = obs_owner[obs_order]
    spots = obs_cell[obs_order]
    sorted_row = obs_row[obs_order]
    sorted_col = observation_column[obs_order]
    local = jnp.where((owners == myself)[None, :], cells[:, spots], 0.0)
    priors = lax.psum(local, ("mem", "reg"))
    for block in range(NBLK):
        lower = block * NOB
        upper = (block + 1) * NOB
        chosen = obs_order[lower:upper]
        prior = priors[:, lower:upper]
        anomaly, weights = measured_kalman_gain(
            prior, obs_value[chosen], observation_variance[chosen], obs_noise[chosen]
        )
        orow = sorted_row[lower:upper]
        ocol = sorted_col[lower:upper]
        row_taper = bell(owned_rows[:, None] - orow[None, :], grid_rows, latitude_weighting)
        col_taper = bell(col_index[:, None] - ocol[None, :], columns, col_scale)
        cells = increment(
            cells,
            anomaly,
            weights,
            (row_taper[:, None, :] * col_taper[None, :, :]).reshape(
                slab_rows * columns, orow.shape[0]
            ),
        )
        obs_taper = bell(sorted_row[:, None] - orow[None, :], grid_rows, latitude_weighting) * bell(
            sorted_col[:, None] - ocol[None, :], columns, col_scale
        )
        priors = increment(priors, anomaly, weights, obs_taper)
    return lax.all_to_all(
        cells.reshape(members, slab_rows, columns), "mem", split_axis=0, concat_axis=1, tiled=True
    )


SUBLANES = 8
LANES = 128
POINTS = [(dr, dc) for dr in range(-2, 3) for dc in range(-2, 3) if abs(dr) + abs(dc) <= 2]
CROSS = [(0, 0), (-1, 0), (1, 0), (0, -1), (0, 1)]
TILES = -(-(len(POINTS) + 3 * len(CROSS)) // SUBLANES)
CODE_STEP = 2.0**-20
CODE_TOP = 32767.0
SEEN_UNIT = 2.0**-11
SEEN_REST = 2.0**-15
VMEM_GRANT = 8 << 20


def iota(axis, shape=(SUBLANES, LANES)):
    return lax.broadcasted_iota(jnp.int32, shape, axis)


def row_of(x, i):
    return jnp.broadcast_to(x[i : i + 1, :], x.shape)


def stencil(q, north, south, rate_row, rate_col, rate_diff):
    columns = q.shape[1]
    west = pltpu.roll(q, 1, axis=1)
    east = pltpu.roll(q, columns - 1, axis=1)
    return (
        q
        - 0.5 * rate_col * (east - west)
        - 0.5 * rate_row * (south - north)
        + rate_diff * (north + south + east + west - 4.0 * q)
    )


def slot(c):
    return c % SUBLANES, c // SUBLANES * LANES


def start_kernel(
    sizes,
    q_hbm,
    row_hbm,
    col_hbm,
    diff_hbm,
    owner_hbm,
    cell_hbm,
    order_hbm,
    value_hbm,
    variance_hbm,
    noise_hbm,
    pair_ref,
    cross_ref,
    points_ref,
    partial_ref,
    sorted_ref,
    noise_out,
    row_ref,
    col_ref,
    diff_ref,
    q_ref,
    owner_ref,
    cell_ref,
    order_ref,
    value_ref,
    variance_ref,
    noise_ref,
    arrived,
):
    fetched = (
        (owner_hbm, owner_ref),
        (cell_hbm, cell_ref),
        (order_hbm, order_ref),
        (value_hbm, value_ref),
        (variance_hbm, variance_ref),
        (noise_hbm, noise_ref),
        (q_hbm, q_ref),
        (row_hbm, row_ref),
        (col_hbm, col_ref),
        (diff_hbm, diff_ref),
    )
    copies = [
        pltpu.make_async_copy(source, target, arrived.at[n])
        for n, (source, target) in enumerate(fetched)
    ]
    for copy in copies:
        copy.start()
    for copy in copies[:6]:
        copy.wait()
    reg_count, region_rows, slab_rows, columns = sizes
    grid_rows = reg_count * region_rows
    packed = columns // SUBLANES
    me = lax.axis_index("reg")
    sub = iota(0)
    owner = owner_ref[...]
    cell = cell_ref[...]
    shift = columns.bit_length() - 1
    obs_row = (
        (owner & (reg_count - 1)) * region_rows
        + (owner >> (reg_count.bit_length() - 1)) * slab_rows
        + (cell >> shift)
    )
    obs_col = cell & (columns - 1)
    table = jnp.where(
        sub == 0,
        obs_row.astype(jnp.float32),
        jnp.where(
            sub == 1,
            obs_col.astype(jnp.float32),
            jnp.where(sub == 2, value_ref[...], jnp.where(sub == 3, variance_ref[...], 0.0)),
        ),
    )
    square = (LANES, LANES)
    pick = (iota(0, square) == order_ref[...]).astype(jnp.float32)
    both = jnp.dot(
        jnp.concatenate([table, noise_ref[...]], axis=0),
        pick,
        precision=HIGH,
        preferred_element_type=jnp.float32,
    )
    table = both[:SUBLANES]
    sorted_ref[...] = table
    noise_out[...] = both[SUBLANES:]
    orow = row_of(table, 0).astype(jnp.int32)
    ocol = row_of(table, 1).astype(jnp.int32)

    for copy in copies[6:]:
        copy.wait()
    q = q_ref[0]
    rates = [r[...].astype(jnp.float32) for r in (row_ref, col_ref, diff_ref)]
    local_row = orow - me * region_rows
    for dc in range(-2, 3):
        index = (ocol + dc) & (columns - 1)
        lane = index & (LANES - 1)
        tile = index >> (LANES.bit_length() - 1)
        wanted = [(q, 0, POINTS)]
        if abs(dc) <= 1:
            for n, rate in enumerate(rates):
                wanted.append((rate, len(POINTS) + n * len(CROSS), CROSS))
        hits = [tile == t for t in range(columns // LANES)]
        for array, base, points in wanted:
            found = jnp.zeros((SUBLANES, LANES), jnp.float32)
            for t in range(columns // LANES):
                taken = jnp.take_along_axis(
                    array[:, t * LANES : (t + 1) * LANES], lane, axis=1, mode="promise_in_bounds"
                )
                found = jnp.where(hits[t], taken, found)
            for n, (dr, shift_col) in enumerate(points):
                if shift_col != dc:
                    continue
                here = ((local_row + dr) & (grid_rows - 1)) == sub
                s, at = slot(base + n)
                points_ref[s : s + 1, at : at + LANES] = jnp.sum(
                    jnp.where(here, found, 0.0), axis=0, keepdims=True
                )
    for c in range(len(POINTS) + 3 * len(CROSS), TILES * SUBLANES):
        s, at = slot(c)
        points_ref[s : s + 1, at : at + LANES] = jnp.zeros((1, LANES), jnp.float32)

    rate_row, rate_col, rate_diff = rates
    wide = iota(0, (SUBLANES, columns))
    north = jnp.where(wide == 0, 0.0, pltpu.roll(q, 1, axis=0))
    south = jnp.where(wide == SUBLANES - 1, 0.0, pltpu.roll(q, SUBLANES - 1, axis=0))
    partial = stencil(q, north, south, rate_row, rate_col, rate_diff)
    partial_ref[...] = partial
    even = (me & 1) == 0
    edges = [
        (array[SUBLANES - 1 :, :], array[:1, :])
        for array in (q, partial)
    ] + [((rate_diff - 0.5 * rate_row)[SUBLANES - 1 :, :], (rate_diff + 0.5 * rate_row)[:1, :])]
    for n, (lower, upper) in enumerate(edges):
        for ref, row in (
            (pair_ref, jnp.where(even, lower, upper)),
            (cross_ref, jnp.where(even, upper, lower)),
        ):
            for s in range(SUBLANES):
                ref[s : s + 1, n * packed : (n + 1) * packed] = row[
                    :, s * packed : (s + 1) * packed
                ]
    pair_ref[:, 3 * packed :] = points_ref[...]
    cross_ref[:, 3 * packed :] = points_ref[...]


def bell_of(dist, period, scale):
    dist = jnp.abs(dist)
    dist = jnp.minimum(dist, period - dist) / scale
    return jnp.exp(-0.5 * (dist * dist))


def halves(x):
    high = x.astype(jnp.bfloat16)
    return high, (x - high.astype(jnp.float32)).astype(jnp.bfloat16)


def taper_kernel(sizes, sorted_ref, columns_ref, obs_ref, rows_ref):
    reg_count, region_rows, slab_rows, columns = sizes
    grid_rows = reg_count * region_rows
    row_scale, col_scale = float(region_rows // 2), float(columns // 4)
    me = lax.axis_index("reg")
    square = (LANES, LANES)
    row_lanes = jnp.broadcast_to(sorted_ref[0:1, :], square)
    col_lanes = jnp.broadcast_to(sorted_ref[1:2, :], square)
    row_subs = row_lanes.T
    col_subs = col_lanes.T
    for t in range(columns // LANES):
        at = (t * LANES + iota(1, square)).astype(jnp.float32)
        high, low = halves(bell_of(at - col_subs, float(columns), col_scale))
        columns_ref[0, :, t * LANES : (t + 1) * LANES] = high
        columns_ref[1, :, t * LANES : (t + 1) * LANES] = low
    high, low = halves(
        bell_of(row_lanes - row_subs, float(grid_rows), row_scale)
        * bell_of(col_lanes - col_subs, float(columns), col_scale)
    )
    obs_ref[0] = high
    obs_ref[1] = low
    rows = (me * region_rows + iota(0)).astype(jnp.float32)
    rows_ref[...] = bell_of(rows - row_lanes[:SUBLANES], float(grid_rows), row_scale)


def middle_kernel(
    sizes,
    partial_ref,
    row_ref,
    col_ref,
    diff_ref,
    pair_ref,
    cross_ref,
    paired_ref,
    crossed_ref,
    field_ref,
    code_ref,
    steps_ref,
    edge_ref,
):
    reg_count, region_rows, slab_rows, columns = sizes
    packed = columns // SUBLANES
    wide = iota(0, (SUBLANES, columns))
    rate_row, rate_col, rate_diff = [
        r[...].astype(jnp.float32) for r in (row_ref, col_ref, diff_ref)
    ]

    def section(ref, n):
        return ref[:, n * packed : (n + 1) * packed]

    def ahead(ref, sent_ref):
        return section(ref, 0), section(ref, 1) + section(ref, 2) * section(sent_ref, 0)

    even = (lax.axis_index("reg") & 1) == 0
    paired, crossed = ahead(paired_ref, pair_ref), ahead(crossed_ref, cross_ref)
    outer = [
        jnp.where(even, one, other)
        for x, y in zip(paired, crossed)
        for one, other in ((y, x), (x, y))
    ]
    for n, array in enumerate(outer):
        for s in range(SUBLANES):
            edge_ref[n : n + 1, s * packed : (s + 1) * packed] = array[s : s + 1, :]

    def edge(n):
        return jnp.broadcast_to(edge_ref[n : n + 1, :], (SUBLANES, columns))

    first, last = wide == 0, wide == SUBLANES - 1
    field = (
        partial_ref[...]
        + jnp.where(first, (rate_diff + 0.5 * rate_row) * edge(0), 0.0)
        + jnp.where(last, (rate_diff - 0.5 * rate_row) * edge(1), 0.0)
    )
    north = jnp.where(first, edge(2), pltpu.roll(field, 1, axis=0))
    south = jnp.where(last, edge(3), pltpu.roll(field, SUBLANES - 1, axis=0))
    field = stencil(field, north, south, rate_row, rate_col, rate_diff)

    field_ref[...] = field
    peak = jnp.max(jnp.max(jnp.abs(field), axis=1, keepdims=True), axis=0, keepdims=True)
    steps = jnp.maximum(jnp.ceil(peak * (1.0 / (CODE_TOP * CODE_STEP))), 1.0)
    code = jnp.round(field * (1.0 / (steps * CODE_STEP)))
    code_ref[...] = code.astype(jnp.int32).astype(jnp.int16)
    steps_ref[...] = jnp.broadcast_to(steps, (SUBLANES, LANES))


def observe_kernel(
    sizes, points_ref, paired_ref, crossed_ref, far_ref, code_ref, steps_ref, out_ref
):
    packed = sizes[-1] // SUBLANES
    points = (
        points_ref[...] + far_ref[...] + paired_ref[:, 3 * packed :] + crossed_ref[:, 3 * packed :]
    )

    def point(c):
        s, at = slot(c)
        return points[s : s + 1, at : at + LANES]

    q0 = {p: point(n) for n, p in enumerate(POINTS)}
    rates = [
        {p: point(len(POINTS) + n * len(CROSS) + i) for i, p in enumerate(CROSS)} for n in range(3)
    ]

    def at_point(values, p):
        i, j = p
        here = values[p]
        north, south = values[i - 1, j], values[i + 1, j]
        west, east = values[i, j - 1], values[i, j + 1]
        return (
            here
            - 0.5 * rates[1][p] * (east - west)
            - 0.5 * rates[0][p] * (south - north)
            + rates[2][p] * (north + south + east + west - 4.0 * here)
        )

    q1 = {p: at_point(q0, p) for p in CROSS}
    seen = jnp.broadcast_to(at_point(q1, (0, 0)), (SUBLANES, LANES)) / SEEN_UNIT
    whole = jnp.round(seen)
    rest = jnp.round((seen - whole) / SEEN_REST)
    sub = iota(0)
    tail = jnp.where(sub == 0, whole, jnp.where(sub == 1, rest, steps_ref[...]))
    message = jnp.concatenate([code_ref[...], tail.astype(jnp.int32).astype(jnp.int16)], axis=1)
    for d in range(out_ref.shape[0]):
        out_ref[d] = message


def gain(anomaly, precision, innovation):
    members = anomaly.shape[0]
    sub = iota(0)
    weighted = anomaly * precision

    def against(x):
        total = jnp.sum(weighted * x, axis=1, keepdims=True)
        return jnp.broadcast_to(total, weighted.shape)

    system = [
        against(row_of(anomaly, b)) + jnp.where(sub == b, float(members - 1), 0.0)
        for b in range(members)
    ]
    load = [against(row_of(innovation, m)) for m in range(members)]
    held = anomaly
    for k in range(members):
        inverse = 1.0 / row_of(system[k], k)
        mine = sub == k

        def step(x, k=k, inverse=inverse, mine=mine):
            scaled = row_of(x, k) * inverse
            return jnp.where(mine, scaled, x - system[k] * scaled)

        held = step(held)
        for b in range(k + 1, members):
            system[b] = step(system[b])
    fitted = jnp.zeros_like(anomaly)
    for m in range(members):
        total = jnp.sum(load[m] * held, axis=0, keepdims=True)
        fitted = jnp.where(sub == m, jnp.broadcast_to(total, held.shape), fitted)
    return precision * (innovation - fitted)


def twice(x, block):
    lane = iota(1)
    half = LANES // 2
    return jnp.where(lane // half == block, x, pltpu.roll(x, half, axis=1))


def split(rows):
    half = LANES // 2
    high = rows.astype(jnp.bfloat16).astype(jnp.float32)
    left = jnp.where(iota(1, rows.shape) < half, high, rows - high).astype(jnp.bfloat16)
    return jnp.concatenate([left, left], axis=1)


def stacked(table_ref, block, part=slice(None)):
    half = LANES // 2
    high = table_ref[0, block * half : (block + 1) * half, part]
    low = table_ref[1, block * half : (block + 1) * half, part]
    return jnp.concatenate([high, high, low, low], axis=0)


def finish_kernel(
    sizes,
    order,
    x_ref,
    field_ref,
    sorted_ref,
    noise_ref,
    columns_ref,
    obs_ref,
    rows_ref,
    out_ref,
    now_ref,
):
    columns = sizes[-1]
    members = x_ref.shape[0]
    me = lax.axis_index("mem")
    sub, lane = iota(0), iota(1)
    half = LANES // 2
    place = [order.index(m) for m in range(members)]
    seen = jnp.zeros((SUBLANES, LANES), jnp.float32)
    steps = []
    for m in range(members):
        tail = x_ref[place[m], :, columns:].astype(jnp.float32)
        value = (row_of(tail, 0) + row_of(tail, 1) * SEEN_REST) * SEEN_UNIT
        seen = jnp.where(sub == m, value, seen)
        steps.append(row_of(tail, 2) * CODE_STEP)
    value, variance = row_of(sorted_ref, 2), row_of(sorted_ref, 3)
    observed = value + jnp.sqrt(variance) * noise_ref[...]
    inverse_variance = 1.0 / variance
    scale = 1.0 / (members - 1)
    def added(starts, fields, weights):
        apart = [x - fields[-1] for x in fields[:-1]]
        updated = []
        for n, total in enumerate(starts):
            for a, x in enumerate(apart):
                at = (a * len(starts) + n) * SUBLANES
                total = total + x * weights[at : at + SUBLANES]
            updated.append(total)
        return updated

    current = [x_ref[place[m], :, :columns].astype(jnp.float32) * steps[m][:, :1] for m in range(members)]
    for m in range(members):
        now_ref[m] = current[m]
    base = field_ref[...] - now_ref[me]
    for block in range(NBLK):
        last = block + 1 == NBLK
        anomaly = seen - jnp.sum(seen, axis=0, keepdims=True) * (1.0 / members)
        precision = jnp.where(lane // half == block, inverse_variance, 0.0)
        gains = gain(anomaly, precision, observed - seen) * scale
        gains, local = twice(gains, block), twice(anomaly, block)
        pairs = [row_of(local, a) * gains for a in range(members)]
        row_taper = twice(rows_ref[...], block)
        used = pairs[: members - 1]
        if last:
            own = [
                jnp.sum(jnp.where(sub == me, pair, 0.0), axis=0, keepdims=True) for pair in used
            ]
            left = [row_taper * x for x in own]
        else:
            moved = jnp.dot(
                split(jnp.concatenate(pairs, axis=0)),
                stacked(obs_ref, block),
                preferred_element_type=jnp.float32,
            )
            for a in range(members):
                seen = seen + row_of(anomaly, a) * moved[a * SUBLANES : (a + 1) * SUBLANES]
            left = [row_taper * row_of(pair, m) for pair in used for m in range(members)]
        weights = jnp.dot(
            split(jnp.concatenate(left, axis=0)),
            stacked(columns_ref, block),
            preferred_element_type=jnp.float32,
        )
        if last:
            (out_ref[0],) = added([now_ref[me] + base], current, weights)
        else:
            current = added(current, current, weights)
            for m in range(members):
                now_ref[m] = current[m]


def call(kernel, outs, args, scratch=(), cost=None, space=pltpu.VMEM):
    held = pl.BlockSpec(memory_space=pltpu.VMEM)
    return pl.pallas_call(
        kernel,
        out_shape=[jax.ShapeDtypeStruct(s, d) for s, d in outs],
        in_specs=[pl.BlockSpec(memory_space=space)] * len(args),
        out_specs=[held] * len(outs),
        scratch_shapes=list(scratch),
        cost_estimate=cost,
        compiler_params=pltpu.CompilerParams(vmem_limit_bytes=VMEM_GRANT),
    )(*args)


def on_tile(
    prior_tracer_draws,
    courant_row,
    courant_column,
    diffusion,
    obs_value,
    observation_variance,
    obs_noise,
    obs_owner,
    obs_cell,
    obs_order,
):
    f32 = jnp.float32
    region_rows, columns = prior_tracer_draws.shape[1:]
    members = obs_noise.shape[1]
    mem_count, reg_count = lax.axis_size("mem"), lax.axis_size("reg")
    sizes = (reg_count, region_rows, region_rows // mem_count, columns)
    packed = columns // SUBLANES
    tile = (SUBLANES, LANES)
    field = (SUBLANES, columns)
    points_shape = (SUBLANES, TILES * LANES)
    message = (SUBLANES, 3 * packed + TILES * LANES)
    rates = (courant_row, courant_column, diffusion)
    flat = [x.reshape(1, LANES) for x in (obs_owner, obs_cell, obs_order, obs_value, observation_variance)]
    operands = (prior_tracer_draws, *rates, *flat, obs_noise.T)
    pair, cross, points, partial, table, noise, *rates = call(
        functools.partial(start_kernel, sizes),
        [(message, f32), (message, f32), (points_shape, f32), (field, f32), (tile, f32), (tile, f32)]
        + [(x.shape, x.dtype) for x in rates],
        [pltpu.with_memory_space_constraint(x, pltpu.HBM) for x in operands],
        scratch=[pltpu.VMEM(prior_tracer_draws.shape, f32)]
        + [pltpu.VMEM(x.shape, x.dtype) for x in operands[4:]]
        + [pltpu.SemaphoreType.DMA((len(operands),))],
        space=pltpu.HBM,
    )

    pairs = [(i, i ^ 1) for i in range(reg_count)]
    crosses = [(i, (i - 1 + 2 * (i & 1)) % reg_count) for i in range(reg_count)]
    crossed = lax.ppermute(cross, "reg", crosses)
    paired = lax.ppermute(pair, "reg", pairs)
    far = lax.ppermute(points, "reg", [(i, i ^ 2) for i in range(reg_count)])
    col_taper, obs_taper, row_taper = call(
        functools.partial(taper_kernel, sizes),
        [((2, LANES, columns), jnp.bfloat16), ((2, LANES, LANES), jnp.bfloat16), (tile, f32)],
        (table,),
        cost=pl.CostEstimate(flops=10 * LANES * columns, bytes_accessed=8 * LANES * columns, transcendentals=LANES * columns),
    )
    forecast, code, steps = call(
        functools.partial(middle_kernel, sizes),
        [(field, f32), (field, jnp.int16), (tile, f32)],
        (partial, *rates, pair, cross, paired, crossed),
        scratch=[pltpu.VMEM(field, f32)],
    )
    (send,) = call(
        functools.partial(observe_kernel, sizes),
        [((mem_count, SUBLANES, columns + LANES), jnp.int16)],
        (points, paired, crossed, far, code, steps),
    )
    half = mem_count // 2
    along = [*range(half // 2, -1, -1), *range(half // 2 + 1, half)]
    order = [2 * z + y for y in range(2) for z in along]
    slabs = lax.all_to_all(
        send, "mem", split_axis=0, concat_axis=0, tiled=True, axis_index_groups=[order]
    )
    (out,) = call(
        functools.partial(finish_kernel, sizes, order),
        [(prior_tracer_draws.shape, f32)],
        (slabs, forecast, table, noise, col_taper, obs_taper, row_taper),
        scratch=[pltpu.VMEM((members, *field), f32)],
    )
    return out


def fits_tile(*shapes):
    draws, noise = shapes
    members, region_rows, columns = draws
    counts = (lax.axis_size("mem"), lax.axis_size("reg"))
    return (
        members == 1
        and noise[1] == counts[0] == region_rows == SUBLANES
        and noise[0] == NOB * NBLK == LANES
        and counts[1] == 4
        and columns % (SUBLANES * LANES) == 0
        and columns & (columns - 1) == 0
    )


def on_device(*args):
    return (on_tile if fits_tile(args[0].shape, args[6].shape) else on_slabs)(*args)


def solution(mesh):
    placed = (
        P("mem", "reg", None),
        P("reg", None),
        P("reg", None),
        P("reg", None),
        P(),
        P(),
        P(),
        P(),
        P(),
        P(),
    )
    return jax.shard_map(
        on_device, mesh=mesh, in_specs=placed, out_specs=P("mem", "reg", None), check_vma=False
    )
```

```python
import functools

import jax
import jax.numpy as jnp
from jax import lax
from jax.experimental import pallas as pl
from jax.experimental.pallas import tpu as pltpu
from jax.sharding import PartitionSpec as P

NOB = 64
NBLK = 2


HIGH = lax.Precision.HIGHEST


def extended(cells, sides, width):
    for axis, dim in sides:
        count = lax.axis_size(axis)
        head = lax.slice_in_dim(cells, 0, width, axis=dim)
        tail = lax.slice_in_dim(cells, cells.shape[dim] - width, cells.shape[dim], axis=dim)
        cells = jnp.concatenate(
            [
                lax.ppermute(tail, axis, [(i, (i + 1) % count) for i in range(count)]),
                cells,
                lax.ppermute(head, axis, [((i + 1) % count, i) for i in range(count)]),
            ],
            axis=dim,
        )
    return cells


def bell(delta, period, scale):
    delta = delta % period
    dist = jnp.minimum(delta, period - delta).astype(jnp.float32)
    return jnp.exp(-0.5 * (dist / scale) ** 2)


def advance_rows(haloed_extended_grid, courant_row, courant_column, diffusion):
    centre = haloed_extended_grid[1:-1]
    north = haloed_extended_grid[:-2]
    south = haloed_extended_grid[2:]
    west = jnp.roll(centre, 1, axis=1)
    east = jnp.roll(centre, -1, axis=1)
    return (
        centre
        - 0.5 * courant_column * (east - west)
        - 0.5 * courant_row * (south - north)
        + diffusion * (north + south + east + west - 4.0 * centre)
    )


def measured_kalman_gain(prior, values, variance, noise):
    members = prior.shape[0]
    anomaly = prior - jnp.mean(prior, axis=0)
    spread = jnp.dot(anomaly.T, anomaly, precision=HIGH, preferred_element_type=jnp.float32) / (
        members - 1
    )
    system = spread + jnp.diag(variance)
    factor = jnp.linalg.cholesky(system)
    innovation = values[:, None] + jnp.sqrt(variance)[:, None] * noise - prior.T
    weights = jax.scipy.linalg.cho_solve((factor, True), innovation)
    return (anomaly, weights)


def increment(columns, anomaly, weights, taper):
    members = columns.shape[0]
    centred = columns - jnp.mean(columns, axis=0)
    cross = lax.dot_general(
        centred,
        anomaly,
        (((0,), (0,)), ((), ())),
        precision=HIGH,
        preferred_element_type=jnp.float32,
    ) / (members - 1)
    return columns + lax.dot_general(
        weights,
        taper * cross,
        (((0,), (1,)), ((), ())),
        precision=HIGH,
        preferred_element_type=jnp.float32,
    )


def on_slabs(
    prior_tracer_draws,
    courant_row,
    courant_column,
    diffusion,
    obs_value,
    observation_variance,
    obs_noise,
    obs_owner,
    obs_cell,
    obs_order,
):
    region_rows = prior_tracer_draws.shape[1]
    columns = prior_tracer_draws.shape[2]
    mem_count = lax.axis_size("mem")
    reg_count = lax.axis_size("reg")
    slab_rows = region_rows // mem_count
    grid_rows = region_rows * reg_count
    latitude_weighting = region_rows // 2
    col_scale = columns // 4
    rate_row = courant_row.astype(jnp.float32)
    column_rate = courant_column.astype(jnp.float32)
    rate_diff = diffusion.astype(jnp.float32)
    field = prior_tracer_draws[0]
    for step in range(2):
        haloed_extended_grid = extended(field, (("reg", 0),), 1)
        field = advance_rows(haloed_extended_grid, rate_row, column_rate, rate_diff)
    slabs = lax.all_to_all(field[None], "mem", split_axis=1, concat_axis=0, tiled=True)
    members = slabs.shape[0]
    cells = slabs.reshape(members, slab_rows * columns)
    me_mem = lax.axis_index("mem")
    me_reg = lax.axis_index("reg")
    myself = me_mem * reg_count + me_reg
    owned_rows = me_reg * region_rows + me_mem * slab_rows + jnp.arange(slab_rows, dtype=jnp.int32)
    obs_row = (
        obs_owner % reg_count * region_rows
        + obs_owner // reg_count * slab_rows
        + obs_cell // columns
    )
    observation_column = obs_cell % columns
    col_index = jnp.arange(columns, dtype=jnp.int32)
    owners = obs_owner[obs_order]
    spots = obs_cell[obs_order]
    sorted_row = obs_row[obs_order]
    sorted_col = observation_column[obs_order]
    local = jnp.where((owners == myself)[None, :], cells[:, spots], 0.0)
    priors = lax.psum(local, ("mem", "reg"))
    for block in range(NBLK):
        lower = block * NOB
        upper = (block + 1) * NOB
        chosen = obs_order[lower:upper]
        prior = priors[:, lower:upper]
        anomaly, weights = measured_kalman_gain(
            prior, obs_value[chosen], observation_variance[chosen], obs_noise[chosen]
        )
        orow = sorted_row[lower:upper]
        ocol = sorted_col[lower:upper]
        row_taper = bell(owned_rows[:, None] - orow[None, :], grid_rows, latitude_weighting)
        col_taper = bell(col_index[:, None] - ocol[None, :], columns, col_scale)
        cells = increment(
            cells,
            anomaly,
            weights,
            (row_taper[:, None, :] * col_taper[None, :, :]).reshape(
                slab_rows * columns, orow.shape[0]
            ),
        )
        obs_taper = bell(sorted_row[:, None] - orow[None, :], grid_rows, latitude_weighting) * bell(
            sorted_col[:, None] - ocol[None, :], columns, col_scale
        )
        priors = increment(priors, anomaly, weights, obs_taper)
    return lax.all_to_all(
        cells.reshape(members, slab_rows, columns), "mem", split_axis=0, concat_axis=1, tiled=True
    )


SUBLANES = 8
LANES = 128
POINTS = [(dr, dc) for dr in range(-2, 3) for dc in range(-2, 3) if abs(dr) + abs(dc) <= 2]
CROSS = [(0, 0), (-1, 0), (1, 0), (0, -1), (0, 1)]
TILES = -(-(len(POINTS) + 3 * len(CROSS)) // SUBLANES)
CODE_STEP = 2.0**-20
CODE_TOP = 32767.0
SEEN_UNIT = 2.0**-11
SEEN_REST = 2.0**-15
VMEM_GRANT = 8 << 20


def iota(axis, shape=(SUBLANES, LANES)):
    return lax.broadcasted_iota(jnp.int32, shape, axis)


def row_of(x, i):
    return jnp.broadcast_to(x[i : i + 1, :], x.shape)


def stencil(q, north, south, rate_row, rate_col, rate_diff):
    columns = q.shape[1]
    west = pltpu.roll(q, 1, axis=1)
    east = pltpu.roll(q, columns - 1, axis=1)
    return (
        q
        - 0.5 * rate_col * (east - west)
        - 0.5 * rate_row * (south - north)
        + rate_diff * (north + south + east + west - 4.0 * q)
    )


def slot(c):
    return c % SUBLANES, c // SUBLANES * LANES


def start_kernel(
    sizes,
    q_hbm,
    row_hbm,
    col_hbm,
    diff_hbm,
    owner_hbm,
    cell_hbm,
    order_hbm,
    value_hbm,
    variance_hbm,
    noise_hbm,
    pair_ref,
    cross_ref,
    points_ref,
    partial_ref,
    sorted_ref,
    noise_out,
    row_ref,
    col_ref,
    diff_ref,
    q_ref,
    owner_ref,
    cell_ref,
    order_ref,
    value_ref,
    variance_ref,
    noise_ref,
    arrived,
):
    fetched = (
        (owner_hbm, owner_ref),
        (cell_hbm, cell_ref),
        (order_hbm, order_ref),
        (value_hbm, value_ref),
        (variance_hbm, variance_ref),
        (noise_hbm, noise_ref),
        (q_hbm, q_ref),
        (row_hbm, row_ref),
        (col_hbm, col_ref),
        (diff_hbm, diff_ref),
    )
    copies = [
        pltpu.make_async_copy(source, target, arrived.at[n])
        for n, (source, target) in enumerate(fetched)
    ]
    for copy in copies:
        copy.start()
    for copy in copies[:6]:
        copy.wait()
    reg_count, region_rows, slab_rows, columns = sizes
    grid_rows = reg_count * region_rows
    packed = columns // SUBLANES
    me = lax.axis_index("reg")
    sub = iota(0)
    owner = owner_ref[...]
    cell = cell_ref[...]
    shift = columns.bit_length() - 1
    obs_row = (
        (owner & (reg_count - 1)) * region_rows
        + (owner >> (reg_count.bit_length() - 1)) * slab_rows
        + (cell >> shift)
    )
    obs_col = cell & (columns - 1)
    table = jnp.where(
        sub == 0,
        obs_row.astype(jnp.float32),
        jnp.where(
            sub == 1,
            obs_col.astype(jnp.float32),
            jnp.where(sub == 2, value_ref[...], jnp.where(sub == 3, variance_ref[...], 0.0)),
        ),
    )
    square = (LANES, LANES)
    pick = (iota(0, square) == order_ref[...]).astype(jnp.float32)
    both = jnp.dot(
        jnp.concatenate([table, noise_ref[...]], axis=0),
        pick,
        precision=HIGH,
        preferred_element_type=jnp.float32,
    )
    table = both[:SUBLANES]
    sorted_ref[...] = table
    noise_out[...] = both[SUBLANES:]
    orow = row_of(table, 0).astype(jnp.int32)
    ocol = row_of(table, 1).astype(jnp.int32)

    for copy in copies[6:]:
        copy.wait()
    q = q_ref[0]
    rates = [r[...].astype(jnp.float32) for r in (row_ref, col_ref, diff_ref)]
    local_row = orow - me * region_rows
    for dc in range(-2, 3):
        index = (ocol + dc) & (columns - 1)
        lane = index & (LANES - 1)
        tile = index >> (LANES.bit_length() - 1)
        wanted = [(q, 0, POINTS)]
        if abs(dc) <= 1:
            for n, rate in enumerate(rates):
                wanted.append((rate, len(POINTS) + n * len(CROSS), CROSS))
        hits = [tile == t for t in range(columns // LANES)]
        for array, base, points in wanted:
            found = jnp.zeros((SUBLANES, LANES), jnp.float32)
            for t in range(columns // LANES):
                taken = jnp.take_along_axis(
                    array[:, t * LANES : (t + 1) * LANES], lane, axis=1, mode="promise_in_bounds"
                )
                found = jnp.where(hits[t], taken, found)
            for n, (dr, shift_col) in enumerate(points):
                if shift_col != dc:
                    continue
                here = ((local_row + dr) & (grid_rows - 1)) == sub
                s, at = slot(base + n)
                points_ref[s : s + 1, at : at + LANES] = jnp.sum(
                    jnp.where(here, found, 0.0), axis=0, keepdims=True
                )
    for c in range(len(POINTS) + 3 * len(CROSS), TILES * SUBLANES):
        s, at = slot(c)
        points_ref[s : s + 1, at : at + LANES] = jnp.zeros((1, LANES), jnp.float32)

    rate_row, rate_col, rate_diff = rates
    wide = iota(0, (SUBLANES, columns))
    north = jnp.where(wide == 0, 0.0, pltpu.roll(q, 1, axis=0))
    south = jnp.where(wide == SUBLANES - 1, 0.0, pltpu.roll(q, SUBLANES - 1, axis=0))
    partial = stencil(q, north, south, rate_row, rate_col, rate_diff)
    partial_ref[...] = partial
    even = (me & 1) == 0
    edges = [
        (array[SUBLANES - 1 :, :], array[:1, :])
        for array in (q, partial)
    ] + [((rate_diff - 0.5 * rate_row)[SUBLANES - 1 :, :], (rate_diff + 0.5 * rate_row)[:1, :])]
    for n, (lower, upper) in enumerate(edges):
        for ref, row in (
            (pair_ref, jnp.where(even, lower, upper)),
            (cross_ref, jnp.where(even, upper, lower)),
        ):
            for s in range(SUBLANES):
                ref[s : s + 1, n * packed : (n + 1) * packed] = row[
                    :, s * packed : (s + 1) * packed
                ]
    pair_ref[:, 3 * packed :] = points_ref[...]
    cross_ref[:, 3 * packed :] = points_ref[...]


def bell_of(dist, period, scale):
    dist = jnp.abs(dist)
    dist = jnp.minimum(dist, period - dist) / scale
    return jnp.exp(-0.5 * (dist * dist))


def halves(x):
    high = x.astype(jnp.bfloat16)
    return high, (x - high.astype(jnp.float32)).astype(jnp.bfloat16)


def taper_kernel(sizes, sorted_ref, columns_ref, obs_ref, rows_ref):
    reg_count, region_rows, slab_rows, columns = sizes
    grid_rows = reg_count * region_rows
    row_scale, col_scale = float(region_rows // 2), float(columns // 4)
    me = lax.axis_index("reg")
    square = (LANES, LANES)
    row_lanes = jnp.broadcast_to(sorted_ref[0:1, :], square)
    col_lanes = jnp.broadcast_to(sorted_ref[1:2, :], square)
    row_subs = row_lanes.T
    col_subs = col_lanes.T
    for t in range(columns // LANES):
        at = (t * LANES + iota(1, square)).astype(jnp.float32)
        high, low = halves(bell_of(at - col_subs, float(columns), col_scale))
        columns_ref[0, :, t * LANES : (t + 1) * LANES] = high
        columns_ref[1, :, t * LANES : (t + 1) * LANES] = low
    high, low = halves(
        bell_of(row_lanes - row_subs, float(grid_rows), row_scale)
        * bell_of(col_lanes - col_subs, float(columns), col_scale)
    )
    obs_ref[0] = high
    obs_ref[1] = low
    rows = (me * region_rows + iota(0)).astype(jnp.float32)
    rows_ref[...] = bell_of(rows - row_lanes[:SUBLANES], float(grid_rows), row_scale)


def middle_kernel(
    sizes,
    partial_ref,
    row_ref,
    col_ref,
    diff_ref,
    pair_ref,
    cross_ref,
    paired_ref,
    crossed_ref,
    field_ref,
    code_ref,
    steps_ref,
    edge_ref,
):
    reg_count, region_rows, slab_rows, columns = sizes
    packed = columns // SUBLANES
    wide = iota(0, (SUBLANES, columns))
    rate_row, rate_col, rate_diff = [
        r[...].astype(jnp.float32) for r in (row_ref, col_ref, diff_ref)
    ]

    def section(ref, n):
        return ref[:, n * packed : (n + 1) * packed]

    def ahead(ref, sent_ref):
        return section(ref, 0), section(ref, 1) + section(ref, 2) * section(sent_ref, 0)

    even = (lax.axis_index("reg") & 1) == 0
    paired, crossed = ahead(paired_ref, pair_ref), ahead(crossed_ref, cross_ref)
    outer = [
        jnp.where(even, one, other)
        for x, y in zip(paired, crossed)
        for one, other in ((y, x), (x, y))
    ]
    for n, array in enumerate(outer):
        for s in range(SUBLANES):
            edge_ref[n : n + 1, s * packed : (s + 1) * packed] = array[s : s + 1, :]

    def edge(n):
        return jnp.broadcast_to(edge_ref[n : n + 1, :], (SUBLANES, columns))

    first, last = wide == 0, wide == SUBLANES - 1
    field = (
        partial_ref[...]
        + jnp.where(first, (rate_diff + 0.5 * rate_row) * edge(0), 0.0)
        + jnp.where(last, (rate_diff - 0.5 * rate_row) * edge(1), 0.0)
    )
    north = jnp.where(first, edge(2), pltpu.roll(field, 1, axis=0))
    south = jnp.where(last, edge(3), pltpu.roll(field, SUBLANES - 1, axis=0))
    field = stencil(field, north, south, rate_row, rate_col, rate_diff)

    field_ref[...] = field
    peak = jnp.max(jnp.max(jnp.abs(field), axis=1, keepdims=True), axis=0, keepdims=True)
    steps = jnp.maximum(jnp.ceil(peak * (1.0 / (CODE_TOP * CODE_STEP))), 1.0)
    code = jnp.round(field * (1.0 / (steps * CODE_STEP)))
    code_ref[...] = code.astype(jnp.int32).astype(jnp.int16)
    steps_ref[...] = jnp.broadcast_to(steps, (SUBLANES, LANES))


def observe_kernel(
    sizes, points_ref, paired_ref, crossed_ref, far_ref, code_ref, steps_ref, out_ref
):
    packed = sizes[-1] // SUBLANES
    points = (
        points_ref[...] + far_ref[...] + paired_ref[:, 3 * packed :] + crossed_ref[:, 3 * packed :]
    )

    def point(c):
        s, at = slot(c)
        return points[s : s + 1, at : at + LANES]

    q0 = {p: point(n) for n, p in enumerate(POINTS)}
    rates = [
        {p: point(len(POINTS) + n * len(CROSS) + i) for i, p in enumerate(CROSS)} for n in range(3)
    ]

    def at_point(values, p):
        i, j = p
        here = values[p]
        north, south = values[i - 1, j], values[i + 1, j]
        west, east = values[i, j - 1], values[i, j + 1]
        return (
            here
            - 0.5 * rates[1][p] * (east - west)
            - 0.5 * rates[0][p] * (south - north)
            + rates[2][p] * (north + south + east + west - 4.0 * here)
        )

    q1 = {p: at_point(q0, p) for p in CROSS}
    seen = jnp.broadcast_to(at_point(q1, (0, 0)), (SUBLANES, LANES)) / SEEN_UNIT
    whole = jnp.round(seen)
    rest = jnp.round((seen - whole) / SEEN_REST)
    sub = iota(0)
    tail = jnp.where(sub == 0, whole, jnp.where(sub == 1, rest, steps_ref[...]))
    message = jnp.concatenate([code_ref[...], tail.astype(jnp.int32).astype(jnp.int16)], axis=1)
    for d in range(out_ref.shape[0]):
        out_ref[d] = message


def gain(anomaly, precision, innovation):
    members = anomaly.shape[0]
    sub = iota(0)
    weighted = anomaly * precision

    def against(x):
        total = jnp.sum(weighted * x, axis=1, keepdims=True)
        return jnp.broadcast_to(total, weighted.shape)

    system = [
        against(row_of(anomaly, b)) + jnp.where(sub == b, float(members - 1), 0.0)
        for b in range(members)
    ]
    load = [against(row_of(innovation, m)) for m in range(members)]
    held = anomaly
    for k in range(members):
        inverse = 1.0 / row_of(system[k], k)
        mine = sub == k

        def step(x, k=k, inverse=inverse, mine=mine):
            scaled = row_of(x, k) * inverse
            return jnp.where(mine, scaled, x - system[k] * scaled)

        held = step(held)
        for b in range(k + 1, members):
            system[b] = step(system[b])
    fitted = jnp.zeros_like(anomaly)
    for m in range(members):
        total = jnp.sum(load[m] * held, axis=0, keepdims=True)
        fitted = jnp.where(sub == m, jnp.broadcast_to(total, held.shape), fitted)
    return precision * (innovation - fitted)


def twice(x, block):
    lane = iota(1)
    half = LANES // 2
    return jnp.where(lane // half == block, x, pltpu.roll(x, half, axis=1))


def split(rows):
    half = LANES // 2
    high = rows.astype(jnp.bfloat16).astype(jnp.float32)
    left = jnp.where(iota(1, rows.shape) < half, high, rows - high).astype(jnp.bfloat16)
    return jnp.concatenate([left, left], axis=1)


def stacked(table_ref, block, part=slice(None)):
    half = LANES // 2
    high = table_ref[0, block * half : (block + 1) * half, part]
    low = table_ref[1, block * half : (block + 1) * half, part]
    return jnp.concatenate([high, high, low, low], axis=0)


def finish_kernel(
    sizes,
    order,
    x_ref,
    field_ref,
    sorted_ref,
    noise_ref,
    columns_ref,
    obs_ref,
    rows_ref,
    out_ref,
    now_ref,
):
    columns = sizes[-1]
    members = x_ref.shape[0]
    me = lax.axis_index("mem")
    sub, lane = iota(0), iota(1)
    half = LANES // 2
    place = [order.index(m) for m in range(members)]
    seen = jnp.zeros((SUBLANES, LANES), jnp.float32)
    steps = []
    for m in range(members):
        tail = x_ref[place[m], :, columns:].astype(jnp.float32)
        value = (row_of(tail, 0) + row_of(tail, 1) * SEEN_REST) * SEEN_UNIT
        seen = jnp.where(sub == m, value, seen)
        steps.append(row_of(tail, 2) * CODE_STEP)
    value, variance = row_of(sorted_ref, 2), row_of(sorted_ref, 3)
    observed = value + jnp.sqrt(variance) * noise_ref[...]
    inverse_variance = 1.0 / variance
    scale = 1.0 / (members - 1)
    def added(starts, fields, weights):
        apart = [x - fields[-1] for x in fields[:-1]]
        updated = []
        for n, total in enumerate(starts):
            for a, x in enumerate(apart):
                at = (a * len(starts) + n) * SUBLANES
                total = total + x * weights[at : at + SUBLANES]
            updated.append(total)
        return updated

    current = [x_ref[place[m], :, :columns].astype(jnp.float32) * steps[m][:, :1] for m in range(members)]
    mine, my_step = place[0], steps[0]
    for m in range(1, members):
        mine = jnp.where(me == m, place[m], mine)
        my_step = jnp.where(me == m, steps[m], my_step)
    base = field_ref[...] - x_ref[mine, :, :columns].astype(jnp.float32) * my_step[:, :1]
    for block in range(NBLK):
        last = block + 1 == NBLK
        anomaly = seen - jnp.sum(seen, axis=0, keepdims=True) * (1.0 / members)
        precision = jnp.where(lane // half == block, inverse_variance, 0.0)
        gains = gain(anomaly, precision, observed - seen) * scale
        gains, local = twice(gains, block), twice(anomaly, block)
        pairs = [row_of(local, a) * gains for a in range(members)]
        row_taper = twice(rows_ref[...], block)
        used = pairs[: members - 1]
        if last:
            own = [
                jnp.sum(jnp.where(sub == me, pair, 0.0), axis=0, keepdims=True) for pair in used
            ]
            left = [row_taper * x for x in own]
        else:
            moved = jnp.dot(
                split(jnp.concatenate(pairs, axis=0)),
                stacked(obs_ref, block),
                preferred_element_type=jnp.float32,
            )
            for a in range(members):
                seen = seen + row_of(anomaly, a) * moved[a * SUBLANES : (a + 1) * SUBLANES]
            left = [row_taper * row_of(pair, m) for pair in used for m in range(members)]
        weights = jnp.dot(
            split(jnp.concatenate(left, axis=0)),
            stacked(columns_ref, block),
            preferred_element_type=jnp.float32,
        )
        if last:
            (out_ref[0],) = added([now_ref[me] + base], current, weights)
        else:
            current = added(current, current, weights)
            for m in range(members):
                now_ref[m] = current[m]


def call(kernel, outs, args, scratch=(), cost=None, space=pltpu.VMEM):
    held = pl.BlockSpec(memory_space=pltpu.VMEM)
    return pl.pallas_call(
        kernel,
        out_shape=[jax.ShapeDtypeStruct(s, d) for s, d in outs],
        in_specs=[pl.BlockSpec(memory_space=space)] * len(args),
        out_specs=[held] * len(outs),
        scratch_shapes=list(scratch),
        cost_estimate=cost,
        compiler_params=pltpu.CompilerParams(vmem_limit_bytes=VMEM_GRANT),
    )(*args)


def on_tile(
    prior_tracer_draws,
    courant_row,
    courant_column,
    diffusion,
    obs_value,
    observation_variance,
    obs_noise,
    obs_owner,
    obs_cell,
    obs_order,
):
    f32 = jnp.float32
    region_rows, columns = prior_tracer_draws.shape[1:]
    members = obs_noise.shape[1]
    mem_count, reg_count = lax.axis_size("mem"), lax.axis_size("reg")
    sizes = (reg_count, region_rows, region_rows // mem_count, columns)
    packed = columns // SUBLANES
    tile = (SUBLANES, LANES)
    field = (SUBLANES, columns)
    points_shape = (SUBLANES, TILES * LANES)
    message = (SUBLANES, 3 * packed + TILES * LANES)
    rates = (courant_row, courant_column, diffusion)
    flat = [x.reshape(1, LANES) for x in (obs_owner, obs_cell, obs_order, obs_value, observation_variance)]
    operands = (prior_tracer_draws, *rates, *flat, obs_noise.T)
    pair, cross, points, partial, table, noise, *rates = call(
        functools.partial(start_kernel, sizes),
        [(message, f32), (message, f32), (points_shape, f32), (field, f32), (tile, f32), (tile, f32)]
        + [(x.shape, x.dtype) for x in rates],
        [pltpu.with_memory_space_constraint(x, pltpu.HBM) for x in operands],
        scratch=[pltpu.VMEM(prior_tracer_draws.shape, f32)]
        + [pltpu.VMEM(x.shape, x.dtype) for x in operands[4:]]
        + [pltpu.SemaphoreType.DMA((len(operands),))],
        space=pltpu.HBM,
    )

    pairs = [(i, i ^ 1) for i in range(reg_count)]
    crosses = [(i, (i - 1 + 2 * (i & 1)) % reg_count) for i in range(reg_count)]
    crossed = lax.ppermute(cross, "reg", crosses)
    paired = lax.ppermute(pair, "reg", pairs)
    far = lax.ppermute(points, "reg", [(i, i ^ 2) for i in range(reg_count)])
    col_taper, obs_taper, row_taper = call(
        functools.partial(taper_kernel, sizes),
        [((2, LANES, columns), jnp.bfloat16), ((2, LANES, LANES), jnp.bfloat16), (tile, f32)],
        (table,),
        cost=pl.CostEstimate(flops=10 * LANES * columns, bytes_accessed=8 * LANES * columns, transcendentals=LANES * columns),
    )
    forecast, code, steps = call(
        functools.partial(middle_kernel, sizes),
        [(field, f32), (field, jnp.int16), (tile, f32)],
        (partial, *rates, pair, cross, paired, crossed),
        scratch=[pltpu.VMEM(field, f32)],
    )
    (send,) = call(
        functools.partial(observe_kernel, sizes),
        [((mem_count, SUBLANES, columns + LANES), jnp.int16)],
        (points, paired, crossed, far, code, steps),
    )
    half = mem_count // 2
    along = [*range(half // 2, -1, -1), *range(half // 2 + 1, half)]
    order = [2 * z + y for y in range(2) for z in along]
    slabs = lax.all_to_all(
        send, "mem", split_axis=0, concat_axis=0, tiled=True, axis_index_groups=[order]
    )
    (out,) = call(
        functools.partial(finish_kernel, sizes, order),
        [(prior_tracer_draws.shape, f32)],
        (slabs, forecast, table, noise, col_taper, obs_taper, row_taper),
        scratch=[pltpu.VMEM((members, *field), f32)],
    )
    return out


def fits_tile(*shapes):
    draws, noise = shapes
    members, region_rows, columns = draws
    counts = (lax.axis_size("mem"), lax.axis_size("reg"))
    return (
        members == 1
        and noise[1] == counts[0] == region_rows == SUBLANES
        and noise[0] == NOB * NBLK == LANES
        and counts[1] == 4
        and columns % (SUBLANES * LANES) == 0
        and columns & (columns - 1) == 0
    )


def on_device(*args):
    return (on_tile if fits_tile(args[0].shape, args[6].shape) else on_slabs)(*args)


def solution(mesh):
    placed = (
        P("mem", "reg", None),
        P("reg", None),
        P("reg", None),
        P("reg", None),
        P(),
        P(),
        P(),
        P(),
        P(),
        P(),
    )
    return jax.shard_map(
        on_device, mesh=mesh, in_specs=placed, out_specs=P("mem", "reg", None), check_vma=False
    )
```

```python
import functools

import jax
import jax.numpy as jnp
from jax import lax
from jax.experimental import pallas as pl
from jax.experimental.pallas import tpu as pltpu
from jax.sharding import PartitionSpec as P

NOB = 64
NBLK = 2


HIGH = lax.Precision.HIGHEST


def extended(cells, sides, width):
    for axis, dim in sides:
        count = lax.axis_size(axis)
        head = lax.slice_in_dim(cells, 0, width, axis=dim)
        tail = lax.slice_in_dim(cells, cells.shape[dim] - width, cells.shape[dim], axis=dim)
        cells = jnp.concatenate(
            [
                lax.ppermute(tail, axis, [(i, (i + 1) % count) for i in range(count)]),
                cells,
                lax.ppermute(head, axis, [((i + 1) % count, i) for i in range(count)]),
            ],
            axis=dim,
        )
    return cells


def bell(delta, period, scale):
    delta = delta % period
    dist = jnp.minimum(delta, period - delta).astype(jnp.float32)
    return jnp.exp(-0.5 * (dist / scale) ** 2)


def advance_rows(haloed_extended_grid, courant_row, courant_column, diffusion):
    centre = haloed_extended_grid[1:-1]
    north = haloed_extended_grid[:-2]
    south = haloed_extended_grid[2:]
    west = jnp.roll(centre, 1, axis=1)
    east = jnp.roll(centre, -1, axis=1)
    return (
        centre
        - 0.5 * courant_column * (east - west)
        - 0.5 * courant_row * (south - north)
        + diffusion * (north + south + east + west - 4.0 * centre)
    )


def measured_kalman_gain(prior, values, variance, noise):
    members = prior.shape[0]
    anomaly = prior - jnp.mean(prior, axis=0)
    spread = jnp.dot(anomaly.T, anomaly, precision=HIGH, preferred_element_type=jnp.float32) / (
        members - 1
    )
    system = spread + jnp.diag(variance)
    factor = jnp.linalg.cholesky(system)
    innovation = values[:, None] + jnp.sqrt(variance)[:, None] * noise - prior.T
    weights = jax.scipy.linalg.cho_solve((factor, True), innovation)
    return (anomaly, weights)


def increment(columns, anomaly, weights, taper):
    members = columns.shape[0]
    centred = columns - jnp.mean(columns, axis=0)
    cross = lax.dot_general(
        centred,
        anomaly,
        (((0,), (0,)), ((), ())),
        precision=HIGH,
        preferred_element_type=jnp.float32,
    ) / (members - 1)
    return columns + lax.dot_general(
        weights,
        taper * cross,
        (((0,), (1,)), ((), ())),
        precision=HIGH,
        preferred_element_type=jnp.float32,
    )


def on_slabs(
    prior_tracer_draws,
    courant_row,
    courant_column,
    diffusion,
    obs_value,
    observation_variance,
    obs_noise,
    obs_owner,
    obs_cell,
    obs_order,
):
    region_rows = prior_tracer_draws.shape[1]
    columns = prior_tracer_draws.shape[2]
    mem_count = lax.axis_size("mem")
    reg_count = lax.axis_size("reg")
    slab_rows = region_rows // mem_count
    grid_rows = region_rows * reg_count
    latitude_weighting = region_rows // 2
    col_scale = columns // 4
    rate_row = courant_row.astype(jnp.float32)
    column_rate = courant_column.astype(jnp.float32)
    rate_diff = diffusion.astype(jnp.float32)
    field = prior_tracer_draws[0]
    for step in range(2):
        haloed_extended_grid = extended(field, (("reg", 0),), 1)
        field = advance_rows(haloed_extended_grid, rate_row, column_rate, rate_diff)
    slabs = lax.all_to_all(field[None], "mem", split_axis=1, concat_axis=0, tiled=True)
    members = slabs.shape[0]
    cells = slabs.reshape(members, slab_rows * columns)
    me_mem = lax.axis_index("mem")
    me_reg = lax.axis_index("reg")
    myself = me_mem * reg_count + me_reg
    owned_rows = me_reg * region_rows + me_mem * slab_rows + jnp.arange(slab_rows, dtype=jnp.int32)
    obs_row = (
        obs_owner % reg_count * region_rows
        + obs_owner // reg_count * slab_rows
        + obs_cell // columns
    )
    observation_column = obs_cell % columns
    col_index = jnp.arange(columns, dtype=jnp.int32)
    owners = obs_owner[obs_order]
    spots = obs_cell[obs_order]
    sorted_row = obs_row[obs_order]
    sorted_col = observation_column[obs_order]
    local = jnp.where((owners == myself)[None, :], cells[:, spots], 0.0)
    priors = lax.psum(local, ("mem", "reg"))
    for block in range(NBLK):
        lower = block * NOB
        upper = (block + 1) * NOB
        chosen = obs_order[lower:upper]
        prior = priors[:, lower:upper]
        anomaly, weights = measured_kalman_gain(
            prior, obs_value[chosen], observation_variance[chosen], obs_noise[chosen]
        )
        orow = sorted_row[lower:upper]
        ocol = sorted_col[lower:upper]
        row_taper = bell(owned_rows[:, None] - orow[None, :], grid_rows, latitude_weighting)
        col_taper = bell(col_index[:, None] - ocol[None, :], columns, col_scale)
        cells = increment(
            cells,
            anomaly,
            weights,
            (row_taper[:, None, :] * col_taper[None, :, :]).reshape(
                slab_rows * columns, orow.shape[0]
            ),
        )
        obs_taper = bell(sorted_row[:, None] - orow[None, :], grid_rows, latitude_weighting) * bell(
            sorted_col[:, None] - ocol[None, :], columns, col_scale
        )
        priors = increment(priors, anomaly, weights, obs_taper)
    return lax.all_to_all(
        cells.reshape(members, slab_rows, columns), "mem", split_axis=0, concat_axis=1, tiled=True
    )


SUBLANES = 8
LANES = 128
POINTS = [(dr, dc) for dr in range(-2, 3) for dc in range(-2, 3) if abs(dr) + abs(dc) <= 2]
CROSS = [(0, 0), (-1, 0), (1, 0), (0, -1), (0, 1)]
TILES = -(-(len(POINTS) + 3 * len(CROSS)) // SUBLANES)
CODE_STEP = 2.0**-20
CODE_TOP = 32767.0
SEEN_UNIT = 2.0**-11
SEEN_REST = 2.0**-15
VMEM_GRANT = 8 << 20


def iota(axis, shape=(SUBLANES, LANES)):
    return lax.broadcasted_iota(jnp.int32, shape, axis)


def row_of(x, i):
    return jnp.broadcast_to(x[i : i + 1, :], x.shape)


def stencil(q, north, south, rate_row, rate_col, rate_diff):
    columns = q.shape[1]
    west = pltpu.roll(q, 1, axis=1)
    east = pltpu.roll(q, columns - 1, axis=1)
    return (
        q
        - 0.5 * rate_col * (east - west)
        - 0.5 * rate_row * (south - north)
        + rate_diff * (north + south + east + west - 4.0 * q)
    )


def slot(c):
    return c % SUBLANES, c // SUBLANES * LANES


def start_kernel(
    sizes,
    q_hbm,
    row_hbm,
    col_hbm,
    diff_hbm,
    owner_hbm,
    cell_hbm,
    order_hbm,
    value_hbm,
    variance_hbm,
    noise_hbm,
    pair_ref,
    cross_ref,
    points_ref,
    partial_ref,
    sorted_ref,
    noise_out,
    row_ref,
    col_ref,
    diff_ref,
    q_ref,
    owner_ref,
    cell_ref,
    order_ref,
    value_ref,
    variance_ref,
    noise_ref,
    arrived,
):
    fetched = (
        (owner_hbm, owner_ref),
        (cell_hbm, cell_ref),
        (order_hbm, order_ref),
        (value_hbm, value_ref),
        (variance_hbm, variance_ref),
        (noise_hbm, noise_ref),
        (q_hbm, q_ref),
        (row_hbm, row_ref),
        (col_hbm, col_ref),
        (diff_hbm, diff_ref),
    )
    copies = [
        pltpu.make_async_copy(source, target, arrived.at[n])
        for n, (source, target) in enumerate(fetched)
    ]
    for copy in copies:
        copy.start()
    for copy in copies[:6]:
        copy.wait()
    reg_count, region_rows, slab_rows, columns = sizes
    grid_rows = reg_count * region_rows
    packed = columns // SUBLANES
    me = lax.axis_index("reg")
    sub = iota(0)
    owner = owner_ref[...]
    cell = cell_ref[...]
    shift = columns.bit_length() - 1
    obs_row = (
        (owner & (reg_count - 1)) * region_rows
        + (owner >> (reg_count.bit_length() - 1)) * slab_rows
        + (cell >> shift)
    )
    obs_col = cell & (columns - 1)
    table = jnp.where(
        sub == 0,
        obs_row.astype(jnp.float32),
        jnp.where(
            sub == 1,
            obs_col.astype(jnp.float32),
            jnp.where(sub == 2, value_ref[...], jnp.where(sub == 3, variance_ref[...], 0.0)),
        ),
    )
    square = (LANES, LANES)
    pick = (iota(0, square) == order_ref[...]).astype(jnp.float32)
    both = jnp.dot(
        jnp.concatenate([table, noise_ref[...]], axis=0),
        pick,
        precision=HIGH,
        preferred_element_type=jnp.float32,
    )
    table = both[:SUBLANES]
    sorted_ref[...] = table
    noise_out[...] = both[SUBLANES:]
    orow = row_of(table, 0).astype(jnp.int32)
    ocol = row_of(table, 1).astype(jnp.int32)

    for copy in copies[6:]:
        copy.wait()
    q = q_ref[0]
    rates = [r[...].astype(jnp.float32) for r in (row_ref, col_ref, diff_ref)]
    local_row = orow - me * region_rows
    for dc in range(-2, 3):
        index = (ocol + dc) & (columns - 1)
        lane = index & (LANES - 1)
        tile = index >> (LANES.bit_length() - 1)
        wanted = [(q, 0, POINTS)]
        if abs(dc) <= 1:
            for n, rate in enumerate(rates):
                wanted.append((rate, len(POINTS) + n * len(CROSS), CROSS))
        hits = [tile == t for t in range(columns // LANES)]
        for array, base, points in wanted:
            found = jnp.zeros((SUBLANES, LANES), jnp.float32)
            for t in range(columns // LANES):
                taken = jnp.take_along_axis(
                    array[:, t * LANES : (t + 1) * LANES], lane, axis=1, mode="promise_in_bounds"
                )
                found = jnp.where(hits[t], taken, found)
            for n, (dr, shift_col) in enumerate(points):
                if shift_col != dc:
                    continue
                here = ((local_row + dr) & (grid_rows - 1)) == sub
                s, at = slot(base + n)
                points_ref[s : s + 1, at : at + LANES] = jnp.sum(
                    jnp.where(here, found, 0.0), axis=0, keepdims=True
                )
    for c in range(len(POINTS) + 3 * len(CROSS), TILES * SUBLANES):
        s, at = slot(c)
        points_ref[s : s + 1, at : at + LANES] = jnp.zeros((1, LANES), jnp.float32)

    rate_row, rate_col, rate_diff = rates
    wide = iota(0, (SUBLANES, columns))
    north = jnp.where(wide == 0, 0.0, pltpu.roll(q, 1, axis=0))
    south = jnp.where(wide == SUBLANES - 1, 0.0, pltpu.roll(q, SUBLANES - 1, axis=0))
    partial = stencil(q, north, south, rate_row, rate_col, rate_diff)
    partial_ref[...] = partial
    even = (me & 1) == 0
    edges = [
        (array[SUBLANES - 1 :, :], array[:1, :])
        for array in (q, partial)
    ] + [((rate_diff - 0.5 * rate_row)[SUBLANES - 1 :, :], (rate_diff + 0.5 * rate_row)[:1, :])]
    for n, (lower, upper) in enumerate(edges):
        for ref, row in (
            (pair_ref, jnp.where(even, lower, upper)),
            (cross_ref, jnp.where(even, upper, lower)),
        ):
            for s in range(SUBLANES):
                ref[s : s + 1, n * packed : (n + 1) * packed] = row[
                    :, s * packed : (s + 1) * packed
                ]
    pair_ref[:, 3 * packed :] = points_ref[...]
    cross_ref[:, 3 * packed :] = points_ref[...]


def bell_of(dist, period, scale):
    dist = jnp.abs(dist)
    dist = jnp.minimum(dist, period - dist) / scale
    return jnp.exp(-0.5 * (dist * dist))


def halves(x):
    high = x.astype(jnp.bfloat16)
    return high, (x - high.astype(jnp.float32)).astype(jnp.bfloat16)


def taper_kernel(sizes, sorted_ref, columns_ref, obs_ref, rows_ref):
    reg_count, region_rows, slab_rows, columns = sizes
    grid_rows = reg_count * region_rows
    row_scale, col_scale = float(region_rows // 2), float(columns // 4)
    me = lax.axis_index("reg")
    square = (LANES, LANES)
    row_lanes = jnp.broadcast_to(sorted_ref[0:1, :], square)
    col_lanes = jnp.broadcast_to(sorted_ref[1:2, :], square)
    row_subs = row_lanes.T
    col_subs = col_lanes.T
    for t in range(columns // LANES):
        at = (t * LANES + iota(1, square)).astype(jnp.float32)
        high, low = halves(bell_of(at - col_subs, float(columns), col_scale))
        columns_ref[0, :, t * LANES : (t + 1) * LANES] = high
        columns_ref[1, :, t * LANES : (t + 1) * LANES] = low
    high, low = halves(
        bell_of(row_lanes - row_subs, float(grid_rows), row_scale)
        * bell_of(col_lanes - col_subs, float(columns), col_scale)
    )
    obs_ref[0] = high
    obs_ref[1] = low
    rows = (me * region_rows + iota(0)).astype(jnp.float32)
    rows_ref[...] = bell_of(rows - row_lanes[:SUBLANES], float(grid_rows), row_scale)


def middle_kernel(
    sizes,
    partial_ref,
    row_ref,
    col_ref,
    diff_ref,
    pair_ref,
    cross_ref,
    paired_ref,
    crossed_ref,
    field_ref,
    code_ref,
    steps_ref,
    edge_ref,
):
    reg_count, region_rows, slab_rows, columns = sizes
    packed = columns // SUBLANES
    wide = iota(0, (SUBLANES, columns))
    rate_row, rate_col, rate_diff = [
        r[...].astype(jnp.float32) for r in (row_ref, col_ref, diff_ref)
    ]

    def section(ref, n):
        return ref[:, n * packed : (n + 1) * packed]

    def ahead(ref, sent_ref):
        return section(ref, 0), section(ref, 1) + section(ref, 2) * section(sent_ref, 0)

    even = (lax.axis_index("reg") & 1) == 0
    paired, crossed = ahead(paired_ref, pair_ref), ahead(crossed_ref, cross_ref)
    outer = [
        jnp.where(even, one, other)
        for x, y in zip(paired, crossed)
        for one, other in ((y, x), (x, y))
    ]
    for n, array in enumerate(outer):
        for s in range(SUBLANES):
            edge_ref[n : n + 1, s * packed : (s + 1) * packed] = array[s : s + 1, :]

    def edge(n):
        return jnp.broadcast_to(edge_ref[n : n + 1, :], (SUBLANES, columns))

    first, last = wide == 0, wide == SUBLANES - 1
    field = (
        partial_ref[...]
        + jnp.where(first, (rate_diff + 0.5 * rate_row) * edge(0), 0.0)
        + jnp.where(last, (rate_diff - 0.5 * rate_row) * edge(1), 0.0)
    )
    north = jnp.where(first, edge(2), pltpu.roll(field, 1, axis=0))
    south = jnp.where(last, edge(3), pltpu.roll(field, SUBLANES - 1, axis=0))
    field = stencil(field, north, south, rate_row, rate_col, rate_diff)

    field_ref[...] = field
    peak = jnp.max(jnp.max(jnp.abs(field), axis=1, keepdims=True), axis=0, keepdims=True)
    steps = jnp.maximum(jnp.ceil(peak * (1.0 / (CODE_TOP * CODE_STEP))), 1.0)
    code = jnp.round(field * (1.0 / (steps * CODE_STEP)))
    code_ref[...] = code.astype(jnp.int32).astype(jnp.int16)
    steps_ref[...] = jnp.broadcast_to(steps, (SUBLANES, LANES))


def observe_kernel(
    sizes, points_ref, paired_ref, crossed_ref, far_ref, code_ref, steps_ref, taper_ref, out_ref
):
    packed = sizes[-1] // SUBLANES
    points = (
        points_ref[...] + far_ref[...] + paired_ref[:, 3 * packed :] + crossed_ref[:, 3 * packed :]
    )

    def point(c):
        s, at = slot(c)
        return points[s : s + 1, at : at + LANES]

    q0 = {p: point(n) for n, p in enumerate(POINTS)}
    rates = [
        {p: point(len(POINTS) + n * len(CROSS) + i) for i, p in enumerate(CROSS)} for n in range(3)
    ]

    def at_point(values, p):
        i, j = p
        here = values[p]
        north, south = values[i - 1, j], values[i + 1, j]
        west, east = values[i, j - 1], values[i, j + 1]
        return (
            here
            - 0.5 * rates[1][p] * (east - west)
            - 0.5 * rates[0][p] * (south - north)
            + rates[2][p] * (north + south + east + west - 4.0 * here)
        )

    q1 = {p: at_point(q0, p) for p in CROSS}
    seen = jnp.broadcast_to(at_point(q1, (0, 0)), (SUBLANES, LANES)) / SEEN_UNIT
    whole = jnp.round(seen)
    rest = jnp.round((seen - whole) / SEEN_REST)
    sub = iota(0)
    tail = jnp.where(sub == 0, whole, jnp.where(sub == 1, rest, steps_ref[...]))
    message = jnp.concatenate([code_ref[...], tail.astype(jnp.int32).astype(jnp.int16)], axis=1)
    for d in range(out_ref.shape[0]):
        out_ref[d] = message


def gain(anomaly, precision, innovation):
    members = anomaly.shape[0]
    sub = iota(0)
    weighted = anomaly * precision

    def against(x):
        total = jnp.sum(weighted * x, axis=1, keepdims=True)
        return jnp.broadcast_to(total, weighted.shape)

    system = [
        against(row_of(anomaly, b)) + jnp.where(sub == b, float(members - 1), 0.0)
        for b in range(members)
    ]
    load = [against(row_of(innovation, m)) for m in range(members)]
    held = anomaly
    for k in range(members):
        inverse = 1.0 / row_of(system[k], k)
        mine = sub == k

        def step(x, k=k, inverse=inverse, mine=mine):
            scaled = row_of(x, k) * inverse
            return jnp.where(mine, scaled, x - system[k] * scaled)

        held = step(held)
        for b in range(k + 1, members):
            system[b] = step(system[b])
    fitted = jnp.zeros_like(anomaly)
    for m in range(members):
        total = jnp.sum(load[m] * held, axis=0, keepdims=True)
        fitted = jnp.where(sub == m, jnp.broadcast_to(total, held.shape), fitted)
    return precision * (innovation - fitted)


def twice(x, block):
    lane = iota(1)
    half = LANES // 2
    return jnp.where(lane // half == block, x, pltpu.roll(x, half, axis=1))


def split(rows):
    half = LANES // 2
    high = rows.astype(jnp.bfloat16).astype(jnp.float32)
    left = jnp.where(iota(1, rows.shape) < half, high, rows - high).astype(jnp.bfloat16)
    return jnp.concatenate([left, left], axis=1)


def stacked(table_ref, block, part=slice(None)):
    half = LANES // 2
    high = table_ref[0, block * half : (block + 1) * half, part]
    low = table_ref[1, block * half : (block + 1) * half, part]
    return jnp.concatenate([high, high, low, low], axis=0)


def finish_kernel(
    sizes,
    order,
    x_ref,
    field_ref,
    sorted_ref,
    noise_ref,
    columns_ref,
    obs_ref,
    rows_ref,
    out_ref,
    now_ref,
):
    columns = sizes[-1]
    members = x_ref.shape[0]
    me = lax.axis_index("mem")
    sub, lane = iota(0), iota(1)
    half = LANES // 2
    place = [order.index(m) for m in range(members)]
    seen = jnp.zeros((SUBLANES, LANES), jnp.float32)
    steps = []
    for m in range(members):
        tail = x_ref[place[m], :, columns:].astype(jnp.float32)
        value = (row_of(tail, 0) + row_of(tail, 1) * SEEN_REST) * SEEN_UNIT
        seen = jnp.where(sub == m, value, seen)
        steps.append(row_of(tail, 2) * CODE_STEP)
    value, variance = row_of(sorted_ref, 2), row_of(sorted_ref, 3)
    observed = value + jnp.sqrt(variance) * noise_ref[...]
    inverse_variance = 1.0 / variance
    scale = 1.0 / (members - 1)
    def added(starts, fields, weights):
        apart = [x - fields[-1] for x in fields[:-1]]
        updated = []
        for n, total in enumerate(starts):
            for a, x in enumerate(apart):
                at = (a * len(starts) + n) * SUBLANES
                total = total + x * weights[at : at + SUBLANES]
            updated.append(total)
        return updated

    current = [x_ref[place[m], :, :columns].astype(jnp.float32) * steps[m][:, :1] for m in range(members)]
    for m in range(members):
        now_ref[m] = current[m]
    base = field_ref[...] - now_ref[me]
    for block in range(NBLK):
        last = block + 1 == NBLK
        anomaly = seen - jnp.sum(seen, axis=0, keepdims=True) * (1.0 / members)
        precision = jnp.where(lane // half == block, inverse_variance, 0.0)
        gains = gain(anomaly, precision, observed - seen) * scale
        gains, local = twice(gains, block), twice(anomaly, block)
        pairs = [row_of(local, a) * gains for a in range(members)]
        row_taper = twice(rows_ref[...], block)
        used = pairs[: members - 1]
        if last:
            own = [
                jnp.sum(jnp.where(sub == me, pair, 0.0), axis=0, keepdims=True) for pair in used
            ]
            left = [row_taper * x for x in own]
        else:
            moved = jnp.dot(
                split(jnp.concatenate(pairs, axis=0)),
                stacked(obs_ref, block),
                preferred_element_type=jnp.float32,
            )
            for a in range(members):
                seen = seen + row_of(anomaly, a) * moved[a * SUBLANES : (a + 1) * SUBLANES]
            left = [row_taper * row_of(pair, m) for pair in used for m in range(members)]
        weights = jnp.dot(
            split(jnp.concatenate(left, axis=0)),
            stacked(columns_ref, block),
            preferred_element_type=jnp.float32,
        )
        if last:
            (out_ref[0],) = added([now_ref[me] + base], current, weights)
        else:
            current = added(current, current, weights)
            for m in range(members):
                now_ref[m] = current[m]


def call(kernel, outs, args, scratch=(), cost=None, space=pltpu.VMEM):
    held = pl.BlockSpec(memory_space=pltpu.VMEM)
    return pl.pallas_call(
        kernel,
        out_shape=[jax.ShapeDtypeStruct(s, d) for s, d in outs],
        in_specs=[pl.BlockSpec(memory_space=space)] * len(args),
        out_specs=[held] * len(outs),
        scratch_shapes=list(scratch),
        cost_estimate=cost,
        compiler_params=pltpu.CompilerParams(vmem_limit_bytes=VMEM_GRANT),
    )(*args)


def on_tile(
    prior_tracer_draws,
    courant_row,
    courant_column,
    diffusion,
    obs_value,
    observation_variance,
    obs_noise,
    obs_owner,
    obs_cell,
    obs_order,
):
    f32 = jnp.float32
    region_rows, columns = prior_tracer_draws.shape[1:]
    members = obs_noise.shape[1]
    mem_count, reg_count = lax.axis_size("mem"), lax.axis_size("reg")
    sizes = (reg_count, region_rows, region_rows // mem_count, columns)
    packed = columns // SUBLANES
    tile = (SUBLANES, LANES)
    field = (SUBLANES, columns)
    points_shape = (SUBLANES, TILES * LANES)
    message = (SUBLANES, 3 * packed + TILES * LANES)
    rates = (courant_row, courant_column, diffusion)
    flat = [x.reshape(1, LANES) for x in (obs_owner, obs_cell, obs_order, obs_value, observation_variance)]
    operands = (prior_tracer_draws, *rates, *flat, obs_noise.T)
    pair, cross, points, partial, table, noise, *rates = call(
        functools.partial(start_kernel, sizes),
        [(message, f32), (message, f32), (points_shape, f32), (field, f32), (tile, f32), (tile, f32)]
        + [(x.shape, x.dtype) for x in rates],
        [pltpu.with_memory_space_constraint(x, pltpu.HBM) for x in operands],
        scratch=[pltpu.VMEM(prior_tracer_draws.shape, f32)]
        + [pltpu.VMEM(x.shape, x.dtype) for x in operands[4:]]
        + [pltpu.SemaphoreType.DMA((len(operands),))],
        space=pltpu.HBM,
    )

    pairs = [(i, i ^ 1) for i in range(reg_count)]
    crosses = [(i, (i - 1 + 2 * (i & 1)) % reg_count) for i in range(reg_count)]
    crossed = lax.ppermute(cross, "reg", crosses)
    paired = lax.ppermute(pair, "reg", pairs)
    far = lax.ppermute(points, "reg", [(i, i ^ 2) for i in range(reg_count)])
    col_taper, obs_taper, row_taper = call(
        functools.partial(taper_kernel, sizes),
        [((2, LANES, columns), jnp.bfloat16), ((2, LANES, LANES), jnp.bfloat16), (tile, f32)],
        (table,),
        cost=pl.CostEstimate(flops=10 * LANES * columns, bytes_accessed=8 * LANES * columns, transcendentals=LANES * columns),
    )
    forecast, code, steps = call(
        functools.partial(middle_kernel, sizes),
        [(field, f32), (field, jnp.int16), (tile, f32)],
        (partial, *rates, pair, cross, paired, crossed),
        scratch=[pltpu.VMEM(field, f32)],
    )
    (send,) = call(
        functools.partial(observe_kernel, sizes),
        [((mem_count, SUBLANES, columns + LANES), jnp.int16)],
        (points, paired, crossed, far, code, steps, row_taper),
    )
    half = mem_count // 2
    along = [*range(half // 2, -1, -1), *range(half // 2 + 1, half)]
    order = [2 * z + 1 for z in along] + [2 * (-z % half) for z in range(half)]
    slabs = lax.all_to_all(
        send, "mem", split_axis=0, concat_axis=0, tiled=True, axis_index_groups=[order]
    )
    (out,) = call(
        functools.partial(finish_kernel, sizes, order),
        [(prior_tracer_draws.shape, f32)],
        (slabs, forecast, table, noise, col_taper, obs_taper, row_taper),
        scratch=[pltpu.VMEM((members, *field), f32)],
    )
    return out


def fits_tile(*shapes):
    draws, noise = shapes
    members, region_rows, columns = draws
    counts = (lax.axis_size("mem"), lax.axis_size("reg"))
    return (
        members == 1
        and noise[1] == counts[0] == region_rows == SUBLANES
        and noise[0] == NOB * NBLK == LANES
        and counts[1] == 4
        and columns % (SUBLANES * LANES) == 0
        and columns & (columns - 1) == 0
    )


def on_device(*args):
    return (on_tile if fits_tile(args[0].shape, args[6].shape) else on_slabs)(*args)


def solution(mesh):
    placed = (
        P("mem", "reg", None),
        P("reg", None),
        P("reg", None),
        P("reg", None),
        P(),
        P(),
        P(),
        P(),
        P(),
        P(),
    )
    return jax.shard_map(
        on_device, mesh=mesh, in_specs=placed, out_specs=P("mem", "reg", None), check_vma=False
    )
```

```python
import functools

import jax
import jax.numpy as jnp
from jax import lax
from jax.experimental import pallas as pl
from jax.experimental.pallas import tpu as pltpu
from jax.sharding import PartitionSpec as P

NOB = 64
NBLK = 2


HIGH = lax.Precision.HIGHEST


def extended(cells, sides, width):
    for axis, dim in sides:
        count = lax.axis_size(axis)
        head = lax.slice_in_dim(cells, 0, width, axis=dim)
        tail = lax.slice_in_dim(cells, cells.shape[dim] - width, cells.shape[dim], axis=dim)
        cells = jnp.concatenate(
            [
                lax.ppermute(tail, axis, [(i, (i + 1) % count) for i in range(count)]),
                cells,
                lax.ppermute(head, axis, [((i + 1) % count, i) for i in range(count)]),
            ],
            axis=dim,
        )
    return cells


def bell(delta, period, scale):
    delta = delta % period
    dist = jnp.minimum(delta, period - delta).astype(jnp.float32)
    return jnp.exp(-0.5 * (dist / scale) ** 2)


def advance_rows(haloed_extended_grid, courant_row, courant_column, diffusion):
    centre = haloed_extended_grid[1:-1]
    north = haloed_extended_grid[:-2]
    south = haloed_extended_grid[2:]
    west = jnp.roll(centre, 1, axis=1)
    east = jnp.roll(centre, -1, axis=1)
    return (
        centre
        - 0.5 * courant_column * (east - west)
        - 0.5 * courant_row * (south - north)
        + diffusion * (north + south + east + west - 4.0 * centre)
    )


def measured_kalman_gain(prior, values, variance, noise):
    members = prior.shape[0]
    anomaly = prior - jnp.mean(prior, axis=0)
    spread = jnp.dot(anomaly.T, anomaly, precision=HIGH, preferred_element_type=jnp.float32) / (
        members - 1
    )
    system = spread + jnp.diag(variance)
    factor = jnp.linalg.cholesky(system)
    innovation = values[:, None] + jnp.sqrt(variance)[:, None] * noise - prior.T
    weights = jax.scipy.linalg.cho_solve((factor, True), innovation)
    return (anomaly, weights)


def increment(columns, anomaly, weights, taper):
    members = columns.shape[0]
    centred = columns - jnp.mean(columns, axis=0)
    cross = lax.dot_general(
        centred,
        anomaly,
        (((0,), (0,)), ((), ())),
        precision=HIGH,
        preferred_element_type=jnp.float32,
    ) / (members - 1)
    return columns + lax.dot_general(
        weights,
        taper * cross,
        (((0,), (1,)), ((), ())),
        precision=HIGH,
        preferred_element_type=jnp.float32,
    )


def on_slabs(
    prior_tracer_draws,
    courant_row,
    courant_column,
    diffusion,
    obs_value,
    observation_variance,
    obs_noise,
    obs_owner,
    obs_cell,
    obs_order,
):
    region_rows = prior_tracer_draws.shape[1]
    columns = prior_tracer_draws.shape[2]
    mem_count = lax.axis_size("mem")
    reg_count = lax.axis_size("reg")
    slab_rows = region_rows // mem_count
    grid_rows = region_rows * reg_count
    latitude_weighting = region_rows // 2
    col_scale = columns // 4
    rate_row = courant_row.astype(jnp.float32)
    column_rate = courant_column.astype(jnp.float32)
    rate_diff = diffusion.astype(jnp.float32)
    field = prior_tracer_draws[0]
    for step in range(2):
        haloed_extended_grid = extended(field, (("reg", 0),), 1)
        field = advance_rows(haloed_extended_grid, rate_row, column_rate, rate_diff)
    slabs = lax.all_to_all(field[None], "mem", split_axis=1, concat_axis=0, tiled=True)
    members = slabs.shape[0]
    cells = slabs.reshape(members, slab_rows * columns)
    me_mem = lax.axis_index("mem")
    me_reg = lax.axis_index("reg")
    myself = me_mem * reg_count + me_reg
    owned_rows = me_reg * region_rows + me_mem * slab_rows + jnp.arange(slab_rows, dtype=jnp.int32)
    obs_row = (
        obs_owner % reg_count * region_rows
        + obs_owner // reg_count * slab_rows
        + obs_cell // columns
    )
    observation_column = obs_cell % columns
    col_index = jnp.arange(columns, dtype=jnp.int32)
    owners = obs_owner[obs_order]
    spots = obs_cell[obs_order]
    sorted_row = obs_row[obs_order]
    sorted_col = observation_column[obs_order]
    local = jnp.where((owners == myself)[None, :], cells[:, spots], 0.0)
    priors = lax.psum(local, ("mem", "reg"))
    for block in range(NBLK):
        lower = block * NOB
        upper = (block + 1) * NOB
        chosen = obs_order[lower:upper]
        prior = priors[:, lower:upper]
        anomaly, weights = measured_kalman_gain(
            prior, obs_value[chosen], observation_variance[chosen], obs_noise[chosen]
        )
        orow = sorted_row[lower:upper]
        ocol = sorted_col[lower:upper]
        row_taper = bell(owned_rows[:, None] - orow[None, :], grid_rows, latitude_weighting)
        col_taper = bell(col_index[:, None] - ocol[None, :], columns, col_scale)
        cells = increment(
            cells,
            anomaly,
            weights,
            (row_taper[:, None, :] * col_taper[None, :, :]).reshape(
                slab_rows * columns, orow.shape[0]
            ),
        )
        obs_taper = bell(sorted_row[:, None] - orow[None, :], grid_rows, latitude_weighting) * bell(
            sorted_col[:, None] - ocol[None, :], columns, col_scale
        )
        priors = increment(priors, anomaly, weights, obs_taper)
    return lax.all_to_all(
        cells.reshape(members, slab_rows, columns), "mem", split_axis=0, concat_axis=1, tiled=True
    )


SUBLANES = 8
LANES = 128
POINTS = [(dr, dc) for dr in range(-2, 3) for dc in range(-2, 3) if abs(dr) + abs(dc) <= 2]
CROSS = [(0, 0), (-1, 0), (1, 0), (0, -1), (0, 1)]
TILES = -(-(len(POINTS) + 3 * len(CROSS)) // SUBLANES)
CODE_STEP = 2.0**-20
CODE_TOP = 32767.0
SEEN_UNIT = 2.0**-11
SEEN_REST = 2.0**-15
VMEM_GRANT = 8 << 20


def iota(axis, shape=(SUBLANES, LANES)):
    return lax.broadcasted_iota(jnp.int32, shape, axis)


def row_of(x, i):
    return jnp.broadcast_to(x[i : i + 1, :], x.shape)


def stencil(q, north, south, rate_row, rate_col, rate_diff):
    columns = q.shape[1]
    west = pltpu.roll(q, 1, axis=1)
    east = pltpu.roll(q, columns - 1, axis=1)
    return (
        q
        - 0.5 * rate_col * (east - west)
        - 0.5 * rate_row * (south - north)
        + rate_diff * (north + south + east + west - 4.0 * q)
    )


def slot(c):
    return c % SUBLANES, c // SUBLANES * LANES


def start_kernel(
    sizes,
    q_hbm,
    row_hbm,
    col_hbm,
    diff_hbm,
    owner_hbm,
    cell_hbm,
    order_hbm,
    value_hbm,
    variance_hbm,
    noise_hbm,
    pair_ref,
    cross_ref,
    points_ref,
    partial_ref,
    sorted_ref,
    noise_out,
    row_ref,
    col_ref,
    diff_ref,
    q_ref,
    owner_ref,
    cell_ref,
    order_ref,
    value_ref,
    variance_ref,
    noise_ref,
    arrived,
):
    fetched = (
        (owner_hbm, owner_ref),
        (cell_hbm, cell_ref),
        (order_hbm, order_ref),
        (value_hbm, value_ref),
        (variance_hbm, variance_ref),
        (noise_hbm, noise_ref),
        (q_hbm, q_ref),
        (row_hbm, row_ref),
        (col_hbm, col_ref),
        (diff_hbm, diff_ref),
    )
    copies = [
        pltpu.make_async_copy(source, target, arrived.at[n])
        for n, (source, target) in enumerate(fetched)
    ]
    for copy in copies:
        copy.start()
    for copy in copies[:6]:
        copy.wait()
    reg_count, region_rows, slab_rows, columns = sizes
    grid_rows = reg_count * region_rows
    packed = columns // SUBLANES
    me = lax.axis_index("reg")
    sub = iota(0)
    owner = owner_ref[...]
    cell = cell_ref[...]
    shift = columns.bit_length() - 1
    obs_row = (
        (owner & (reg_count - 1)) * region_rows
        + (owner >> (reg_count.bit_length() - 1)) * slab_rows
        + (cell >> shift)
    )
    obs_col = cell & (columns - 1)
    table = jnp.where(
        sub == 0,
        obs_row.astype(jnp.float32),
        jnp.where(
            sub == 1,
            obs_col.astype(jnp.float32),
            jnp.where(sub == 2, value_ref[...], jnp.where(sub == 3, variance_ref[...], 0.0)),
        ),
    )
    square = (LANES, LANES)
    pick = (iota(0, square) == order_ref[...]).astype(jnp.float32)
    both = jnp.dot(
        jnp.concatenate([table, noise_ref[...]], axis=0),
        pick,
        precision=HIGH,
        preferred_element_type=jnp.float32,
    )
    table = both[:SUBLANES]
    sorted_ref[...] = table
    noise_out[...] = both[SUBLANES:]
    orow = row_of(table, 0).astype(jnp.int32)
    ocol = row_of(table, 1).astype(jnp.int32)

    for copy in copies[6:]:
        copy.wait()
    q = q_ref[0]
    rates = [r[...].astype(jnp.float32) for r in (row_ref, col_ref, diff_ref)]
    local_row = orow - me * region_rows
    for dc in range(-2, 3):
        index = (ocol + dc) & (columns - 1)
        lane = index & (LANES - 1)
        tile = index >> (LANES.bit_length() - 1)
        wanted = [(q, 0, POINTS)]
        if abs(dc) <= 1:
            for n, rate in enumerate(rates):
                wanted.append((rate, len(POINTS) + n * len(CROSS), CROSS))
        hits = [tile == t for t in range(columns // LANES)]
        for array, base, points in wanted:
            found = jnp.zeros((SUBLANES, LANES), jnp.float32)
            for t in range(columns // LANES):
                taken = jnp.take_along_axis(
                    array[:, t * LANES : (t + 1) * LANES], lane, axis=1, mode="promise_in_bounds"
                )
                found = jnp.where(hits[t], taken, found)
            for n, (dr, shift_col) in enumerate(points):
                if shift_col != dc:
                    continue
                here = ((local_row + dr) & (grid_rows - 1)) == sub
                s, at = slot(base + n)
                points_ref[s : s + 1, at : at + LANES] = jnp.sum(
                    jnp.where(here, found, 0.0), axis=0, keepdims=True
                )
    for c in range(len(POINTS) + 3 * len(CROSS), TILES * SUBLANES):
        s, at = slot(c)
        points_ref[s : s + 1, at : at + LANES] = jnp.zeros((1, LANES), jnp.float32)

    rate_row, rate_col, rate_diff = rates
    wide = iota(0, (SUBLANES, columns))
    north = jnp.where(wide == 0, 0.0, pltpu.roll(q, 1, axis=0))
    south = jnp.where(wide == SUBLANES - 1, 0.0, pltpu.roll(q, SUBLANES - 1, axis=0))
    partial = stencil(q, north, south, rate_row, rate_col, rate_diff)
    partial_ref[...] = partial
    even = (me & 1) == 0
    edges = [
        (array[SUBLANES - 1 :, :], array[:1, :])
        for array in (q, partial)
    ] + [((rate_diff - 0.5 * rate_row)[SUBLANES - 1 :, :], (rate_diff + 0.5 * rate_row)[:1, :])]
    for n, (lower, upper) in enumerate(edges):
        for ref, row in (
            (pair_ref, jnp.where(even, lower, upper)),
            (cross_ref, jnp.where(even, upper, lower)),
        ):
            for s in range(SUBLANES):
                ref[s : s + 1, n * packed : (n + 1) * packed] = row[
                    :, s * packed : (s + 1) * packed
                ]
    pair_ref[:, 3 * packed :] = points_ref[...]
    cross_ref[:, 3 * packed :] = points_ref[...]


def bell_of(dist, period, scale):
    dist = jnp.abs(dist)
    dist = jnp.minimum(dist, period - dist) / scale
    return jnp.exp(-0.5 * (dist * dist))


def halves(x):
    high = x.astype(jnp.bfloat16)
    return high, (x - high.astype(jnp.float32)).astype(jnp.bfloat16)


def taper_kernel(sizes, sorted_ref, columns_ref, obs_ref, rows_ref):
    reg_count, region_rows, slab_rows, columns = sizes
    grid_rows = reg_count * region_rows
    row_scale, col_scale = float(region_rows // 2), float(columns // 4)
    me = lax.axis_index("reg")
    square = (LANES, LANES)
    row_lanes = jnp.broadcast_to(sorted_ref[0:1, :], square)
    col_lanes = jnp.broadcast_to(sorted_ref[1:2, :], square)
    row_subs = row_lanes.T
    col_subs = col_lanes.T
    for t in range(columns // LANES):
        at = (t * LANES + iota(1, square)).astype(jnp.float32)
        high, low = halves(bell_of(at - col_subs, float(columns), col_scale))
        columns_ref[0, :, t * LANES : (t + 1) * LANES] = high
        columns_ref[1, :, t * LANES : (t + 1) * LANES] = low
    high, low = halves(
        bell_of(row_lanes - row_subs, float(grid_rows), row_scale)
        * bell_of(col_lanes - col_subs, float(columns), col_scale)
    )
    obs_ref[0] = high
    obs_ref[1] = low
    rows = (me * region_rows + iota(0)).astype(jnp.float32)
    rows_ref[...] = bell_of(rows - row_lanes[:SUBLANES], float(grid_rows), row_scale)


def middle_kernel(
    sizes,
    partial_ref,
    row_ref,
    col_ref,
    diff_ref,
    pair_ref,
    cross_ref,
    paired_ref,
    crossed_ref,
    field_ref,
    code_ref,
    steps_ref,
    edge_ref,
):
    reg_count, region_rows, slab_rows, columns = sizes
    packed = columns // SUBLANES
    wide = iota(0, (SUBLANES, columns))
    rate_row, rate_col, rate_diff = [
        r[...].astype(jnp.float32) for r in (row_ref, col_ref, diff_ref)
    ]

    def section(ref, n):
        return ref[:, n * packed : (n + 1) * packed]

    def ahead(ref, sent_ref):
        return section(ref, 0), section(ref, 1) + section(ref, 2) * section(sent_ref, 0)

    even = (lax.axis_index("reg") & 1) == 0
    paired, crossed = ahead(paired_ref, pair_ref), ahead(crossed_ref, cross_ref)
    outer = [
        jnp.where(even, one, other)
        for x, y in zip(paired, crossed)
        for one, other in ((y, x), (x, y))
    ]
    for n, array in enumerate(outer):
        for s in range(SUBLANES):
            edge_ref[n : n + 1, s * packed : (s + 1) * packed] = array[s : s + 1, :]

    def edge(n):
        return jnp.broadcast_to(edge_ref[n : n + 1, :], (SUBLANES, columns))

    first, last = wide == 0, wide == SUBLANES - 1
    field = (
        partial_ref[...]
        + jnp.where(first, (rate_diff + 0.5 * rate_row) * edge(0), 0.0)
        + jnp.where(last, (rate_diff - 0.5 * rate_row) * edge(1), 0.0)
    )
    north = jnp.where(first, edge(2), pltpu.roll(field, 1, axis=0))
    south = jnp.where(last, edge(3), pltpu.roll(field, SUBLANES - 1, axis=0))
    field = stencil(field, north, south, rate_row, rate_col, rate_diff)

    field_ref[...] = field
    peak = jnp.max(jnp.max(jnp.abs(field), axis=1, keepdims=True), axis=0, keepdims=True)
    steps = jnp.maximum(jnp.ceil(peak * (1.0 / (CODE_TOP * CODE_STEP))), 1.0)
    code = jnp.round(field * (1.0 / (steps * CODE_STEP)))
    code_ref[...] = code.astype(jnp.int32).astype(jnp.int16)
    steps_ref[...] = jnp.broadcast_to(steps, (SUBLANES, LANES))


def observe_kernel(
    sizes, points_ref, paired_ref, crossed_ref, far_ref, code_ref, steps_ref, out_ref
):
    packed = sizes[-1] // SUBLANES
    points = (
        points_ref[...] + far_ref[...] + paired_ref[:, 3 * packed :] + crossed_ref[:, 3 * packed :]
    )

    def point(c):
        s, at = slot(c)
        return points[s : s + 1, at : at + LANES]

    q0 = {p: point(n) for n, p in enumerate(POINTS)}
    rates = [
        {p: point(len(POINTS) + n * len(CROSS) + i) for i, p in enumerate(CROSS)} for n in range(3)
    ]

    def at_point(values, p):
        i, j = p
        here = values[p]
        north, south = values[i - 1, j], values[i + 1, j]
        west, east = values[i, j - 1], values[i, j + 1]
        return (
            here
            - 0.5 * rates[1][p] * (east - west)
            - 0.5 * rates[0][p] * (south - north)
            + rates[2][p] * (north + south + east + west - 4.0 * here)
        )

    q1 = {p: at_point(q0, p) for p in CROSS}
    seen = jnp.broadcast_to(at_point(q1, (0, 0)), (SUBLANES, LANES)) / SEEN_UNIT
    whole = jnp.round(seen)
    rest = jnp.round((seen - whole) / SEEN_REST)
    sub = iota(0)
    tail = jnp.where(sub == 0, whole, jnp.where(sub == 1, rest, steps_ref[...]))
    message = jnp.concatenate([code_ref[...], tail.astype(jnp.int32).astype(jnp.int16)], axis=1)
    for d in range(out_ref.shape[0]):
        out_ref[d] = message


def gain(anomaly, precision, innovation):
    members = anomaly.shape[0]
    sub = iota(0)
    weighted = anomaly * precision

    def against(x):
        total = jnp.sum(weighted * x, axis=1, keepdims=True)
        return jnp.broadcast_to(total, weighted.shape)

    system = [
        against(row_of(anomaly, b)) + jnp.where(sub == b, float(members - 1), 0.0)
        for b in range(members)
    ]
    load = [against(row_of(innovation, m)) for m in range(members)]
    held = anomaly
    for k in range(members):
        inverse = 1.0 / row_of(system[k], k)
        mine = sub == k

        def step(x, k=k, inverse=inverse, mine=mine):
            scaled = row_of(x, k) * inverse
            return jnp.where(mine, scaled, x - system[k] * scaled)

        held = step(held)
        for b in range(k + 1, members):
            system[b] = step(system[b])
    fitted = jnp.zeros_like(anomaly)
    for m in range(members):
        total = jnp.sum(load[m] * held, axis=0, keepdims=True)
        fitted = jnp.where(sub == m, jnp.broadcast_to(total, held.shape), fitted)
    return precision * (innovation - fitted)


def twice(x, block):
    lane = iota(1)
    half = LANES // 2
    return jnp.where(lane // half == block, x, pltpu.roll(x, half, axis=1))


def split(rows):
    half = LANES // 2
    high = rows.astype(jnp.bfloat16).astype(jnp.float32)
    left = jnp.where(iota(1, rows.shape) < half, high, rows - high).astype(jnp.bfloat16)
    return jnp.concatenate([left, left], axis=1)


def stacked(table_ref, block, part=slice(None)):
    half = LANES // 2
    high = table_ref[0, block * half : (block + 1) * half, part]
    low = table_ref[1, block * half : (block + 1) * half, part]
    return jnp.concatenate([high, high, low, low], axis=0)


def finish_kernel(
    sizes,
    order,
    x_ref,
    field_ref,
    sorted_ref,
    noise_ref,
    columns_ref,
    obs_ref,
    rows_ref,
    out_ref,
    now_ref,
):
    columns = sizes[-1]
    members = x_ref.shape[0]
    me = lax.axis_index("mem")
    sub, lane = iota(0), iota(1)
    half = LANES // 2
    place = [order.index(m) for m in range(members)]
    seen = jnp.zeros((SUBLANES, LANES), jnp.float32)
    steps = []
    for m in range(members):
        tail = x_ref[place[m], :, columns:].astype(jnp.float32)
        value = (row_of(tail, 0) + row_of(tail, 1) * SEEN_REST) * SEEN_UNIT
        seen = jnp.where(sub == m, value, seen)
        steps.append(row_of(tail, 2) * CODE_STEP)
    value, variance = row_of(sorted_ref, 2), row_of(sorted_ref, 3)
    observed = value + jnp.sqrt(variance) * noise_ref[...]
    inverse_variance = 1.0 / variance
    scale = 1.0 / (members - 1)
    def added(starts, fields, weights):
        apart = [x - fields[-1] for x in fields[:-1]]
        updated = []
        for n, total in enumerate(starts):
            for a, x in enumerate(apart):
                at = (a * len(starts) + n) * SUBLANES
                total = total + x * weights[at : at + SUBLANES]
            updated.append(total)
        return updated

    current = [x_ref[place[m], :, :columns].astype(jnp.float32) * steps[m][:, :1] for m in range(members)]
    for m in range(members):
        now_ref[m] = current[m]
    base = field_ref[...] - now_ref[me]
    for block in range(NBLK):
        last = block + 1 == NBLK
        anomaly = seen - jnp.sum(seen, axis=0, keepdims=True) * (1.0 / members)
        precision = jnp.where(lane // half == block, inverse_variance, 0.0)
        gains = gain(anomaly, precision, observed - seen) * scale
        gains, local = twice(gains, block), twice(anomaly, block)
        pairs = [row_of(local, a) * gains for a in range(members)]
        row_taper = twice(rows_ref[...], block)
        used = pairs[: members - 1]
        if last:
            own = [
                jnp.sum(jnp.where(sub == me, pair, 0.0), axis=0, keepdims=True) for pair in used
            ]
            left = [row_taper * x for x in own]
        else:
            moved = jnp.dot(
                split(jnp.concatenate(pairs, axis=0)),
                stacked(obs_ref, block),
                preferred_element_type=jnp.float32,
            )
            for a in range(members):
                seen = seen + row_of(anomaly, a) * moved[a * SUBLANES : (a + 1) * SUBLANES]
            left = [row_taper * row_of(pair, m) for pair in used for m in range(members)]
        weights = jnp.dot(
            split(jnp.concatenate(left, axis=0)),
            stacked(columns_ref, block),
            preferred_element_type=jnp.float32,
        )
        if last:
            (out_ref[0],) = added([now_ref[me] + base], current, weights)
        else:
            current = added(current, current, weights)
            for m in range(members):
                now_ref[m] = current[m]


def call(kernel, outs, args, scratch=(), cost=None, space=pltpu.VMEM, flags=None):
    held = pl.BlockSpec(memory_space=pltpu.VMEM)
    return pl.pallas_call(
        kernel,
        out_shape=[jax.ShapeDtypeStruct(s, d) for s, d in outs],
        in_specs=[pl.BlockSpec(memory_space=space)] * len(args),
        out_specs=[held] * len(outs),
        scratch_shapes=list(scratch),
        cost_estimate=cost,
        compiler_params=pltpu.CompilerParams(vmem_limit_bytes=VMEM_GRANT, flags=flags),
    )(*args)


def on_tile(
    prior_tracer_draws,
    courant_row,
    courant_column,
    diffusion,
    obs_value,
    observation_variance,
    obs_noise,
    obs_owner,
    obs_cell,
    obs_order,
):
    f32 = jnp.float32
    region_rows, columns = prior_tracer_draws.shape[1:]
    members = obs_noise.shape[1]
    mem_count, reg_count = lax.axis_size("mem"), lax.axis_size("reg")
    sizes = (reg_count, region_rows, region_rows // mem_count, columns)
    packed = columns // SUBLANES
    tile = (SUBLANES, LANES)
    field = (SUBLANES, columns)
    points_shape = (SUBLANES, TILES * LANES)
    message = (SUBLANES, 3 * packed + TILES * LANES)
    rates = (courant_row, courant_column, diffusion)
    flat = [x.reshape(1, LANES) for x in (obs_owner, obs_cell, obs_order, obs_value, observation_variance)]
    operands = (prior_tracer_draws, *rates, *flat, obs_noise.T)
    pair, cross, points, partial, table, noise, *rates = call(
        functools.partial(start_kernel, sizes),
        [(message, f32), (message, f32), (points_shape, f32), (field, f32), (tile, f32), (tile, f32)]
        + [(x.shape, x.dtype) for x in rates],
        [pltpu.with_memory_space_constraint(x, pltpu.HBM) for x in operands],
        scratch=[pltpu.VMEM(prior_tracer_draws.shape, f32)]
        + [pltpu.VMEM(x.shape, x.dtype) for x in operands[4:]]
        + [pltpu.SemaphoreType.DMA((len(operands),))],
        space=pltpu.HBM,
    )

    pairs = [(i, i ^ 1) for i in range(reg_count)]
    crosses = [(i, (i - 1 + 2 * (i & 1)) % reg_count) for i in range(reg_count)]
    crossed = lax.ppermute(cross, "reg", crosses)
    paired = lax.ppermute(pair, "reg", pairs)
    far = lax.ppermute(points, "reg", [(i, i ^ 2) for i in range(reg_count)])
    col_taper, obs_taper, row_taper = call(
        functools.partial(taper_kernel, sizes),
        [((2, LANES, columns), jnp.bfloat16), ((2, LANES, LANES), jnp.bfloat16), (tile, f32)],
        (table,),
        cost=pl.CostEstimate(flops=10 * LANES * columns, bytes_accessed=8 * LANES * columns, transcendentals=LANES * columns),
    )
    forecast, code, steps = call(
        functools.partial(middle_kernel, sizes),
        [(field, f32), (field, jnp.int16), (tile, f32)],
        (partial, *rates, pair, cross, paired, crossed),
        scratch=[pltpu.VMEM(field, f32)],
    )
    (send,) = call(
        functools.partial(observe_kernel, sizes),
        [((mem_count, SUBLANES, columns + LANES), jnp.int16)],
        (points, paired, crossed, far, code, steps),
    )
    half = mem_count // 2
    along = [*range(half // 2, -1, -1), *range(half // 2 + 1, half)]
    order = [2 * z + y for y in range(2) for z in along]
    slabs = lax.all_to_all(
        send, "mem", split_axis=0, concat_axis=0, tiled=True, axis_index_groups=[order]
    )
    (out,) = call(
        functools.partial(finish_kernel, sizes, order),
        [(prior_tracer_draws.shape, f32)],
        (slabs, forecast, table, noise, col_taper, obs_taper, row_taper),
        scratch=[pltpu.VMEM((members, *field), f32)],
    )
    return out


def fits_tile(*shapes):
    draws, noise = shapes
    members, region_rows, columns = draws
    counts = (lax.axis_size("mem"), lax.axis_size("reg"))
    return (
        members == 1
        and noise[1] == counts[0] == region_rows == SUBLANES
        and noise[0] == NOB * NBLK == LANES
        and counts[1] == 4
        and columns % (SUBLANES * LANES) == 0
        and columns & (columns - 1) == 0
    )


def on_device(*args):
    return (on_tile if fits_tile(args[0].shape, args[6].shape) else on_slabs)(*args)


def solution(mesh):
    placed = (
        P("mem", "reg", None),
        P("reg", None),
        P("reg", None),
        P("reg", None),
        P(),
        P(),
        P(),
        P(),
        P(),
        P(),
    )
    return jax.shard_map(
        on_device, mesh=mesh, in_specs=placed, out_specs=P("mem", "reg", None), check_vma=False
    )
```
